32 devices in a mesh: ex: 2 (over x), ey: 2 (over y), lin: 8 (over z, core).
Axes of the slice: x: 2, y: 2, z: 4, core: 2. Of those that a mesh axis runs over, the one named last changes fastest.
Arguments:
- load: float32 [5, 5, 5, 4, 16, 256], P(None, None, None, None, ('ey', 'lin'), 'ex'), may hold values from -6 to 6
- kappa: float32 [4, 16, 256], P(None, ('ey', 'lin'), 'ex'), may hold values from 0.3 to 3
- wet: int32 [4, 16, 256], P(None, ('ey', 'lin'), 'ex'), may hold values 0 or 1
Outputs:
- solution: float32 [5, 5, 5, 4, 16, 256], P(None, None, None, None, ('ey', 'lin'), 'ex')
- residual: float32 [5, 5, 5, 4, 16, 256], P(None, None, None, None, ('ey', 'lin'), 'ex')
The draws below stay inside these ranges and needn't reach their ends.
All inputs are finite; a program needn't handle non-finite values. No bound on the sum of `wet` on one device may be relied on, other than what follows from the above.
Results may differ from the reference program's by a relative error of at most 0.00016.
Values sent between devices are 32-bit elements; how exact they have to be, the bound alone decides.
A program may use at most 64 MiB of HBM per device.

```python
import math
import jax
import jax.numpy as jnp
import numpy as np
from jax import lax

LOBATTO_NODES = 5
ELEMENTS_DEPTH = 4
CYCLES = 2
NPRE = 2
NPOST = 2
NC = 4
ELEMENTS_ALONG = 256
ELEMENTS_ACROSS = 16


def set_ends(values, stream_key, low, top_value):
    shape = values.shape
    index_at = [jax.random.randint(jax.random.fold_in(stream_key, axis), (), 0, shape[axis]) for axis in range(len(shape))]
    values = values.at[tuple(index_at)].set(low)
    longest = shape.index(max(shape))
    index_at[longest] = (index_at[longest] + 1) % shape[longest]
    return values.at[tuple(index_at)].set(top_value)


def block_scale(key, extent, split, low, top_value):
    level, own = 1.0, jax.random.fold_in(key, 6)
    for position, shards_of in split:
        steps = jnp.exp(jax.random.uniform(jax.random.fold_in(own, position), (shards_of,), jnp.float32, low / len(split), top_value / len(split)))
        level = level * jnp.repeat(steps, extent[position] // shards_of).reshape([-1 if axis == position else 1 for axis in range(len(extent))])
    return level


def scatter_about(own_key, dims, deviation, bound, shards=(), kind=jnp.bfloat16):
    values = jax.random.normal(own_key, dims, jnp.float32) * deviation
    if len(shards) > 0:
        values = block_scale(own_key, dims, shards, -0.22, 0.18) * values
    return jnp.clip(values, min=-bound, max=bound).astype(kind)


def setup_inputs(seed: int = 0) -> dict:
    splits = jax.random.split(jax.random.key(seed), 4)
    load = scatter_about(splits[0], (LOBATTO_NODES, LOBATTO_NODES, LOBATTO_NODES, ELEMENTS_DEPTH, ELEMENTS_ACROSS, ELEMENTS_ALONG), 1.0, 6.0, ((4, 16), (5, 2)), jnp.float32)
    kappa = jnp.clip(jnp.exp(math.log(3.0) - 2.3025851 * jax.random.uniform(splits[1], (ELEMENTS_DEPTH, ELEMENTS_ACROSS, ELEMENTS_ALONG), jnp.float32) ** block_scale(splits[1], (ELEMENTS_DEPTH, ELEMENTS_ACROSS, ELEMENTS_ALONG), ((1, 16), (2, 2)), -0.2, 0.2)), 0.3, 3.0)
    wet = set_ends((jax.random.randint(splits[2], (ELEMENTS_DEPTH, ELEMENTS_ACROSS, ELEMENTS_ALONG), 0, 4) < 3).astype(jnp.int32), jax.random.fold_in(splits[2], 1), 0, 1)
    return dict(load=load, kappa=kappa, wet=wet)


fine_relax = 0.25
coarse_relax = 0.4

def node_tables():
    points = np.array([-1.0, -math.sqrt(3.0 / 7.0), 0.0, math.sqrt(3.0 / 7.0), 1.0])
    weights = np.array([0.1, 49.0 / 90.0, 32.0 / 45.0, 49.0 / 90.0, 0.1])
    eye_table = np.eye(points.shape[0])
    spread = points[:, None] - points[None, :] + eye_table
    factors = np.prod(spread, axis=1)
    deriv = factors[:, None] / (factors[None, :] * spread)
    deriv = np.where(eye_table > 0, (np.sum(1.0 / spread, axis=1) - 1.0)[:, None], deriv)
    stiff = deriv.T @ (weights[:, None] * deriv)
    mass = eye_table * weights[:, None]
    interp = np.stack([(1.0 - points) / 2.0, (1.0 + points) / 2.0], axis=1)
    coarse_stiff = interp.T @ stiff @ interp
    coarse_mass = interp.T @ mass @ interp
    return [jnp.asarray(table, jnp.float32) for table in (stiff, mass, interp, coarse_stiff, coarse_mass)]

def along(matrix, field, axis):
    if axis == 0:
        return jnp.einsum('pa,a...->p...', matrix, field, precision=lax.Precision.HIGHEST)
    if axis == 1:
        return jnp.einsum('qb,ab...->aq...', matrix, field, precision=lax.Precision.HIGHEST)
    return jnp.einsum('rc,abc...->abr...', matrix, field, precision=lax.Precision.HIGHEST)

def element_apply(field, coeff, stiff, mass):
    mass_c = along(mass, field, 2)
    mass_bc = along(mass, mass_c, 1)
    first_term = along(stiff, mass_bc, 0)
    second_term = along(mass, along(stiff, mass_c, 1), 0)
    third_term = along(mass, along(mass, along(stiff, field, 2), 1), 0)
    return coeff * (first_term + second_term + third_term)

def element_diagonal(coeff, stiff, mass):
    stiff_diag = jnp.diagonal(stiff)
    mass_diag = jnp.diagonal(mass)
    local = stiff_diag[:, None, None] * mass_diag[None, :, None] * mass_diag[None, None, :] + mass_diag[:, None, None] * stiff_diag[None, :, None] * mass_diag[None, None, :] + mass_diag[:, None, None] * mass_diag[None, :, None] * stiff_diag[None, None, :]
    return local[:, :, :, None, None, None] * coeff[None, None, None]

def pair_sum(field, node_axis, fetch):
    count = field.shape[node_axis]
    lower = lax.index_in_dim(field, 0, node_axis, keepdims=False)
    upper = lax.index_in_dim(field, count - 1, node_axis, keepdims=False)
    elem_axis = node_axis + 2
    length = lower.shape[elem_axis]
    lower_first = lax.slice_in_dim(lower, 0, 1, axis=elem_axis)
    upper_last = lax.slice_in_dim(upper, length - 1, length, axis=elem_axis)
    outer = fetch(jnp.concatenate([lower_first, upper_last], axis=elem_axis))
    inner = lax.slice_in_dim(upper, 0, length - 1, axis=elem_axis) + lax.slice_in_dim(lower, 1, length, axis=elem_axis)
    head = lower_first + lax.slice_in_dim(outer, 0, 1, axis=elem_axis)
    tail = upper_last + lax.slice_in_dim(outer, 3, 4, axis=elem_axis)
    new_lower = jnp.concatenate([head, inner], axis=elem_axis)
    new_upper = jnp.concatenate([inner, tail], axis=elem_axis)
    middle = lax.slice_in_dim(field, 1, count - 1, axis=node_axis)
    return jnp.concatenate([jnp.expand_dims(new_lower, node_axis), middle, jnp.expand_dims(new_upper, node_axis)], axis=node_axis)

def pad_edge(axis):

    def padded(edge):
        widths = [(1, 1) if dim == axis else (0, 0) for dim in range(edge.ndim)]
        return jnp.pad(edge, widths)
    return padded

def assemble(field, fetch_x, fetch_y, fetch_z):
    field = pair_sum(field, 2, fetch_x)
    field = pair_sum(field, 1, fetch_y)
    return pair_sum(field, 0, fetch_z)

def surface_mask(count, layers, offset, total):
    node = jnp.arange(count, dtype=jnp.int32)[:, None]
    layer = jnp.arange(layers, dtype=jnp.int32)[None, :] + offset
    keep = jnp.where((node == count - 1) & (layer == total - 1), jnp.float32(0.0), jnp.float32(1.0))
    return keep.reshape(count, 1, 1, layers, 1, 1)

def coarse_sweeps(local, coeff, coarse_sum, keep, inverse, coarse_stiff, coarse_mass):
    restricted = keep * coarse_sum(local)
    correction = inverse * restricted
    for sweep in range(NC - 1):
        image = keep * coarse_sum(element_apply(correction, coeff, coarse_stiff, coarse_mass))
        correction = correction + inverse * (restricted - image)
    return correction

def multigrid(load, coeff, fine_sum, keep, coarse_correct, tables):
    stiff, mass, interp, coarse_stiff, coarse_mass = tables
    inverse = fine_relax / fine_sum(element_diagonal(coeff, stiff, mass))
    rhs = keep * fine_sum(load)
    solution = jnp.zeros_like(load)

    def sweep_once(solution):
        change = keep * fine_sum(load - element_apply(solution, coeff, stiff, mass))
        return solution + inverse * change
    transpose = interp.T
    for cycle in range(CYCLES):
        for sweep in range(NPRE):
            if cycle == 0 and sweep == 0:
                solution = solution + inverse * rhs
            else:
                solution = sweep_once(solution)
        local = load - element_apply(solution, coeff, stiff, mass)
        local = along(transpose, along(transpose, along(transpose, local, 2), 1), 0)
        correction = coarse_correct(local)
        solution = solution + along(interp, along(interp, along(interp, correction, 2), 1), 0)
        for sweep in range(NPOST):
            solution = sweep_once(solution)
    residual = keep * fine_sum(load - element_apply(solution, coeff, stiff, mass))
    return (solution, residual)

def reference(load, kappa, wet):
    tables = node_tables()
    stiff, mass, interp, coarse_stiff, coarse_mass = tables
    coeff = kappa * jnp.where(wet == 1, jnp.float32(1.0), jnp.float32(0.05))

    def whole_sum(field):
        return assemble(field, pad_edge(4), pad_edge(3), pad_edge(2))
    fine_retain_mask = surface_mask(LOBATTO_NODES, ELEMENTS_DEPTH, 0, ELEMENTS_DEPTH)
    coarse_retain_mask = surface_mask(2, ELEMENTS_DEPTH, 0, ELEMENTS_DEPTH)
    coarse_inverse = coarse_relax / whole_sum(element_diagonal(coeff, coarse_stiff, coarse_mass))

    def coarse_correct(local):
        return coarse_sweeps(local, coeff, whole_sum, coarse_retain_mask, coarse_inverse, coarse_stiff, coarse_mass)
    return multigrid(load, coeff, whole_sum, fine_retain_mask, coarse_correct, tables)
```

```python
import functools
import math

import jax
import jax.numpy as jnp
import numpy as np
from jax import lax
from jax.experimental import pallas as pl
from jax.experimental.pallas import tpu as pltpu
from jax.sharding import PartitionSpec as P

N = 5
CYCLES = 2
NPRE = 2
NPOST = 2
NC = 4
PERIOD = NPRE + NPOST
FINE_RELAX = 0.25
COARSE_RELAX = 0.4
STEPS = CYCLES * PERIOD + 1
REACH = NC + 2
SPAN = 2 * REACH
OWN = REACH
HALO = 32
MESH = pl.DeviceIdType.MESH
F32 = jnp.float32


def node_tables():
    points = np.array([-1.0, -math.sqrt(3.0 / 7.0), 0.0, math.sqrt(3.0 / 7.0), 1.0])
    weights = np.array([0.1, 49.0 / 90.0, 32.0 / 45.0, 49.0 / 90.0, 0.1])
    eye_table = np.eye(points.shape[0])
    spread = points[:, None] - points[None, :] + eye_table
    factors = np.prod(spread, axis=1)
    deriv = factors[:, None] / (factors[None, :] * spread)
    deriv = np.where(eye_table > 0, (np.sum(1.0 / spread, axis=1) - 1.0)[:, None], deriv)
    stiff = deriv.T @ (weights[:, None] * deriv)
    mass = eye_table * weights[:, None]
    interp = np.stack([(1.0 - points) / 2.0, (1.0 + points) / 2.0], axis=1)
    return stiff, weights, interp, interp.T @ stiff @ interp, interp.T @ mass @ interp


S, WEIGHTS, INTERP, SC, WC = node_tables()
ALPHA = (S[0, 0] + S[0, 4]) / 2
BETA = (S[0, 1] + S[0, 3]) / 2
GAMMA = (S[1, 1] + S[1, 3]) / 2
KAPPA = (S[0, 1] - S[0, 3]) / (S[0, 0] - S[0, 4])
ODD = (S[0, 0] - S[0, 4]) / 2
DELTA = (S[1, 1] - S[1, 3]) / (2 * KAPPA ** 2) - ODD
W0, W1, W2 = WEIGHTS[:3]
MU = [W0 / 2, W1 / 2, W2 / 4, W1 / (2 * KAPPA ** 2), W0 / 2]
MUB = [W0, W1 / 2, W2 / 4, W1 / (2 * KAPPA ** 2), W0]
NU = [1.0, 2.0, 4.0, 2 * KAPPA ** 2, 1.0]
SLOPE = KAPPA * (INTERP[1, 0] - INTERP[3, 0])
RISE = ODD * (1 + SLOPE)
NODE = [0, 1, 2, 1, 4]
DIAG = np.diag(S) / WEIGHTS
W3 = WEIGHTS[:, None, None] * WEIGHTS[None, :, None] * WEIGHTS[None, None, :]
K3 = W3 * (DIAG[:, None, None] + DIAG[None, :, None] + DIAG[None, None, :])
CS = (SC[0, 0] - SC[0, 1]) / 2
CE, CO = (WC[0, 0] + WC[0, 1]) / 2, (WC[0, 0] - WC[0, 1]) / 2
C1, C2, C3 = CS * CE * CE, 2 * CS * CO * CE, 3 * CS * CO * CO
SENDS = [d for d in range(-REACH + 1, REACH + 1) if d != 0]
RECVS = [d for d in range(-REACH, REACH) if d != 0]


def st(b, a, c):
    return (b * 4 + a) * 4 + c


def xi(b, i, k):
    return (b * N + i) * N + k


def line_apply(e0, e1, z, o1, o0, scale):
    q0, q1 = e0 - z, e1 - z
    r0 = float(ALPHA * scale) * q0 + float(BETA * scale) * q1
    r1 = float(BETA * scale) * q0 + float(GAMMA * scale) * q1
    s0 = float(ODD * scale) * (o0 + o1)
    return r0, r1, r0 + r1, s0 + float(DELTA * scale) * o1, s0


def plus(x, y):
    if x is None or y is None:
        return x if y is None else y
    return x + y


def minus(x, y):
    if y is None:
        return x
    return -y if x is None else x - y


def kernel(
    sizes, load_ref, kappa_ref, wet_ref, sol_out, res_out,
    ghost_load, halo_pack, halo_got, own_coeff, other_coeff, coeffs,
    rhs, sol, tot, sinv, xs, bs, face, packed, got, cgot, cinv,
    ex_send, ex_recv, k_send, k_recv, f_send, f_recv, c_send, c_recv,
):
    ex_count, ey_count, lin_count, layers, width = sizes
    ex, ey, lin = lax.axis_index("ex"), lax.axis_index("ey"), lax.axis_index("lin")
    rows = ey_count * lin_count
    row = ey * lin_count + lin
    par = lax.rem(lin, 2)
    sgn = 1 - 2 * par
    fold = width // HALO
    groups = -(-N * N // fold)

    sub = lax.broadcasted_iota(jnp.int32, (2 * layers, width), 0)
    lane = lax.broadcasted_iota(jnp.int32, (2 * layers, width), 1)
    layer = sub % layers
    bottom, top = layer == 0, layer == layers - 1
    first_lane, last_lane = lane == 0, lane == width - 1
    near = jnp.where(ex == 0, lane, width - 1 - lane)
    real = (sub < layers) | (near < HALO)
    lower = sub < layers

    def before(x):
        y = pltpu.roll(x, 1, 1)
        return jnp.where(first_lane, pltpu.roll(y, layers, 0), y)

    def after(x):
        y = pltpu.roll(x, width - 1, 1)
        return jnp.where(last_lane, pltpu.roll(y, layers, 0), y)

    def below(low, high):
        return jnp.where(bottom, low, low + pltpu.roll(high, 1, 0))

    def above(low):
        return jnp.where(top, 0.0, pltpu.roll(low, 2 * layers - 1, 0))

    def there(d):
        at = row + sgn * d
        return (at >= 0) & (at < rows)

    def place(d, other=False):
        at = row + sgn * d
        return (1 - ex if other else ex, at // lin_count, at % lin_count)

    def when_there(d, fn):
        @pl.when(there(d))
        def _():
            fn(d)

    def slot_at(d):
        return REACH + (-d if d % 2 == 0 else d)

    def remote(src, dst, send, recv, device):
        return pltpu.make_async_remote_copy(
            src_ref=src, dst_ref=dst, send_sem=send, recv_sem=recv, device_id=device, device_id_type=MESH)

    coeffs[...] = jnp.zeros_like(coeffs)
    cgot[...] = jnp.zeros_like(cgot)

    @pl.when(jnp.logical_not(there(-1)))
    def _():
        ghost_load[...] = jnp.zeros_like(ghost_load)
        halo_got[1] = jnp.zeros_like(halo_got[1])

    def greet(device):
        pl.semaphore_signal(pltpu.get_barrier_semaphore(), inc=1, device_id=device, device_id_type=MESH)

    greet((1 - ex, ey, lin))
    when_there(-1, lambda d: greet(place(d, True)))
    expected = 1 + there(-1).astype(jnp.int32)
    for d in range(1, REACH + 1):
        for e in (-d, d):
            when_there(e, lambda e: greet(place(e)))
            expected = expected + there(e).astype(jnp.int32)

    coeff_own = kappa_ref[...] * jnp.where(wet_ref[...] == 1, F32(1.0), F32(0.05))
    own_coeff[...] = coeff_own

    def raw(a, b, c):
        return (a * N + b + par * (N - 1 - 2 * b)) * N + c

    half_lane = lax.broadcasted_iota(jnp.int32, (layers, width), 1)
    source = jnp.where(ex == 0, fold - 1, 0)
    turn = (half_lane // HALO + fold - source) % fold

    def pack_plane(b, _):
        for g in range(groups):
            mixed = None
            for j in range(fold):
                n = g * fold + j
                if n < N * N:
                    x = load_ref[raw(n // N, b, n % N)]
                    mixed = x if j == 0 else jnp.where(turn == j, pltpu.roll(x, HALO * j, 1), mixed)
            halo_pack[b * groups + g] = mixed
        return 0

    lax.fori_loop(0, N, pack_plane, 0)
    pl.semaphore_wait(pltpu.get_barrier_semaphore(), expected)

    across = (1 - ex, ey, lin)
    coeff_copy = remote(own_coeff, other_coeff, ex_send.at[0], ex_recv.at[0], across)
    halo_copy = remote(halo_pack, halo_got.at[0], ex_send.at[1], ex_recv.at[1], across)

    def load_copy():
        return remote(load_ref, ghost_load, ex_send.at[2], ex_recv.at[2], place(-1))

    def corner_copy():
        return remote(halo_pack, halo_got.at[1], ex_send.at[3], ex_recv.at[3], place(-1, True))

    coeff_copy.start()
    halo_copy.start()
    when_there(-1, lambda d: load_copy().start())
    when_there(-1, lambda d: corner_copy().start())

    coeff_copy.wait()
    coeffs[OWN] = jnp.where(real, jnp.concatenate([coeff_own, other_coeff[...]], axis=0), 0.0)
    for d in SENDS:
        when_there(d, lambda d: remote(
            coeffs.at[OWN], coeffs.at[slot_at(d)], k_send.at[REACH + d], k_recv.at[slot_at(d)], place(d)).start())

    def to_dual(f):
        return [(f[1] + f[3]) * 0.5, f[2] * 0.5, (f[1] - f[3]) * float(0.5 / KAPPA)]

    def load_plane(r, b, own_ref):
        source_b = b if r == 0 else N - 1 - b
        tiles = []
        for n in range(N * N):
            mine = own_ref[raw(n // N, b, n % N)]
            other = halo_got[r, source_b * groups + n // fold]
            j = n % fold
            if j:
                other = pltpu.roll(other, width - HALO * j, 1)
            tiles.append(jnp.where(real, jnp.concatenate([mine, other], axis=0), 0.0))
        lines = []
        for a in range(N):
            f = tiles[a * N:a * N + N]
            lines.append([f[0] + before(f[4])] + to_dual(f))
        columns = []
        for c in range(4):
            f = [lines[a][c] for a in range(N)]
            columns.append([below(f[0], f[4])] + to_dual(f))
        return [[columns[c][a] for c in range(4)] for a in range(4)]

    def build_rhs(r, own_ref):
        for b, at in ((0, 0), (4, 4), (2, 2), (1, 1), (3, 3)):
            p = load_plane(r, b, own_ref)
            for a in range(4):
                for c in range(4):
                    x = p[a][c]
                    if b == 2:
                        x = x * 0.5
                    if b == 3:
                        first = rhs[r, st(1, a, c)]
                        rhs[r, st(3, a, c)] = (first - x) * float(0.5 / KAPPA)
                        rhs[r, st(1, a, c)] = (first + x) * 0.5
                    else:
                        rhs[r, st(at, a, c)] = x

    halo_copy.wait()
    build_rhs(0, load_ref)

    block = lax.rem(lane + jnp.where(ex == 0, 0, HALO - 1), width) // HALO

    def swap(x):
        return pltpu.roll(x, layers, 0)

    def pack(s, x):
        for p in range(8):
            packed[s, p] = jnp.where(lower, x[2 * p], swap(x[2 * p + 1]))
        for p in range(8 // fold):
            halves = []
            for h in range(2):
                group = x[(2 * p + h) * fold:(2 * p + h + 1) * fold]
                mixed = group[0]
                for j in range(1, fold):
                    mixed = jnp.where(block == j, pltpu.roll(group[j], HALO * j, 1), mixed)
                halves.append(mixed)
            packed[s, 8 + p] = jnp.where(lower, swap(halves[0]), halves[1])

    def unpack(kind, s):
        x = []
        for p in range(8 // fold):
            tile = got[kind, s, 8 + p]
            for half in (swap(tile), tile):
                for j in range(fold):
                    other = half if j == 0 else pltpu.roll(half, width - HALO * j, 1)
                    n = len(x)
                    mine = got[kind, s, n // 2]
                    mine = mine if n % 2 == 0 else swap(mine)
                    x.append(jnp.where(lower, mine, jnp.where(block == 0, other, 0.0)))
        return x

    def near_copy(s):
        return remote(packed.at[s], got.at[0, s], f_send.at[0, s], f_recv.at[0, s], place(1))

    def far_copy(s):
        return remote(packed.at[s], got.at[1, s], f_send.at[1, s], f_recv.at[1, s], place(2))

    def send_face(s, values):
        pack(s, values)
        near_copy(s).start()

        @pl.when(there(2) & (s < STEPS - 1))
        def _():
            far_copy(s).start()

    def add_near(s):
        near_copy(s).wait()
        for n, x in enumerate(unpack(0, s)):
            tot[0, 64 + n] = tot[0, 64 + n] + x

    def add_far(s):
        @pl.when(there(-2))
        def _():
            far_copy(s).wait_recv()
            for n, x in enumerate(unpack(1, s)):
                tot[1, n] = tot[1, n] + x

    def expand(r):
        for b in range(N):
            w = []
            for a in range(4):
                v = [sol[r, st(b, a, c)] for c in range(4)]
                up = after(v[0])
                w.append([v[0] + up, v[1], v[2], v[3], v[0] - up])
            for k in range(N):
                up = above(w[0][k])
                xs[r, xi(b, 0, k)] = w[0][k] + up
                xs[r, xi(b, 4, k)] = w[0][k] - up
                for a in range(1, 4):
                    xs[r, xi(b, a, k)] = w[a][k]

    def cross(r):
        for i in range(N):
            for k in range(N):
                v = [xs[r, xi(b, i, k)] for b in range(N)]
                r0, r1, rz, s1, s0 = line_apply(v[0] + v[4], v[1], v[2], v[3], v[0] - v[4], MU[i] * MU[k])
                for b, x in enumerate((r0 + s0, r1, rz, s1, r0 - s0)):
                    bs[r, xi(b, i, k)] = x

    def gather(y):
        g = []
        for k in range(N):
            low, high = plus(y[0][k], y[4][k]), minus(y[0][k], y[4][k])
            g.append([None if low is None else below(low, high)] + [y[i][k] for i in range(1, 4)])
        h = []
        for a in range(4):
            low, high = plus(g[0][a], g[4][a]), minus(g[0][a], g[4][a])
            h.append([None if low is None else low + before(high)] + [g[k][a] for k in range(1, 4)])
        return h

    def plane(r, b):
        coeff = coeffs[OWN - r]
        x = [[xs[r, xi(b, i, k)] for k in range(N)] for i in range(N)]
        along_c = [line_apply(*x[i], MUB[b] * MU[i]) for i in range(N)]
        along_a = [line_apply(*[x[i][k] for i in range(N)], MUB[b] * MU[k]) for k in range(N)]
        y = []
        for i in range(N):
            line = []
            for k in range(N):
                terms = sorted(((b == 2, bs[r, xi(b, i, k)]), (k == 2, along_c[i][k]), (i == 2, along_a[k][i])),
                               key=lambda t: t[0])
                total = -terms[0][1] if terms[0][0] else terms[0][1]
                for negative, term in terms[1:]:
                    total = total - term if negative else total + term
                line.append(coeff * total)
            y.append(line)
        h = gather(y)
        return [rhs[r, st(b, a, c)] - h[a][c] for a in range(4) for c in range(4)]

    def put(r, b, values):
        for n, x in enumerate(values):
            tot[r, b * 16 + n] = x

    def update(r, b):
        for n in range(b * 16, b * 16 + 16):
            sol[r, n] = sol[r, n] + sinv[r, n] * tot[r, n]

    def inverted(x):
        return jnp.where(x > 0.0, 1.0 / jnp.where(x > 0.0, x, 1.0), 0.0)

    def invert():
        for r in range(2):
            here = coeffs[OWN - r]
            for bl, x in (((1, 2, 3), here), ((0,), here + coeffs[OWN - r - 1]), ((4,), here + coeffs[OWN - r + 1])):
                xc = x + before(x)
                tiles = [[inverted(below(xc, xc)), inverted(below(x, x))], [inverted(xc), inverted(x)]]
                for b in bl:
                    for a in range(4):
                        for c in range(4):
                            factor = FINE_RELAX * NU[a] * NU[b] * NU[c] / K3[NODE[a], NODE[b], NODE[c]]
                            sinv[r, st(b, a, c)] = float(factor) * tiles[min(a, 1)][min(c, 1)]
        corner = 3.0 * SC[0, 0] * WC[0, 0] ** 2
        for i in range(SPAN - 1):
            pair = coeffs[i] + coeffs[i + 1]
            pair = pair + before(pair)
            cinv[i] = float(COARSE_RELAX / corner) * inverted(below(pair, pair))

    def halves(v):
        even, odd = v[1] + v[2], float(SLOPE) * v[3]
        return even + odd, even - odd

    def coarse_send(cycle):
        q = [[], []]
        for n in range(16):
            v = [face[0, n], tot[0, 16 + n], tot[0, 32 + n], tot[0, 48 + n]]
            low, high = halves(v)
            q[0].append(v[0] + low)
            q[1].append(face[1, n] + high)
        for j in range(2):
            lines = []
            for a in range(4):
                v = q[j][a * 4:a * 4 + 4]
                low, high = halves(v)
                lines.append((v[0] + low) + before(high))
            low, high = halves(lines)
            cgot[cycle, OWN, j] = below(lines[0] + low, high)
        for d in SENDS:
            when_there(d, lambda d: remote(
                cgot.at[cycle, OWN], cgot.at[cycle, slot_at(d)], c_send.at[REACH + d], c_recv.at[cycle, slot_at(d)],
                place(d)).start())

    def correct(cycle):
        for d in SENDS:
            when_there(d, lambda d: remote(
                cgot.at[cycle, OWN], cgot.at[cycle, OWN], c_send.at[REACH + d], c_recv.at[cycle, OWN],
                place(d)).wait_send())
        for d in RECVS:
            when_there(d, lambda d: remote(
                cgot.at[cycle, OWN], cgot.at[cycle, REACH + d], c_send.at[OWN], c_recv.at[cycle, REACH + d],
                place(d)).wait_recv())

        def q(e, j):
            return cgot[cycle, e, j if (e - OWN) % 2 == 0 else 1 - j]

        lines = SPAN - 1
        rc = [q(i, 1) + q(i + 1, 0) for i in range(lines)]
        x = [cinv[i] * rc[i] for i in range(lines)]

        def modes(v):
            up = after(v)
            parts = []
            for k in (v + up, v - up):
                high = above(k)
                parts.append((k + high, k - high))
            return [[parts[k][i] for k in range(2)] for i in range(2)]

        first, last = 0, lines - 1
        for sweep in range(NC - 1):
            m = {i: modes(x[i]) for i in range(first, last + 1)}
            sides = {}
            for e in range(first + 1, last + 1):
                coeff = coeffs[e]
                factor = [float(C1) * coeff, float(C2) * coeff, float(C3) * coeff]
                low, high = m[e - 1], m[e]
                part = []
                for i in range(2):
                    pair = []
                    for k in range(2):
                        odd = factor[i + k] * (low[i][k] - high[i][k])
                        if i + k == 0:
                            pair.append((odd, -odd))
                        else:
                            even = factor[i + k - 1] * (low[i][k] + high[i][k])
                            pair.append((even + odd, even - odd))
                    part.append(pair)
                sides[e] = part
            first, last = first + 1, last - 1
            new = list(x)
            for i in range(first, last + 1):
                y = [[sides[i + 1][a][k][0] + sides[i][a][k][1] for k in range(2)] for a in range(2)]
                g = [below(y[0][k] + y[1][k], y[0][k] - y[1][k]) for k in range(2)]
                image = (g[0] + g[1]) + before(g[0] - g[1])
                new[i] = x[i] + cinv[i] * (rc[i] - image)
            x = new

        base = OWN - 3
        m = {i: modes(x[i]) for i in range(base, base + 5)}
        kind = [0, 0, 0, 1, 1]
        grow = [1.0, 1.0, 1.0, SLOPE, 1.0]

        def ends(centre, weight, tilt):
            y = [[None] * N for _ in range(N)]
            for i in range(N):
                for k in range(N):
                    value = None
                    if centre is not None:
                        value = float(MU[i] * MU[k] * grow[i] * grow[k]) * centre[kind[i]][kind[k]]
                    if i == 4:
                        value = plus(value, float(RISE * weight * MU[k] * grow[k]) * tilt[1][kind[k]])
                    if k == 4:
                        value = plus(value, float(RISE * weight * MU[i] * grow[i]) * tilt[kind[i]][1])
                    y[i][k] = value
            return gather(y)

        def face_image(i):
            up, down = coeffs[i + 1], coeffs[i]
            both = up + down
            centre = [[float(RISE) * (up * (m[i][a][k] - m[i + 1][a][k]) - down * (m[i - 1][a][k] - m[i][a][k]))
                       for k in range(2)] for a in range(2)]
            tilt = [[None if a + k == 0 else both * m[i][a][k] for k in range(2)] for a in range(2)]
            h = ends(centre, W0, tilt)
            return [h[a][c] for a in range(4) for c in range(4)]

        for i, targets in ((OWN - 2, ((1, 0),)), (OWN - 1, ((1, 64), (0, 0))), (OWN, ((0, 64),))):
            values = face_image(i)
            for r, at in targets:
                for n, value in enumerate(values):
                    tot[r, at + n] = tot[r, at + n] - value
        scale = [1.0, 1.0, 1.0, SLOPE]

        def nodal(i):
            v = x[i]
            up = after(v)
            high = above(v)
            tiles = [[v, v + up, v - up], [v + high, m[i][0][0], m[i][0][1]], [v - high, m[i][1][0], m[i][1][1]]]
            pick = [0, 1, 1, 2]
            made = {}
            out = []
            for a in range(4):
                for c in range(4):
                    key = (pick[a], pick[c])
                    if key not in made:
                        factor = float(scale[a] * scale[c])
                        made[key] = tiles[key[0]][key[1]] if factor == 1.0 else factor * tiles[key[0]][key[1]]
                    out.append((key, made[key]))
            return out

        at_line = {i: nodal(i) for i in (OWN - 2, OWN - 1, OWN)}
        for r in range(2):
            low, high = OWN - 1 - r, OWN - r
            coeff = coeffs[OWN - r]
            for kindb in range(2):
                diff = [[None if a + k == 0 else
                         coeff * (m[low][a][k] - m[high][a][k] if kindb else m[low][a][k] + m[high][a][k])
                         for k in range(2)] for a in range(2)]
                h = ends(None, 1.0, diff)
                for b in ((3,) if kindb else (1, 2)):
                    factor = float(MUB[b] * (SLOPE if kindb else 1.0))
                    for a in range(4):
                        for c in range(4):
                            if h[a][c] is not None:
                                tot[r, st(b, a, c)] = tot[r, st(b, a, c)] - factor * h[a][c]
                made = {}
                for n in range(16):
                    key, lower_value = at_line[low][n]
                    upper_value = at_line[high][n][1]
                    if key not in made:
                        made[key] = (float(SLOPE) * (lower_value - upper_value) if kindb
                                     else lower_value + upper_value)
                    for b in ((3,) if kindb else (1, 2)):
                        sol[r, b * 16 + n] = sol[r, b * 16 + n] + made[key]
            for n in range(16):
                sol[r, n] = sol[r, n] + at_line[low][n][1]
                sol[r, 64 + n] = sol[r, 64 + n] + at_line[high][n][1]

    def emit(field, out_ref, dual):
        def split(mid, double, odd):
            if dual:
                odd = float(KAPPA) * odd
                return mid + odd, 2.0 * double, mid - odd
            even, odd = 0.5 * mid, float(0.5 / KAPPA) * odd
            return even + odd, 0.5 * double, even - odd

        def one(b, values):
            lines = []
            for a in range(4):
                v = values[a * 4:a * 4 + 4]
                lines.append([v[0], *split(*v[1:]), after(v[0])])
            for c in range(N):
                v = [lines[a][c] for a in range(4)]
                for a, tile in enumerate([v[0], *split(*v[1:]), above(v[0])]):
                    out_ref[raw(a, b, c)] = tile[0:layers]

        for b in (0, 4):
            one(b, [field[0, b * 16 + n] for n in range(16)])
        mids = [split(field[0, 16 + n], field[0, 32 + n], field[0, 48 + n]) for n in range(16)]
        for b in range(1, 4):
            one(b, [v[b - 1] for v in mids])

    for b in range(N):
        put(0, b, [rhs[0, b * 16 + n] for n in range(16)])
    send_face(0, [tot[0, 64 + n] for n in range(16)])
    sol[...] = jnp.zeros_like(sol)
    for d in SENDS:
        when_there(d, lambda d: remote(
            coeffs.at[OWN], coeffs.at[OWN], k_send.at[REACH + d], k_recv.at[OWN], place(d)).wait_send())
    for d in RECVS:
        when_there(d, lambda d: remote(
            coeffs.at[OWN], coeffs.at[REACH + d], k_send.at[OWN], k_recv.at[REACH + d], place(d)).wait_recv())
    invert()
    when_there(-1, lambda d: load_copy().wait())
    when_there(-1, lambda d: corner_copy().wait())
    build_rhs(1, ghost_load)
    for b in range(N):
        put(1, b, [rhs[1, b * 16 + n] for n in range(16)])
    for n in range(16):
        joined = tot[0, n] + tot[1, 64 + n]
        tot[0, n] = joined
        tot[1, 64 + n] = joined
    for b in range(4):
        update(0, b)
        update(1, b + 1)
    add_near(0)
    update(0, 4)

    def step(s, _):
        cycle = s // PERIOD
        live = s < STEPS - 1
        coarse = (lax.rem(s, PERIOD) == NPRE) & live
        deferred = lax.rem(s - 1, PERIOD) != NPRE

        expand(0)
        cross(0)
        mine = plane(0, 4)
        for n in range(16):
            face[1, n] = mine[n]
        put(0, 4, mine)
        send_face(s, mine)

        @pl.when(there(2))
        def _():
            far_copy(s - 1).wait_send()

        @pl.when(deferred)
        def _():
            add_far(s - 1)
            update(1, 0)

        expand(1)
        cross(1)
        ghost = plane(1, 4)
        mine = plane(0, 0)
        for n in range(16):
            face[0, n] = mine[n]
            joined = mine[n] + ghost[n]
            tot[0, n] = joined
            tot[1, 64 + n] = joined
        for b in range(1, 4):
            put(0, b, plane(0, b))

        @pl.when(coarse)
        def _():
            coarse_send(cycle)

        @pl.when(live)
        def _():
            for b in range(4):
                put(1, b, plane(1, b))

        @pl.when(jnp.logical_not(live))
        def _():
            emit(sol, sol_out, False)

        @pl.when(jnp.logical_not(coarse))
        def _():
            for b in range(4):
                update(0, b)
                update(1, b + 1)

        add_near(s)

        @pl.when(coarse)
        def _():
            add_far(s)
            correct(cycle)
            for b in range(4):
                update(0, b)
                update(1, b + 1)
            update(1, 0)

        update(0, 4)
        return 0

    lax.fori_loop(1, STEPS, step, 0)
    emit(tot, res_out, True)


def per_device(sizes, load, kappa, wet):
    layers, _, width = kappa.shape
    nodes = N * N * N
    tile = (2 * layers, width)
    half = (layers, width)
    sizes = sizes + (layers, width)
    out = jax.ShapeDtypeStruct((nodes, layers, width), F32)
    vmem = pl.BlockSpec(memory_space=pltpu.VMEM)
    fold = width // HALO
    groups = -(-N * N // fold)
    messages = 8 + 8 // fold
    dma = pltpu.SemaphoreType.DMA
    solution, residual = pl.pallas_call(
        functools.partial(kernel, sizes),
        out_shape=(out, out),
        in_specs=[vmem] * 3,
        out_specs=(vmem, vmem),
        scratch_shapes=[
            pltpu.VMEM((nodes,) + half, F32),
            pltpu.VMEM((N * groups,) + half, F32),
            pltpu.VMEM((2, N * groups) + half, F32),
            pltpu.VMEM(half, F32),
            pltpu.VMEM(half, F32),
            pltpu.VMEM((SPAN,) + tile, F32),
            pltpu.VMEM((2, 80) + tile, F32),
            pltpu.VMEM((2, 80) + tile, F32),
            pltpu.VMEM((2, 80) + tile, F32),
            pltpu.VMEM((2, 80) + tile, F32),
            pltpu.VMEM((2, nodes) + tile, F32),
            pltpu.VMEM((2, nodes) + tile, F32),
            pltpu.VMEM((2, 16) + tile, F32),
            pltpu.VMEM((STEPS, messages) + tile, F32),
            pltpu.VMEM((2, STEPS, messages) + tile, F32),
            pltpu.VMEM((CYCLES, SPAN, 2) + tile, F32),
            pltpu.VMEM((SPAN - 1,) + tile, F32),
            dma((4,)), dma((4,)), dma((SPAN + 1,)), dma((SPAN + 1,)),
            dma((2, STEPS)), dma((2, STEPS)), dma((SPAN + 1,)), dma((CYCLES, SPAN + 1)),
        ],
        compiler_params=pltpu.CompilerParams(collective_id=0, has_side_effects=True),
    )(load.reshape(nodes, layers, width), kappa.reshape(layers, width), wet.reshape(layers, width))
    return solution.reshape(load.shape), residual.reshape(load.shape)


def solution(mesh):
    sizes = tuple(mesh.shape[name] for name in ("ex", "ey", "lin"))
    field = P(None, None, None, None, ("ey", "lin"), "ex")
    cell = P(None, ("ey", "lin"), "ex")
    return jax.shard_map(
        functools.partial(per_device, sizes), mesh=mesh, in_specs=(field, cell, cell),
        out_specs=(field, field), check_vma=False,
    )
```

```python
import functools
import math

import jax
import jax.numpy as jnp
import numpy as np
from jax import lax
from jax.experimental import pallas as pl
from jax.experimental.pallas import tpu as pltpu
from jax.sharding import PartitionSpec as P

N = 5
CYCLES = 2
NPRE = 2
NPOST = 2
NC = 4
PERIOD = NPRE + NPOST
FINE_RELAX = 0.25
COARSE_RELAX = 0.4
STEPS = CYCLES * PERIOD + 1
REACH = NC + 2
SPAN = 2 * REACH
OWN = REACH
HALO = 32
MESH = pl.DeviceIdType.MESH
F32 = jnp.float32


def node_tables():
    points = np.array([-1.0, -math.sqrt(3.0 / 7.0), 0.0, math.sqrt(3.0 / 7.0), 1.0])
    weights = np.array([0.1, 49.0 / 90.0, 32.0 / 45.0, 49.0 / 90.0, 0.1])
    eye_table = np.eye(points.shape[0])
    spread = points[:, None] - points[None, :] + eye_table
    factors = np.prod(spread, axis=1)
    deriv = factors[:, None] / (factors[None, :] * spread)
    deriv = np.where(eye_table > 0, (np.sum(1.0 / spread, axis=1) - 1.0)[:, None], deriv)
    stiff = deriv.T @ (weights[:, None] * deriv)
    mass = eye_table * weights[:, None]
    interp = np.stack([(1.0 - points) / 2.0, (1.0 + points) / 2.0], axis=1)
    return stiff, weights, interp, interp.T @ stiff @ interp, interp.T @ mass @ interp


S, WEIGHTS, INTERP, SC, WC = node_tables()
ALPHA = (S[0, 0] + S[0, 4]) / 2
BETA = (S[0, 1] + S[0, 3]) / 2
GAMMA = (S[1, 1] + S[1, 3]) / 2
KAPPA = (S[0, 1] - S[0, 3]) / (S[0, 0] - S[0, 4])
ODD = (S[0, 0] - S[0, 4]) / 2
DELTA = (S[1, 1] - S[1, 3]) / (2 * KAPPA ** 2) - ODD
W0, W1, W2 = WEIGHTS[:3]
MU = [W0 / 2, W1 / 2, W2 / 4, W1 / (2 * KAPPA ** 2), W0 / 2]
MUB = [W0, W1 / 2, W2 / 4, W1 / (2 * KAPPA ** 2), W0]
NU = [1.0, 2.0, 4.0, 2 * KAPPA ** 2, 1.0]
SLOPE = KAPPA * (INTERP[1, 0] - INTERP[3, 0])
RISE = ODD * (1 + SLOPE)
NODE = [0, 1, 2, 1, 4]
DIAG = np.diag(S) / WEIGHTS
W3 = WEIGHTS[:, None, None] * WEIGHTS[None, :, None] * WEIGHTS[None, None, :]
K3 = W3 * (DIAG[:, None, None] + DIAG[None, :, None] + DIAG[None, None, :])
CS = (SC[0, 0] - SC[0, 1]) / 2
CE, CO = (WC[0, 0] + WC[0, 1]) / 2, (WC[0, 0] - WC[0, 1]) / 2
C1, C2, C3 = CS * CE * CE, 2 * CS * CO * CE, 3 * CS * CO * CO
SENDS = [d for d in range(-REACH + 1, REACH + 1) if d != 0]
RECVS = [d for d in range(-REACH, REACH) if d != 0]


def st(b, a, c):
    return (b * 4 + a) * 4 + c


def xi(b, i, k):
    return (b * N + i) * N + k


def line_apply(e0, e1, z, o1, o0, scale):
    q0, q1 = e0 - z, e1 - z
    r0 = float(ALPHA * scale) * q0 + float(BETA * scale) * q1
    r1 = float(BETA * scale) * q0 + float(GAMMA * scale) * q1
    s0 = float(ODD * scale) * (o0 + o1)
    return r0, r1, r0 + r1, s0 + float(DELTA * scale) * o1, s0


def plus(x, y):
    if x is None or y is None:
        return x if y is None else y
    return x + y


def minus(x, y):
    if y is None:
        return x
    return -y if x is None else x - y


def kernel(
    sizes, load_ref, kappa_ref, wet_ref, sol_out, res_out,
    ghost_load, halo_pack, halo_got, own_coeff, other_coeff, coeffs,
    rhs, sol, tot, sinv, xs, bs, coarse_load, packed, got, cgot, cinv,
    ex_send, ex_recv, k_send, k_recv, f_send, f_recv, c_send, c_recv,
):
    ex_count, ey_count, lin_count, layers, width = sizes
    ex, ey, lin = lax.axis_index("ex"), lax.axis_index("ey"), lax.axis_index("lin")
    rows = ey_count * lin_count
    row = ey * lin_count + lin
    par = lax.rem(lin, 2)
    sgn = 1 - 2 * par
    fold = width // HALO
    groups = -(-N * N // fold)

    sub = lax.broadcasted_iota(jnp.int32, (2 * layers, width), 0)
    lane = lax.broadcasted_iota(jnp.int32, (2 * layers, width), 1)
    layer = sub % layers
    bottom, top = layer == 0, layer == layers - 1
    first_lane, last_lane = lane == 0, lane == width - 1
    near = jnp.where(ex == 0, lane, width - 1 - lane)
    real = (sub < layers) | (near < HALO)
    lower = sub < layers

    def before(x):
        y = pltpu.roll(x, 1, 1)
        return jnp.where(first_lane, pltpu.roll(y, layers, 0), y)

    def after(x):
        y = pltpu.roll(x, width - 1, 1)
        return jnp.where(last_lane, pltpu.roll(y, layers, 0), y)

    def below(low, high):
        return jnp.where(bottom, low, low + pltpu.roll(high, 1, 0))

    def above(low):
        return jnp.where(top, 0.0, pltpu.roll(low, 2 * layers - 1, 0))

    def there(d):
        at = row + sgn * d
        return (at >= 0) & (at < rows)

    def place(d, other=False):
        at = row + sgn * d
        return (1 - ex if other else ex, at // lin_count, at % lin_count)

    def when_there(d, fn):
        @pl.when(there(d))
        def _():
            fn(d)

    def slot_at(d):
        return REACH + (-d if d % 2 == 0 else d)

    def remote(src, dst, send, recv, device):
        return pltpu.make_async_remote_copy(
            src_ref=src, dst_ref=dst, send_sem=send, recv_sem=recv, device_id=device, device_id_type=MESH)

    coeffs[...] = jnp.zeros_like(coeffs)
    cgot[...] = jnp.zeros_like(cgot)

    @pl.when(jnp.logical_not(there(-1)))
    def _():
        ghost_load[...] = jnp.zeros_like(ghost_load)
        halo_got[1] = jnp.zeros_like(halo_got[1])

    def greet(device):
        pl.semaphore_signal(pltpu.get_barrier_semaphore(), inc=1, device_id=device, device_id_type=MESH)

    greet((1 - ex, ey, lin))
    when_there(-1, lambda d: greet(place(d, True)))
    expected = 1 + there(-1).astype(jnp.int32)
    for d in range(1, REACH + 1):
        for e in (-d, d):
            when_there(e, lambda e: greet(place(e)))
            expected = expected + there(e).astype(jnp.int32)

    coeff_own = kappa_ref[...] * jnp.where(wet_ref[...] == 1, F32(1.0), F32(0.05))
    own_coeff[...] = coeff_own

    def raw(a, b, c):
        return (a * N + b + par * (N - 1 - 2 * b)) * N + c

    half_lane = lax.broadcasted_iota(jnp.int32, (layers, width), 1)
    source = jnp.where(ex == 0, fold - 1, 0)
    turn = (half_lane // HALO + fold - source) % fold

    def pack_plane(b, _):
        for g in range(groups):
            mixed = None
            for j in range(fold):
                n = g * fold + j
                if n < N * N:
                    x = load_ref[raw(n // N, b, n % N)]
                    mixed = x if j == 0 else jnp.where(turn == j, pltpu.roll(x, HALO * j, 1), mixed)
            halo_pack[b * groups + g] = mixed
        return 0

    lax.fori_loop(0, N, pack_plane, 0)
    pl.semaphore_wait(pltpu.get_barrier_semaphore(), expected)

    across = (1 - ex, ey, lin)
    coeff_copy = remote(own_coeff, other_coeff, ex_send.at[0], ex_recv.at[0], across)
    halo_copy = remote(halo_pack, halo_got.at[0], ex_send.at[1], ex_recv.at[1], across)

    def load_copy():
        return remote(load_ref, ghost_load, ex_send.at[2], ex_recv.at[2], place(-1))

    def corner_copy():
        return remote(halo_pack, halo_got.at[1], ex_send.at[3], ex_recv.at[3], place(-1, True))

    coeff_copy.start()
    halo_copy.start()
    when_there(-1, lambda d: load_copy().start())
    when_there(-1, lambda d: corner_copy().start())

    coeff_copy.wait()
    coeffs[OWN] = jnp.where(real, jnp.concatenate([coeff_own, other_coeff[...]], axis=0), 0.0)
    for d in SENDS:
        when_there(d, lambda d: remote(
            coeffs.at[OWN], coeffs.at[slot_at(d)], k_send.at[REACH + d], k_recv.at[slot_at(d)], place(d)).start())

    def to_dual(f):
        return [(f[1] + f[3]) * 0.5, f[2] * 0.5, (f[1] - f[3]) * float(0.5 / KAPPA)]

    def load_plane(r, b, own_ref):
        source_b = b if r == 0 else N - 1 - b
        tiles = []
        for n in range(N * N):
            mine = own_ref[raw(n // N, b, n % N)]
            other = halo_got[r, source_b * groups + n // fold]
            j = n % fold
            if j:
                other = pltpu.roll(other, width - HALO * j, 1)
            tiles.append(jnp.where(real, jnp.concatenate([mine, other], axis=0), 0.0))
        lines = []
        for a in range(N):
            f = tiles[a * N:a * N + N]
            lines.append([f[0] + before(f[4])] + to_dual(f))
        columns = []
        for c in range(4):
            f = [lines[a][c] for a in range(N)]
            columns.append([below(f[0], f[4])] + to_dual(f))
        return [[columns[c][a] for c in range(4)] for a in range(4)]

    def build_rhs(r, own_ref):
        for b, at in ((0, 0), (4, 4), (2, 2), (1, 1), (3, 3)):
            p = load_plane(r, b, own_ref)
            for a in range(4):
                for c in range(4):
                    x = p[a][c]
                    if b == 2:
                        x = x * 0.5
                    if b == 3:
                        first = rhs[r, st(1, a, c)]
                        rhs[r, st(3, a, c)] = (first - x) * float(0.5 / KAPPA)
                        rhs[r, st(1, a, c)] = (first + x) * 0.5
                    else:
                        rhs[r, st(at, a, c)] = x

    halo_copy.wait()
    build_rhs(0, load_ref)

    block = lax.rem(lane + jnp.where(ex == 0, 0, HALO - 1), width) // HALO

    def swap(x):
        return pltpu.roll(x, layers, 0)

    def pack(s, x):
        for p in range(8):
            packed[s, p] = jnp.where(lower, x[2 * p], swap(x[2 * p + 1]))
        for p in range(8 // fold):
            halves = []
            for h in range(2):
                group = x[(2 * p + h) * fold:(2 * p + h + 1) * fold]
                mixed = group[0]
                for j in range(1, fold):
                    mixed = jnp.where(block == j, pltpu.roll(group[j], HALO * j, 1), mixed)
                halves.append(mixed)
            packed[s, 8 + p] = jnp.where(lower, swap(halves[0]), halves[1])

    def unpack(kind, s):
        x = []
        for p in range(8 // fold):
            tile = got[kind, s, 8 + p]
            for half in (swap(tile), tile):
                for j in range(fold):
                    other = half if j == 0 else pltpu.roll(half, width - HALO * j, 1)
                    n = len(x)
                    mine = got[kind, s, n // 2]
                    mine = mine if n % 2 == 0 else swap(mine)
                    x.append(jnp.where(lower, mine, jnp.where(block == 0, other, 0.0)))
        return x

    def near_copy(s):
        return remote(packed.at[s], got.at[0, s], f_send.at[0, s], f_recv.at[0, s], place(1))

    def far_copy(s):
        return remote(packed.at[s], got.at[1, s], f_send.at[1, s], f_recv.at[1, s], place(2))

    def send_face(s, values):
        pack(s, values)
        near_copy(s).start()

        @pl.when(there(2) & (s < STEPS - 1))
        def _():
            far_copy(s).start()

    def add_near(s):
        near_copy(s).wait()
        for n, x in enumerate(unpack(0, s)):
            tot[0, 64 + n] = tot[0, 64 + n] + x

    def add_far(s):
        @pl.when(there(-2))
        def _():
            far_copy(s).wait_recv()
            for n, x in enumerate(unpack(1, s)):
                tot[1, n] = tot[1, n] + x

    def expand(r, planes):
        for b in planes:
            w = []
            for a in range(4):
                v = [sol[r, st(b, a, c)] for c in range(4)]
                up = after(v[0])
                w.append([v[0] + up, v[1], v[2], v[3], v[0] - up])
            for k in range(N):
                up = above(w[0][k])
                xs[r, xi(b, 0, k)] = w[0][k] + up
                xs[r, xi(b, 4, k)] = w[0][k] - up
                for a in range(1, 4):
                    xs[r, xi(b, a, k)] = w[a][k]

    def cross(r):
        for i in range(N):
            for k in range(N):
                v = [xs[r, xi(b, i, k)] for b in range(N)]
                r0, r1, rz, s1, s0 = line_apply(v[0] + v[4], v[1], v[2], v[3], v[0] - v[4], MU[i] * MU[k])
                for b, x in enumerate((r0 + s0, r1, rz, s1, r0 - s0)):
                    bs[r, xi(b, i, k)] = x

    def gather(y):
        g = []
        for k in range(N):
            low, high = plus(y[0][k], y[4][k]), minus(y[0][k], y[4][k])
            g.append([None if low is None else below(low, high)] + [y[i][k] for i in range(1, 4)])
        h = []
        for a in range(4):
            low, high = plus(g[0][a], g[4][a]), minus(g[0][a], g[4][a])
            h.append([None if low is None else low + before(high)] + [g[k][a] for k in range(1, 4)])
        return h

    def plane(r, b):
        coeff = coeffs[OWN - r]
        x = [[xs[r, xi(b, i, k)] for k in range(N)] for i in range(N)]
        along_c = [line_apply(*x[i], MUB[b] * MU[i]) for i in range(N)]
        along_a = [line_apply(*[x[i][k] for i in range(N)], MUB[b] * MU[k]) for k in range(N)]
        y = []
        for i in range(N):
            line = []
            for k in range(N):
                terms = sorted(((b == 2, bs[r, xi(b, i, k)]), (k == 2, along_c[i][k]), (i == 2, along_a[k][i])),
                               key=lambda t: t[0])
                total = -terms[0][1] if terms[0][0] else terms[0][1]
                for negative, term in terms[1:]:
                    total = total - term if negative else total + term
                line.append(coeff * total)
            y.append(line)
        h = gather(y)
        return [rhs[r, st(b, a, c)] - h[a][c] for a in range(4) for c in range(4)]

    def put(r, b, values):
        for n, x in enumerate(values):
            tot[r, b * 16 + n] = x

    def update(r, b):
        for n in range(b * 16, b * 16 + 16):
            sol[r, n] = sol[r, n] + sinv[r, n] * tot[r, n]

    def inverted(x):
        return jnp.where(x > 0.0, 1.0 / jnp.where(x > 0.0, x, 1.0), 0.0)

    def invert():
        for r in range(2):
            here = coeffs[OWN - r]
            for bl, x in (((1, 2, 3), here), ((0,), here + coeffs[OWN - r - 1]), ((4,), here + coeffs[OWN - r + 1])):
                xc = x + before(x)
                tiles = [[inverted(below(xc, xc)), inverted(below(x, x))], [inverted(xc), inverted(x)]]
                for b in bl:
                    for a in range(4):
                        for c in range(4):
                            factor = FINE_RELAX * NU[a] * NU[b] * NU[c] / K3[NODE[a], NODE[b], NODE[c]]
                            sinv[r, st(b, a, c)] = float(factor) * tiles[min(a, 1)][min(c, 1)]
        corner = 3.0 * SC[0, 0] * WC[0, 0] ** 2
        for i in range(SPAN - 1):
            pair = coeffs[i] + coeffs[i + 1]
            pair = pair + before(pair)
            cinv[i] = float(COARSE_RELAX / corner) * inverted(below(pair, pair))

    def halves(v):
        even, odd = v[1] + v[2], float(SLOPE) * v[3]
        return even + odd, even - odd

    def restrict_load():
        q = [[], []]
        for n in range(16):
            v = [rhs[0, b * 16 + n] for b in range(N)]
            low, high = halves(v)
            q[0].append(v[0] + low)
            q[1].append(v[4] + high)
        for j in range(2):
            lines = []
            for a in range(4):
                v = q[j][a * 4:a * 4 + 4]
                low, high = halves(v)
                lines.append((v[0] + low) + before(high))
            low, high = halves(lines)
            coarse_load[j] = below(lines[0] + low, high)

    def moments(first, mids, second):
        even, odd = first + second, first - second
        return (
            float(RISE) * odd,
            float(W0 / 2) * even + float(W1 / 2) * mids[0] + float(W2 / 4) * mids[1],
            float(W0 / 2) * odd + float(W1 * SLOPE / (2 * KAPPA ** 2)) * mids[2],
        )

    def coarse_send(cycle):
        along_b = []
        for n in range(16):
            v = [sol[0, b * 16 + n] for b in range(N)]
            along_b.append(moments(v[0], v[1:4], v[4]))
        mixed = [[], [], [], []]
        plain = [[], [], [], []]
        for c in range(4):
            along_a = []
            for kind in range(3):
                v = [along_b[a * 4 + c][kind] for a in range(4)]
                along_a.append(moments(v[0], v[1:4], above(v[0])))
            rise, even, odd = along_a
            mixed[1].append(rise[1])
            mixed[2].append(even[0])
            mixed[3].append(rise[2] + odd[0])
            for m, x in enumerate((even[1], odd[1], even[2], odd[2])):
                plain[m].append(x)
        coeff = coeffs[OWN]
        y = [None] * 4
        for m in range(4):
            steep = float(RISE) * (plain[m][0] - after(plain[m][0]))
            if m == 0:
                y[m] = (None, coeff * steep)
            else:
                v = mixed[m]
                part = moments(v[0], v[1:4], after(v[0]))
                y[m] = (coeff * part[1], coeff * (part[2] + steep))
        for j in range(2):
            g = []
            for k in range(2):
                r = []
                for a in range(2):
                    one, two = y[2 * a][k], y[2 * a + 1][k]
                    r.append(plus(one, two) if j == 0 else minus(one, two))
                g.append(below(r[0] + r[1], r[0] - r[1]))
            cgot[cycle, OWN, j] = coarse_load[j] - ((g[0] + g[1]) + before(g[0] - g[1]))
        for d in SENDS:
            when_there(d, lambda d: remote(
                cgot.at[cycle, OWN], cgot.at[cycle, slot_at(d)], c_send.at[REACH + d], c_recv.at[cycle, slot_at(d)],
                place(d)).start())

    def correct(cycle):
        for d in SENDS:
            when_there(d, lambda d: remote(
                cgot.at[cycle, OWN], cgot.at[cycle, OWN], c_send.at[REACH + d], c_recv.at[cycle, OWN],
                place(d)).wait_send())
        for d in RECVS:
            when_there(d, lambda d: remote(
                cgot.at[cycle, OWN], cgot.at[cycle, REACH + d], c_send.at[OWN], c_recv.at[cycle, REACH + d],
                place(d)).wait_recv())

        def q(e, j):
            return cgot[cycle, e, j if (e - OWN) % 2 == 0 else 1 - j]

        lines = SPAN - 1
        rc = [q(i, 1) + q(i + 1, 0) for i in range(lines)]
        x = [cinv[i] * rc[i] for i in range(lines)]

        def modes(v):
            up = after(v)
            parts = []
            for k in (v + up, v - up):
                high = above(k)
                parts.append((k + high, k - high))
            return [[parts[k][i] for k in range(2)] for i in range(2)]

        first, last = 0, lines - 1
        for sweep in range(NC - 1):
            m = {i: modes(x[i]) for i in range(first, last + 1)}
            sides = {}
            for e in range(first + 1, last + 1):
                coeff = coeffs[e]
                factor = [float(C1) * coeff, float(C2) * coeff, float(C3) * coeff]
                low, high = m[e - 1], m[e]
                part = []
                for i in range(2):
                    pair = []
                    for k in range(2):
                        odd = factor[i + k] * (low[i][k] - high[i][k])
                        if i + k == 0:
                            pair.append((odd, -odd))
                        else:
                            even = factor[i + k - 1] * (low[i][k] + high[i][k])
                            pair.append((even + odd, even - odd))
                    part.append(pair)
                sides[e] = part
            first, last = first + 1, last - 1
            new = list(x)
            for i in range(first, last + 1):
                y = [[sides[i + 1][a][k][0] + sides[i][a][k][1] for k in range(2)] for a in range(2)]
                g = [below(y[0][k] + y[1][k], y[0][k] - y[1][k]) for k in range(2)]
                image = (g[0] + g[1]) + before(g[0] - g[1])
                new[i] = x[i] + cinv[i] * (rc[i] - image)
            x = new

        base = OWN - 3
        m = {i: modes(x[i]) for i in range(base, base + 5)}
        kind = [0, 0, 0, 1, 1]
        grow = [1.0, 1.0, 1.0, SLOPE, 1.0]

        def ends(centre, weight, tilt):
            y = [[None] * N for _ in range(N)]
            for i in range(N):
                for k in range(N):
                    value = None
                    if centre is not None:
                        value = float(MU[i] * MU[k] * grow[i] * grow[k]) * centre[kind[i]][kind[k]]
                    if i == 4:
                        value = plus(value, float(RISE * weight * MU[k] * grow[k]) * tilt[1][kind[k]])
                    if k == 4:
                        value = plus(value, float(RISE * weight * MU[i] * grow[i]) * tilt[kind[i]][1])
                    y[i][k] = value
            return gather(y)

        def face_image(i):
            up, down = coeffs[i + 1], coeffs[i]
            both = up + down
            centre = [[float(RISE) * (up * (m[i][a][k] - m[i + 1][a][k]) - down * (m[i - 1][a][k] - m[i][a][k]))
                       for k in range(2)] for a in range(2)]
            tilt = [[None if a + k == 0 else both * m[i][a][k] for k in range(2)] for a in range(2)]
            h = ends(centre, W0, tilt)
            return [h[a][c] for a in range(4) for c in range(4)]

        for i, targets in ((OWN - 2, ((1, 0),)), (OWN - 1, ((1, 64), (0, 0))), (OWN, ((0, 64),))):
            values = face_image(i)
            for r, at in targets:
                for n, value in enumerate(values):
                    tot[r, at + n] = tot[r, at + n] - value
        scale = [1.0, 1.0, 1.0, SLOPE]

        def nodal(i):
            v = x[i]
            up = after(v)
            high = above(v)
            tiles = [[v, v + up, v - up], [v + high, m[i][0][0], m[i][0][1]], [v - high, m[i][1][0], m[i][1][1]]]
            pick = [0, 1, 1, 2]
            made = {}
            out = []
            for a in range(4):
                for c in range(4):
                    key = (pick[a], pick[c])
                    if key not in made:
                        factor = float(scale[a] * scale[c])
                        made[key] = tiles[key[0]][key[1]] if factor == 1.0 else factor * tiles[key[0]][key[1]]
                    out.append((key, made[key]))
            return out

        at_line = {i: nodal(i) for i in (OWN - 2, OWN - 1, OWN)}
        for r in range(2):
            low, high = OWN - 1 - r, OWN - r
            coeff = coeffs[OWN - r]
            for kindb in range(2):
                diff = [[None if a + k == 0 else
                         coeff * (m[low][a][k] - m[high][a][k] if kindb else m[low][a][k] + m[high][a][k])
                         for k in range(2)] for a in range(2)]
                h = ends(None, 1.0, diff)
                for b in ((3,) if kindb else (1, 2)):
                    factor = float(MUB[b] * (SLOPE if kindb else 1.0))
                    for a in range(4):
                        for c in range(4):
                            if h[a][c] is not None:
                                tot[r, st(b, a, c)] = tot[r, st(b, a, c)] - factor * h[a][c]
                made = {}
                for n in range(16):
                    key, lower_value = at_line[low][n]
                    upper_value = at_line[high][n][1]
                    if key not in made:
                        made[key] = (float(SLOPE) * (lower_value - upper_value) if kindb
                                     else lower_value + upper_value)
                    for b in ((3,) if kindb else (1, 2)):
                        sol[r, b * 16 + n] = sol[r, b * 16 + n] + made[key]
            for n in range(16):
                sol[r, n] = sol[r, n] + at_line[low][n][1]
                sol[r, 64 + n] = sol[r, 64 + n] + at_line[high][n][1]

    def emit(field, out_ref, dual):
        def split(mid, double, odd):
            if dual:
                odd = float(KAPPA) * odd
                return mid + odd, 2.0 * double, mid - odd
            even, odd = 0.5 * mid, float(0.5 / KAPPA) * odd
            return even + odd, 0.5 * double, even - odd

        def one(b, values):
            lines = []
            for a in range(4):
                v = values[a * 4:a * 4 + 4]
                lines.append([v[0], *split(*v[1:]), after(v[0])])
            for c in range(N):
                v = [lines[a][c] for a in range(4)]
                for a, tile in enumerate([v[0], *split(*v[1:]), above(v[0])]):
                    out_ref[raw(a, b, c)] = tile[0:layers]

        for b in (0, 4):
            one(b, [field[0, b * 16 + n] for n in range(16)])
        mids = [split(field[0, 16 + n], field[0, 32 + n], field[0, 48 + n]) for n in range(16)]
        for b in range(1, 4):
            one(b, [v[b - 1] for v in mids])

    for b in range(N):
        put(0, b, [rhs[0, b * 16 + n] for n in range(16)])
    send_face(0, [tot[0, 64 + n] for n in range(16)])
    sol[...] = jnp.zeros_like(sol)
    for d in SENDS:
        when_there(d, lambda d: remote(
            coeffs.at[OWN], coeffs.at[OWN], k_send.at[REACH + d], k_recv.at[OWN], place(d)).wait_send())
    for d in RECVS:
        when_there(d, lambda d: remote(
            coeffs.at[OWN], coeffs.at[REACH + d], k_send.at[OWN], k_recv.at[REACH + d], place(d)).wait_recv())
    invert()
    restrict_load()
    when_there(-1, lambda d: load_copy().wait())
    when_there(-1, lambda d: corner_copy().wait())
    build_rhs(1, ghost_load)
    for b in range(N):
        put(1, b, [rhs[1, b * 16 + n] for n in range(16)])
    for n in range(16):
        joined = tot[0, n] + tot[1, 64 + n]
        tot[0, n] = joined
        tot[1, 64 + n] = joined
    for b in range(4):
        update(0, b)
        update(1, b + 1)
    add_near(0)
    update(0, 4)

    def step(s, _):
        cycle = s // PERIOD
        live = s < STEPS - 1
        coarse = (lax.rem(s, PERIOD) == NPRE) & live
        deferred = lax.rem(s - 1, PERIOD) != NPRE

        behind = deferred & (s > 1)

        @pl.when(coarse)
        def _():
            coarse_send(cycle)

        expand(0, range(N))
        cross(0)
        mine = plane(0, 4)
        put(0, 4, mine)
        send_face(s, mine)

        @pl.when(there(2))
        def _():
            far_copy(s - 1).wait_send()

        @pl.when(behind)
        def _():
            for b in range(4):
                put(1, b, plane(1, b))
                if b:
                    update(1, b)
            update(1, 4)

        for b in range(4):
            put(0, b, plane(0, b))
        expand(1, range(1, N))

        @pl.when(deferred)
        def _():
            add_far(s - 1)
            update(1, 0)

        expand(1, (0,))
        cross(1)
        for n, x in enumerate(plane(1, 4)):
            joined = tot[0, n] + x
            tot[0, n] = joined
            tot[1, 64 + n] = joined

        @pl.when(coarse)
        def _():
            for b in range(4):
                put(1, b, plane(1, b))

        @pl.when(jnp.logical_not(live))
        def _():
            emit(sol, sol_out, False)

        @pl.when(jnp.logical_not(coarse))
        def _():
            for b in range(4):
                update(0, b)

        add_near(s)

        @pl.when(coarse)
        def _():
            add_far(s)
            correct(cycle)
            for b in range(4):
                update(0, b)
                update(1, b + 1)
            update(1, 0)

        update(0, 4)
        return 0

    lax.fori_loop(1, STEPS, step, 0)
    emit(tot, res_out, True)


def per_device(sizes, load, kappa, wet):
    layers, _, width = kappa.shape
    nodes = N * N * N
    tile = (2 * layers, width)
    half = (layers, width)
    sizes = sizes + (layers, width)
    out = jax.ShapeDtypeStruct((nodes, layers, width), F32)
    vmem = pl.BlockSpec(memory_space=pltpu.VMEM)
    fold = width // HALO
    groups = -(-N * N // fold)
    messages = 8 + 8 // fold
    dma = pltpu.SemaphoreType.DMA
    solution, residual = pl.pallas_call(
        functools.partial(kernel, sizes),
        out_shape=(out, out),
        in_specs=[vmem] * 3,
        out_specs=(vmem, vmem),
        scratch_shapes=[
            pltpu.VMEM((nodes,) + half, F32),
            pltpu.VMEM((N * groups,) + half, F32),
            pltpu.VMEM((2, N * groups) + half, F32),
            pltpu.VMEM(half, F32),
            pltpu.VMEM(half, F32),
            pltpu.VMEM((SPAN,) + tile, F32),
            pltpu.VMEM((2, 80) + tile, F32),
            pltpu.VMEM((2, 80) + tile, F32),
            pltpu.VMEM((2, 80) + tile, F32),
            pltpu.VMEM((2, 80) + tile, F32),
            pltpu.VMEM((2, nodes) + tile, F32),
            pltpu.VMEM((2, nodes) + tile, F32),
            pltpu.VMEM((2,) + tile, F32),
            pltpu.VMEM((STEPS, messages) + tile, F32),
            pltpu.VMEM((2, STEPS, messages) + tile, F32),
            pltpu.VMEM((CYCLES, SPAN, 2) + tile, F32),
            pltpu.VMEM((SPAN - 1,) + tile, F32),
            dma((4,)), dma((4,)), dma((SPAN + 1,)), dma((SPAN + 1,)),
            dma((2, STEPS)), dma((2, STEPS)), dma((SPAN + 1,)), dma((CYCLES, SPAN + 1)),
        ],
        compiler_params=pltpu.CompilerParams(collective_id=0, has_side_effects=True, vmem_limit_bytes=16 * 2 ** 20),
    )(load.reshape(nodes, layers, width), kappa.reshape(layers, width), wet.reshape(layers, width))
    return solution.reshape(load.shape), residual.reshape(load.shape)


def solution(mesh):
    sizes = tuple(mesh.shape[name] for name in ("ex", "ey", "lin"))
    field = P(None, None, None, None, ("ey", "lin"), "ex")
    cell = P(None, ("ey", "lin"), "ex")
    return jax.shard_map(
        functools.partial(per_device, sizes), mesh=mesh, in_specs=(field, cell, cell),
        out_specs=(field, field), check_vma=False,
    )
```

```python
import functools
import math

import jax
import jax.numpy as jnp
import numpy as np
from jax import lax
from jax.experimental import pallas as pl
from jax.experimental.pallas import tpu as pltpu
from jax.sharding import PartitionSpec as P

N = 5
CYCLES = 2
NPRE = 2
NPOST = 2
NC = 4
PERIOD = NPRE + NPOST
FINE_RELAX = 0.25
COARSE_RELAX = 0.4
STEPS = CYCLES * PERIOD + 1
REACH = NC + 2
SPAN = 2 * REACH
OWN = REACH
HALO = 32
MESH = pl.DeviceIdType.MESH
F32 = jnp.float32


def node_tables():
    points = np.array([-1.0, -math.sqrt(3.0 / 7.0), 0.0, math.sqrt(3.0 / 7.0), 1.0])
    weights = np.array([0.1, 49.0 / 90.0, 32.0 / 45.0, 49.0 / 90.0, 0.1])
    eye_table = np.eye(points.shape[0])
    spread = points[:, None] - points[None, :] + eye_table
    factors = np.prod(spread, axis=1)
    deriv = factors[:, None] / (factors[None, :] * spread)
    deriv = np.where(eye_table > 0, (np.sum(1.0 / spread, axis=1) - 1.0)[:, None], deriv)
    stiff = deriv.T @ (weights[:, None] * deriv)
    mass = eye_table * weights[:, None]
    interp = np.stack([(1.0 - points) / 2.0, (1.0 + points) / 2.0], axis=1)
    return stiff, weights, interp, interp.T @ stiff @ interp, interp.T @ mass @ interp


S, WEIGHTS, INTERP, SC, WC = node_tables()
ALPHA = (S[0, 0] + S[0, 4]) / 2
BETA = (S[0, 1] + S[0, 3]) / 2
GAMMA = (S[1, 1] + S[1, 3]) / 2
KAPPA = (S[0, 1] - S[0, 3]) / (S[0, 0] - S[0, 4])
ODD = (S[0, 0] - S[0, 4]) / 2
DELTA = (S[1, 1] - S[1, 3]) / (2 * KAPPA ** 2) - ODD
W0, W1, W2 = WEIGHTS[:3]
MU = [W0 / 2, W1 / 2, W2 / 4, W1 / (2 * KAPPA ** 2), W0 / 2]
MUB = [W0, W1 / 2, W2 / 4, W1 / (2 * KAPPA ** 2), W0]
NU = [1.0, 2.0, 4.0, 2 * KAPPA ** 2, 1.0]
SLOPE = KAPPA * (INTERP[1, 0] - INTERP[3, 0])
RISE = ODD * (1 + SLOPE)
NODE = [0, 1, 2, 1, 4]
DIAG = np.diag(S) / WEIGHTS
W3 = WEIGHTS[:, None, None] * WEIGHTS[None, :, None] * WEIGHTS[None, None, :]
K3 = W3 * (DIAG[:, None, None] + DIAG[None, :, None] + DIAG[None, None, :])
CS = (SC[0, 0] - SC[0, 1]) / 2
CE, CO = (WC[0, 0] + WC[0, 1]) / 2, (WC[0, 0] - WC[0, 1]) / 2
C1, C2, C3 = CS * CE * CE, 2 * CS * CO * CE, 3 * CS * CO * CO
SENDS = [d for d in range(-REACH + 1, REACH + 1) if d != 0]
RECVS = [d for d in range(-REACH, REACH) if d != 0]
NEAR_SENDS = [-1, 1, 2]
NEAR_RECVS = [-1, 1, -2]


def st(b, a, c):
    return (b * 4 + a) * 4 + c


def xi(b, i, k):
    return (b * N + i) * N + k


def line_apply(e0, e1, z, o1, o0, scale):
    q0, q1 = e0 - z, e1 - z
    r0 = float(ALPHA * scale) * q0 + float(BETA * scale) * q1
    r1 = float(BETA * scale) * q0 + float(GAMMA * scale) * q1
    s0 = float(ODD * scale) * (o0 + o1)
    return r0, r1, r0 + r1, s0 + float(DELTA * scale) * o1, s0


def plus(x, y):
    if x is None or y is None:
        return x if y is None else y
    return x + y


def minus(x, y):
    if y is None:
        return x
    return -y if x is None else x - y


def kernel(
    sizes, load_ref, kappa_ref, wet_ref, sol_out, res_out,
    load, part, got_part, got_halo, halves_of, coeffs,
    rhs, sol, tot, sinv, xs, bs, coarse_load, packed, got, cgot, cinv,
    load_sem, x_send, x_recv, k_send, k_recv, f_send, f_recv, c_send, c_recv,
):
    ex_count, ey_count, lin_count, layers, width = sizes
    ex, ey, lin = lax.axis_index("ex"), lax.axis_index("ey"), lax.axis_index("lin")
    rows = ey_count * lin_count
    row = ey * lin_count + lin
    par = lax.rem(lin, 2)
    sgn = 1 - 2 * par
    fold = width // HALO
    groups = 80 // fold

    sub = lax.broadcasted_iota(jnp.int32, (2 * layers, width), 0)
    lane = lax.broadcasted_iota(jnp.int32, (2 * layers, width), 1)
    layer = sub % layers
    bottom, top = layer == 0, layer == layers - 1
    first_lane, last_lane = lane == 0, lane == width - 1
    near = jnp.where(ex == 0, lane, width - 1 - lane)
    real = (sub < layers) | (near < HALO)
    lower = sub < layers

    def before(x):
        y = pltpu.roll(x, 1, 1)
        return jnp.where(first_lane, pltpu.roll(y, layers, 0), y)

    def after(x):
        y = pltpu.roll(x, width - 1, 1)
        return jnp.where(last_lane, pltpu.roll(y, layers, 0), y)

    def below(low, high):
        return jnp.where(bottom, low, low + pltpu.roll(high, 1, 0))

    def above(low):
        return jnp.where(top, 0.0, pltpu.roll(low, 2 * layers - 1, 0))

    def there(d):
        at = row + sgn * d
        return (at >= 0) & (at < rows)

    def place(d, other=False):
        at = row + sgn * d
        return (1 - ex if other else ex, at // lin_count, at % lin_count)

    def when_there(d, fn):
        @pl.when(there(d))
        def _():
            fn(d)

    def slot_at(d):
        return REACH + (-d if d % 2 == 0 else d)

    def remote(src, dst, send, recv, device):
        return pltpu.make_async_remote_copy(
            src_ref=src, dst_ref=dst, send_sem=send, recv_sem=recv, device_id=device, device_id_type=MESH)

    fetch = pltpu.make_async_copy(load_ref, load, load_sem)
    fetch.start()
    halves_of[...] = jnp.zeros_like(halves_of)
    cgot[...] = jnp.zeros_like(cgot)

    @pl.when(jnp.logical_not(there(-1)))
    def _():
        got_part[...] = jnp.zeros_like(got_part)
        got_halo[1] = jnp.zeros_like(got_halo[1])

    def greet(device):
        pl.semaphore_signal(pltpu.get_barrier_semaphore(), inc=1, device_id=device, device_id_type=MESH)

    greet((1 - ex, ey, lin))
    expected = jnp.int32(1)
    for d in range(1, REACH + 1):
        for e in (-d, d):
            @pl.when(there(e))
            def _():
                greet(place(e))
                if d <= 2:
                    greet(place(e, True))
            expected = expected + jnp.where(there(e), 2 if d <= 2 else 1, 0)

    halves_of[0, OWN] = kappa_ref[...] * jnp.where(wet_ref[...] == 1, F32(1.0), F32(0.05))

    def raw(a, b, c):
        return (a * N + b + par * (N - 1 - 2 * b)) * N + c

    def to_dual(f):
        return [(f[1] + f[3]) * 0.5, f[2] * 0.5, (f[1] - f[3]) * float(0.5 / KAPPA)]

    def load_plane(b):
        nothing = jnp.zeros((layers, width), F32)
        tiles = [jnp.concatenate([load[raw(n // N, b, n % N)], nothing], axis=0) for n in range(N * N)]
        lines = []
        for a in range(N):
            f = tiles[a * N:a * N + N]
            lines.append([f[0] + before(f[4])] + to_dual(f))
        columns = []
        for c in range(4):
            f = [lines[a][c] for a in range(N)]
            columns.append([below(f[0], f[4])] + to_dual(f))
        return [columns[c][a] for a in range(4) for c in range(4)]

    fetch.wait()
    for b in (0, 4, 2, 1, 3):
        for n, x in enumerate(load_plane(b)):
            if b == 3:
                first = rhs[0, 16 + n]
                rhs[0, 48 + n] = (first - x) * float(0.5 / KAPPA)
                rhs[0, 16 + n] = (first + x) * 0.5
            else:
                rhs[0, b * 16 + n] = x * 0.5 if b == 2 else x
    source = jnp.where(ex == 0, fold - 1, 0)
    turn = (lane // HALO + fold - source) % fold
    for g in range(groups):
        mixed = None
        for j in range(fold):
            x = rhs[0, g * fold + j]
            part[groups + 1 + g * fold + j] = x[0:layers]
            mixed = x if j == 0 else jnp.where(turn == j, pltpu.roll(x, HALO * j, 1), mixed)
        part[g] = mixed[0:layers]
    mixed = None
    for j in range(20):
        x = rhs[0, 4 * j]
        mixed = x if j == 0 else jnp.where(lane == j, pltpu.roll(x, j, 1), mixed)
    part[groups] = pltpu.roll(mixed, layers, 0)[0:layers]

    pl.semaphore_wait(pltpu.get_barrier_semaphore(), expected)

    def half_copy(h, d, slot, device, source=0):
        return remote(halves_of.at[source, OWN], halves_of.at[h, slot], k_send.at[h, REACH + d], k_recv.at[h, slot],
                      device)

    def half_sent(h, d):
        half_copy(h, d, OWN, place(d), h).wait_send()

    def half_came(h, d):
        half_copy(h, d, REACH + d, place(d), h).wait_recv()

    half_copy(1, 0, OWN, place(0, True)).start()
    for d in NEAR_SENDS:
        @pl.when(there(d))
        def _():
            half_copy(0, d, slot_at(d), place(d)).start()
            half_copy(1, d, slot_at(d), place(d, True)).start()

    def halo_copy(kind, device):
        return remote(part.at[0:groups + 1], got_halo.at[kind], x_send.at[kind], x_recv.at[kind], device)

    def part_copy(k):
        at, size = ((0, 17), (17, 64))[k]
        return remote(part.at[groups + at:groups + at + size], got_part.at[at:at + size], x_send.at[2 + k],
                      x_recv.at[2 + k], place(-1))

    halo_copy(0, place(0, True)).start()

    @pl.when(there(-1))
    def _():
        part_copy(0).start()
        halo_copy(1, place(-1, True)).start()
        part_copy(1).start()

    for d in SENDS:
        if d not in NEAR_SENDS:
            when_there(d, lambda d: half_copy(0, d, slot_at(d), place(d)).start())

    outer = (sub >= layers) & (near < HALO)
    entering = first_lane & ((sub >= layers) | (ex == 1))

    def assemble(r, b):
        source_b = b if r == 0 or 0 < b < 4 else 4 - b
        nothing = jnp.zeros((layers, width), F32)
        spill = jnp.concatenate([got_halo[r, groups], got_part[0] if r else nothing], axis=0)
        for a in range(4):
            for c in range(4):
                n, m = st(b, a, c), st(source_b, a, c)
                h = got_halo[r, m // fold]
                h = jnp.concatenate([h, h], axis=0)
                if m % fold:
                    h = pltpu.roll(h, width - HALO * (m % fold), 1)
                h = jnp.where(outer, h, 0.0)
                if r == 0:
                    x = rhs[0, n] + h
                else:
                    p = got_part[1 + m]
                    x = jnp.where(lower, jnp.concatenate([p, p], axis=0), h)
                if c == 0:
                    j = m // 4
                    x = x + jnp.where(entering, pltpu.roll(spill, width - j, 1) if j else spill, 0.0)
                rhs[r, n] = -x if r == 1 and b == 3 else x

    block = lax.rem(lane + jnp.where(ex == 0, 0, HALO - 1), width) // HALO

    def swap(x):
        return pltpu.roll(x, layers, 0)

    def pack(s, x):
        for p in range(8):
            packed[s, p] = jnp.where(lower, x[2 * p], swap(x[2 * p + 1]))
        for p in range(8 // fold):
            halves = []
            for h in range(2):
                group = x[(2 * p + h) * fold:(2 * p + h + 1) * fold]
                mixed = group[0]
                for j in range(1, fold):
                    mixed = jnp.where(block == j, pltpu.roll(group[j], HALO * j, 1), mixed)
                halves.append(mixed)
            packed[s, 8 + p] = jnp.where(lower, swap(halves[0]), halves[1])

    def unpack(kind, s):
        x = []
        for p in range(8 // fold):
            tile = got[kind, s, 8 + p]
            for half in (swap(tile), tile):
                for j in range(fold):
                    other = half if j == 0 else pltpu.roll(half, width - HALO * j, 1)
                    n = len(x)
                    mine = got[kind, s, n // 2]
                    mine = mine if n % 2 == 0 else swap(mine)
                    x.append(jnp.where(lower, mine, jnp.where(block == 0, other, 0.0)))
        return x

    def near_copy(s):
        return remote(packed.at[s], got.at[0, s], f_send.at[0, s], f_recv.at[0, s], place(1))

    def far_copy(s):
        return remote(packed.at[s], got.at[1, s], f_send.at[1, s], f_recv.at[1, s], place(2))

    def send_face(s, values):
        pack(s, values)
        near_copy(s).start()

        @pl.when(there(2) & (s < STEPS - 1))
        def _():
            far_copy(s).start()

    def add_near(s):
        near_copy(s).wait()
        for n, x in enumerate(unpack(0, s)):
            tot[0, 64 + n] = tot[0, 64 + n] + x

    def add_far(s):
        @pl.when(there(-2))
        def _():
            far_copy(s).wait_recv()
            for n, x in enumerate(unpack(1, s)):
                tot[1, n] = tot[1, n] + x

    def expand(r, planes):
        for b in planes:
            w = []
            for a in range(4):
                v = [sol[r, st(b, a, c)] for c in range(4)]
                up = after(v[0])
                w.append([v[0] + up, v[1], v[2], v[3], v[0] - up])
            for k in range(N):
                up = above(w[0][k])
                xs[r, xi(b, 0, k)] = w[0][k] + up
                xs[r, xi(b, 4, k)] = w[0][k] - up
                for a in range(1, 4):
                    xs[r, xi(b, a, k)] = w[a][k]

    def cross(r):
        for i in range(N):
            for k in range(N):
                v = [xs[r, xi(b, i, k)] for b in range(N)]
                r0, r1, rz, s1, s0 = line_apply(v[0] + v[4], v[1], v[2], v[3], v[0] - v[4], MU[i] * MU[k])
                for b, x in enumerate((r0 + s0, r1, rz, s1, r0 - s0)):
                    bs[r, xi(b, i, k)] = x

    def gather(y):
        g = []
        for k in range(N):
            low, high = plus(y[0][k], y[4][k]), minus(y[0][k], y[4][k])
            g.append([None if low is None else below(low, high)] + [y[i][k] for i in range(1, 4)])
        h = []
        for a in range(4):
            low, high = plus(g[0][a], g[4][a]), minus(g[0][a], g[4][a])
            h.append([None if low is None else low + before(high)] + [g[k][a] for k in range(1, 4)])
        return h

    def plane(r, b):
        coeff = coeffs[OWN - r]
        x = [[xs[r, xi(b, i, k)] for k in range(N)] for i in range(N)]
        along_c = [line_apply(*x[i], MUB[b] * MU[i]) for i in range(N)]
        along_a = [line_apply(*[x[i][k] for i in range(N)], MUB[b] * MU[k]) for k in range(N)]
        y = []
        for i in range(N):
            line = []
            for k in range(N):
                terms = sorted(((b == 2, bs[r, xi(b, i, k)]), (k == 2, along_c[i][k]), (i == 2, along_a[k][i])),
                               key=lambda t: t[0])
                total = -terms[0][1] if terms[0][0] else terms[0][1]
                for negative, term in terms[1:]:
                    total = total - term if negative else total + term
                line.append(coeff * total)
            y.append(line)
        h = gather(y)
        return [rhs[r, st(b, a, c)] - h[a][c] for a in range(4) for c in range(4)]

    def put(r, b, values):
        for n, x in enumerate(values):
            tot[r, b * 16 + n] = x

    def update(r, b):
        for n in range(b * 16, b * 16 + 16):
            sol[r, n] = sol[r, n] + sinv[r, n] * tot[r, n]

    def inverted(x):
        return jnp.where(x > 0.0, 1.0 / jnp.where(x > 0.0, x, 1.0), 0.0)

    def invert():
        for r in range(2):
            here = coeffs[OWN - r]
            for bl, x in (((1, 2, 3), here), ((0,), here + coeffs[OWN - r - 1]), ((4,), here + coeffs[OWN - r + 1])):
                xc = x + before(x)
                tiles = [[inverted(below(xc, xc)), inverted(below(x, x))], [inverted(xc), inverted(x)]]
                for b in bl:
                    for a in range(4):
                        for c in range(4):
                            factor = FINE_RELAX * NU[a] * NU[b] * NU[c] / K3[NODE[a], NODE[b], NODE[c]]
                            sinv[r, st(b, a, c)] = float(factor) * tiles[min(a, 1)][min(c, 1)]

    def join_coeff(e):
        coeffs[e] = jnp.where(real, jnp.concatenate([halves_of[0, e], halves_of[1, e]], axis=0), 0.0)

    def coarse_invert():
        for d in SENDS:
            @pl.when(there(d))
            def _():
                half_sent(0, d)
                half_sent(1, d)
        for d in RECVS:
            if d not in NEAR_RECVS:
                @pl.when(there(d))
                def _():
                    half_came(0, d)
                    half_came(1, d)
        for e in range(SPAN):
            if abs(e - OWN + 0.5) > 2:
                join_coeff(e)
        corner = 3.0 * SC[0, 0] * WC[0, 0] ** 2
        for i in range(SPAN - 1):
            pair = coeffs[i] + coeffs[i + 1]
            pair = pair + before(pair)
            cinv[i] = float(COARSE_RELAX / corner) * inverted(below(pair, pair))

    def halves(v):
        even, odd = v[1] + v[2], float(SLOPE) * v[3]
        return even + odd, even - odd

    def restrict_load():
        q = [[], []]
        for n in range(16):
            v = [rhs[0, b * 16 + n] for b in range(N)]
            low, high = halves(v)
            q[0].append(v[0] + low)
            q[1].append(v[4] + high)
        for j in range(2):
            lines = []
            for a in range(4):
                v = q[j][a * 4:a * 4 + 4]
                low, high = halves(v)
                lines.append((v[0] + low) + before(high))
            low, high = halves(lines)
            coarse_load[j] = below(lines[0] + low, high)

    def moments(first, mids, second):
        even, odd = first + second, first - second
        return (
            float(RISE) * odd,
            float(W0 / 2) * even + float(W1 / 2) * mids[0] + float(W2 / 4) * mids[1],
            float(W0 / 2) * odd + float(W1 * SLOPE / (2 * KAPPA ** 2)) * mids[2],
        )

    def coarse_send(cycle):
        along_b = []
        for n in range(16):
            v = [sol[0, b * 16 + n] for b in range(N)]
            along_b.append(moments(v[0], v[1:4], v[4]))
        mixed = [[], [], [], []]
        plain = [[], [], [], []]
        for c in range(4):
            along_a = []
            for kind in range(3):
                v = [along_b[a * 4 + c][kind] for a in range(4)]
                along_a.append(moments(v[0], v[1:4], above(v[0])))
            rise, even, odd = along_a
            mixed[1].append(rise[1])
            mixed[2].append(even[0])
            mixed[3].append(rise[2] + odd[0])
            for m, x in enumerate((even[1], odd[1], even[2], odd[2])):
                plain[m].append(x)
        coeff = coeffs[OWN]
        y = [None] * 4
        for m in range(4):
            steep = float(RISE) * (plain[m][0] - after(plain[m][0]))
            if m == 0:
                y[m] = (None, coeff * steep)
            else:
                v = mixed[m]
                part = moments(v[0], v[1:4], after(v[0]))
                y[m] = (coeff * part[1], coeff * (part[2] + steep))
        for j in range(2):
            g = []
            for k in range(2):
                r = []
                for a in range(2):
                    one, two = y[2 * a][k], y[2 * a + 1][k]
                    r.append(plus(one, two) if j == 0 else minus(one, two))
                g.append(below(r[0] + r[1], r[0] - r[1]))
            cgot[cycle, OWN, j] = coarse_load[j] - ((g[0] + g[1]) + before(g[0] - g[1]))
        for d in SENDS:
            when_there(d, lambda d: remote(
                cgot.at[cycle, OWN], cgot.at[cycle, slot_at(d)], c_send.at[REACH + d], c_recv.at[cycle, slot_at(d)],
                place(d)).start())

    def correct(cycle):
        @pl.when(cycle == 0)
        def _():
            coarse_invert()

        for d in SENDS:
            when_there(d, lambda d: remote(
                cgot.at[cycle, OWN], cgot.at[cycle, OWN], c_send.at[REACH + d], c_recv.at[cycle, OWN],
                place(d)).wait_send())
        for d in RECVS:
            when_there(d, lambda d: remote(
                cgot.at[cycle, OWN], cgot.at[cycle, REACH + d], c_send.at[OWN], c_recv.at[cycle, REACH + d],
                place(d)).wait_recv())

        def q(e, j):
            return cgot[cycle, e, j if (e - OWN) % 2 == 0 else 1 - j]

        lines = SPAN - 1
        rc = [q(i, 1) + q(i + 1, 0) for i in range(lines)]
        x = [cinv[i] * rc[i] for i in range(lines)]

        def modes(v):
            up = after(v)
            parts = []
            for k in (v + up, v - up):
                high = above(k)
                parts.append((k + high, k - high))
            return [[parts[k][i] for k in range(2)] for i in range(2)]

        first, last = 0, lines - 1
        for sweep in range(NC - 1):
            m = {i: modes(x[i]) for i in range(first, last + 1)}
            sides = {}
            for e in range(first + 1, last + 1):
                coeff = coeffs[e]
                factor = [float(C1) * coeff, float(C2) * coeff, float(C3) * coeff]
                low, high = m[e - 1], m[e]
                part = []
                for i in range(2):
                    pair = []
                    for k in range(2):
                        odd = factor[i + k] * (low[i][k] - high[i][k])
                        if i + k == 0:
                            pair.append((odd, -odd))
                        else:
                            even = factor[i + k - 1] * (low[i][k] + high[i][k])
                            pair.append((even + odd, even - odd))
                    part.append(pair)
                sides[e] = part
            first, last = first + 1, last - 1
            new = list(x)
            for i in range(first, last + 1):
                y = [[sides[i + 1][a][k][0] + sides[i][a][k][1] for k in range(2)] for a in range(2)]
                g = [below(y[0][k] + y[1][k], y[0][k] - y[1][k]) for k in range(2)]
                image = (g[0] + g[1]) + before(g[0] - g[1])
                new[i] = x[i] + cinv[i] * (rc[i] - image)
            x = new

        base = OWN - 3
        m = {i: modes(x[i]) for i in range(base, base + 5)}
        kind = [0, 0, 0, 1, 1]
        grow = [1.0, 1.0, 1.0, SLOPE, 1.0]

        def ends(centre, weight, tilt):
            y = [[None] * N for _ in range(N)]
            for i in range(N):
                for k in range(N):
                    value = None
                    if centre is not None:
                        value = float(MU[i] * MU[k] * grow[i] * grow[k]) * centre[kind[i]][kind[k]]
                    if i == 4:
                        value = plus(value, float(RISE * weight * MU[k] * grow[k]) * tilt[1][kind[k]])
                    if k == 4:
                        value = plus(value, float(RISE * weight * MU[i] * grow[i]) * tilt[kind[i]][1])
                    y[i][k] = value
            return gather(y)

        def face_image(i):
            up, down = coeffs[i + 1], coeffs[i]
            both = up + down
            centre = [[float(RISE) * (up * (m[i][a][k] - m[i + 1][a][k]) - down * (m[i - 1][a][k] - m[i][a][k]))
                       for k in range(2)] for a in range(2)]
            tilt = [[None if a + k == 0 else both * m[i][a][k] for k in range(2)] for a in range(2)]
            h = ends(centre, W0, tilt)
            return [h[a][c] for a in range(4) for c in range(4)]

        for i, targets in ((OWN - 2, ((1, 0),)), (OWN - 1, ((1, 64), (0, 0))), (OWN, ((0, 64),))):
            values = face_image(i)
            for r, at in targets:
                for n, value in enumerate(values):
                    tot[r, at + n] = tot[r, at + n] - value
        scale = [1.0, 1.0, 1.0, SLOPE]

        def nodal(i):
            v = x[i]
            up = after(v)
            high = above(v)
            tiles = [[v, v + up, v - up], [v + high, m[i][0][0], m[i][0][1]], [v - high, m[i][1][0], m[i][1][1]]]
            pick = [0, 1, 1, 2]
            made = {}
            out = []
            for a in range(4):
                for c in range(4):
                    key = (pick[a], pick[c])
                    if key not in made:
                        factor = float(scale[a] * scale[c])
                        made[key] = tiles[key[0]][key[1]] if factor == 1.0 else factor * tiles[key[0]][key[1]]
                    out.append((key, made[key]))
            return out

        at_line = {i: nodal(i) for i in (OWN - 2, OWN - 1, OWN)}
        for r in range(2):
            low, high = OWN - 1 - r, OWN - r
            coeff = coeffs[OWN - r]
            for kindb in range(2):
                diff = [[None if a + k == 0 else
                         coeff * (m[low][a][k] - m[high][a][k] if kindb else m[low][a][k] + m[high][a][k])
                         for k in range(2)] for a in range(2)]
                h = ends(None, 1.0, diff)
                for b in ((3,) if kindb else (1, 2)):
                    factor = float(MUB[b] * (SLOPE if kindb else 1.0))
                    for a in range(4):
                        for c in range(4):
                            if h[a][c] is not None:
                                tot[r, st(b, a, c)] = tot[r, st(b, a, c)] - factor * h[a][c]
                made = {}
                for n in range(16):
                    key, lower_value = at_line[low][n]
                    upper_value = at_line[high][n][1]
                    if key not in made:
                        made[key] = (float(SLOPE) * (lower_value - upper_value) if kindb
                                     else lower_value + upper_value)
                    for b in ((3,) if kindb else (1, 2)):
                        sol[r, b * 16 + n] = sol[r, b * 16 + n] + made[key]
            for n in range(16):
                sol[r, n] = sol[r, n] + at_line[low][n][1]
                sol[r, 64 + n] = sol[r, 64 + n] + at_line[high][n][1]

    def emit(field, out_ref, dual):
        def split(mid, double, odd):
            if dual:
                odd = float(KAPPA) * odd
                return mid + odd, 2.0 * double, mid - odd
            even, odd = 0.5 * mid, float(0.5 / KAPPA) * odd
            return even + odd, 0.5 * double, even - odd

        def one(b, values):
            lines = []
            for a in range(4):
                v = values[a * 4:a * 4 + 4]
                lines.append([v[0], *split(*v[1:]), after(v[0])])
            for c in range(N):
                v = [lines[a][c] for a in range(4)]
                for a, tile in enumerate([v[0], *split(*v[1:]), above(v[0])]):
                    out_ref[raw(a, b, c)] = tile[0:layers]

        for b in (0, 4):
            one(b, [field[0, b * 16 + n] for n in range(16)])
        mids = [split(field[0, 16 + n], field[0, 32 + n], field[0, 48 + n]) for n in range(16)]
        for b in range(1, 4):
            one(b, [v[b - 1] for v in mids])

    halo_copy(0, place(0, True)).wait()
    for b in (4, 0, 1, 2, 3):
        assemble(0, b)
        put(0, b, [rhs[0, b * 16 + n] for n in range(16)])
        if b == 4:
            send_face(0, [tot[0, 64 + n] for n in range(16)])
    sol[...] = jnp.zeros_like(sol)
    half_copy(1, 0, OWN, place(0, True)).wait()
    for d in SENDS:
        if d not in NEAR_SENDS:
            when_there(d, lambda d: half_copy(1, d, slot_at(d), place(d), 1).start())
    for d in NEAR_RECVS:
        @pl.when(there(d))
        def _():
            half_came(0, d)
            half_came(1, d)
    for e in range(OWN - 2, OWN + 2):
        join_coeff(e)
    invert()
    restrict_load()

    @pl.when(there(-1))
    def _():
        part_copy(0).wait()
        halo_copy(1, place(-1, True)).wait()

    assemble(1, 4)
    for n in range(16):
        joined = tot[0, n] + rhs[1, 64 + n]
        tot[0, n] = joined
        tot[1, 64 + n] = joined
    for b in range(4):
        update(0, b)
    add_near(0)
    update(0, 4)

    def step(s, _):
        cycle = s // PERIOD
        live = s < STEPS - 1
        coarse = (lax.rem(s, PERIOD) == NPRE) & live
        deferred = lax.rem(s - 1, PERIOD) != NPRE

        behind = deferred & (s > 1)

        @pl.when(coarse)
        def _():
            coarse_send(cycle)

        expand(0, range(N))
        cross(0)
        mine = plane(0, 4)
        put(0, 4, mine)
        send_face(s, mine)

        @pl.when(there(2))
        def _():
            far_copy(s - 1).wait_send()

        @pl.when(behind)
        def _():
            for b in range(4):
                put(1, b, plane(1, b))
                if b:
                    update(1, b)
            update(1, 4)

        for b in range(4):
            put(0, b, plane(0, b))

        @pl.when(s == 1)
        def _():
            when_there(-1, lambda d: part_copy(1).wait())
            for b in range(4):
                assemble(1, b)
                put(1, b, [rhs[1, b * 16 + n] for n in range(16)])
                if b:
                    update(1, b)
            update(1, 4)

        expand(1, range(1, N))

        @pl.when(deferred)
        def _():
            add_far(s - 1)
            update(1, 0)

        expand(1, (0,))
        cross(1)
        for n, x in enumerate(plane(1, 4)):
            joined = tot[0, n] + x
            tot[0, n] = joined
            tot[1, 64 + n] = joined

        @pl.when(coarse)
        def _():
            for b in range(4):
                put(1, b, plane(1, b))

        @pl.when(jnp.logical_not(live))
        def _():
            emit(sol, sol_out, False)

        @pl.when(jnp.logical_not(coarse))
        def _():
            for b in range(4):
                update(0, b)

        add_near(s)

        @pl.when(coarse)
        def _():
            add_far(s)
            correct(cycle)
            for b in range(4):
                update(0, b)
                update(1, b + 1)
            update(1, 0)

        update(0, 4)
        return 0

    lax.fori_loop(1, STEPS, step, 0)
    emit(tot, res_out, True)


def per_device(sizes, load, kappa, wet):
    layers, _, width = kappa.shape
    nodes = N * N * N
    tile = (2 * layers, width)
    half = (layers, width)
    sizes = sizes + (layers, width)
    out = jax.ShapeDtypeStruct((nodes, layers, width), F32)
    vmem = pl.BlockSpec(memory_space=pltpu.VMEM)
    fold = width // HALO
    groups = 80 // fold
    messages = 8 + 8 // fold
    dma = pltpu.SemaphoreType.DMA
    solution, residual = pl.pallas_call(
        functools.partial(kernel, sizes),
        out_shape=(out, out),
        in_specs=[pl.BlockSpec(memory_space=pltpu.HBM), vmem, vmem],
        out_specs=(vmem, vmem),
        scratch_shapes=[
            pltpu.VMEM((nodes,) + half, F32),
            pltpu.VMEM((groups + 81,) + half, F32),
            pltpu.VMEM((81,) + half, F32),
            pltpu.VMEM((2, groups + 1) + half, F32),
            pltpu.VMEM((2, SPAN + 1) + half, F32),
            pltpu.VMEM((SPAN,) + tile, F32),
            pltpu.VMEM((2, 80) + tile, F32),
            pltpu.VMEM((2, 80) + tile, F32),
            pltpu.VMEM((2, 80) + tile, F32),
            pltpu.VMEM((2, 80) + tile, F32),
            pltpu.VMEM((2, nodes) + tile, F32),
            pltpu.VMEM((2, nodes) + tile, F32),
            pltpu.VMEM((2,) + tile, F32),
            pltpu.VMEM((STEPS, messages) + tile, F32),
            pltpu.VMEM((2, STEPS, messages) + tile, F32),
            pltpu.VMEM((CYCLES, SPAN, 2) + tile, F32),
            pltpu.VMEM((SPAN - 1,) + tile, F32),
            dma, dma((4,)), dma((4,)), dma((2, SPAN + 1)), dma((2, SPAN + 1)),
            dma((2, STEPS)), dma((2, STEPS)), dma((SPAN + 1,)), dma((CYCLES, SPAN + 1)),
        ],
        compiler_params=pltpu.CompilerParams(collective_id=0, has_side_effects=True, vmem_limit_bytes=16 * 2 ** 20),
    )(load.reshape(nodes, layers, width), kappa.reshape(layers, width), wet.reshape(layers, width))
    return solution.reshape(load.shape), residual.reshape(load.shape)


def solution(mesh):
    sizes = tuple(mesh.shape[name] for name in ("ex", "ey", "lin"))
    field = P(None, None, None, None, ("ey", "lin"), "ex")
    cell = P(None, ("ey", "lin"), "ex")
    return jax.shard_map(
        functools.partial(per_device, sizes), mesh=mesh, in_specs=(field, cell, cell),
        out_specs=(field, field), check_vma=False,
    )
```

```python
import functools
import math

import jax
import jax.numpy as jnp
import numpy as np
from jax import lax
from jax.experimental import pallas as pl
from jax.experimental.pallas import tpu as pltpu
from jax.sharding import PartitionSpec as P

N = 5
CYCLES = 2
NPRE = 2
NPOST = 2
NC = 4
PERIOD = NPRE + NPOST
FINE_RELAX = 0.25
COARSE_RELAX = 0.4
STEPS = CYCLES * PERIOD + 1
REACH = NC + 2
SPAN = 2 * REACH
OWN = REACH
HALO = 32
MESH = pl.DeviceIdType.MESH
F32 = jnp.float32


def node_tables():
    points = np.array([-1.0, -math.sqrt(3.0 / 7.0), 0.0, math.sqrt(3.0 / 7.0), 1.0])
    weights = np.array([0.1, 49.0 / 90.0, 32.0 / 45.0, 49.0 / 90.0, 0.1])
    eye_table = np.eye(points.shape[0])
    spread = points[:, None] - points[None, :] + eye_table
    factors = np.prod(spread, axis=1)
    deriv = factors[:, None] / (factors[None, :] * spread)
    deriv = np.where(eye_table > 0, (np.sum(1.0 / spread, axis=1) - 1.0)[:, None], deriv)
    stiff = deriv.T @ (weights[:, None] * deriv)
    mass = eye_table * weights[:, None]
    interp = np.stack([(1.0 - points) / 2.0, (1.0 + points) / 2.0], axis=1)
    return stiff, weights, interp, interp.T @ stiff @ interp, interp.T @ mass @ interp


S, WEIGHTS, INTERP, SC, WC = node_tables()
ALPHA = (S[0, 0] + S[0, 4]) / 2
BETA = (S[0, 1] + S[0, 3]) / 2
GAMMA = (S[1, 1] + S[1, 3]) / 2
KAPPA = (S[0, 1] - S[0, 3]) / (S[0, 0] - S[0, 4])
ODD = (S[0, 0] - S[0, 4]) / 2
DELTA = (S[1, 1] - S[1, 3]) / (2 * KAPPA ** 2) - ODD
W0, W1, W2 = WEIGHTS[:3]
MU = [W0 / 2, W1 / 2, W2 / 4, W1 / (2 * KAPPA ** 2), W0 / 2]
MUB = [W0, W1 / 2, W2 / 4, W1 / (2 * KAPPA ** 2), W0]
NU = [1.0, 2.0, 4.0, 2 * KAPPA ** 2, 1.0]
SLOPE = KAPPA * (INTERP[1, 0] - INTERP[3, 0])
RISE = ODD * (1 + SLOPE)
NODE = [0, 1, 2, 1, 4]
DIAG = np.diag(S) / WEIGHTS
W3 = WEIGHTS[:, None, None] * WEIGHTS[None, :, None] * WEIGHTS[None, None, :]
K3 = W3 * (DIAG[:, None, None] + DIAG[None, :, None] + DIAG[None, None, :])
CS = (SC[0, 0] - SC[0, 1]) / 2
CE, CO = (WC[0, 0] + WC[0, 1]) / 2, (WC[0, 0] - WC[0, 1]) / 2
C1, C2, C3 = CS * CE * CE, 2 * CS * CO * CE, 3 * CS * CO * CO
SENDS = [d for d in range(-REACH + 1, REACH + 1) if d != 0]
RECVS = [d for d in range(-REACH, REACH) if d != 0]
NEAR_SENDS = [-1, 1, 2]
NEAR_RECVS = [-1, 1, -2]


def st(b, a, c):
    return (b * 4 + a) * 4 + c


def xi(b, i, k):
    return (b * N + i) * N + k


def line_apply(e0, e1, z, o1, o0, scale):
    q0, q1 = e0 - z, e1 - z
    r0 = float(ALPHA * scale) * q0 + float(BETA * scale) * q1
    r1 = float(BETA * scale) * q0 + float(GAMMA * scale) * q1
    s0 = float(ODD * scale) * (o0 + o1)
    return r0, r1, r0 + r1, s0 + float(DELTA * scale) * o1, s0


def plus(x, y):
    if x is None or y is None:
        return x if y is None else y
    return x + y


def minus(x, y):
    if y is None:
        return x
    return -y if x is None else x - y


def kernel(
    sizes, load_ref, kappa_ref, wet_ref, sol_out, res_out,
    load, kappa, wet, part, got_part, got_halo, halves_of, coeffs,
    rhs, sol, tot, sinv, xs, bs, coarse_load, packed, got, cgot, cinv,
    load_sem, x_send, x_recv, k_send, k_recv, f_send, f_recv, c_send, c_recv,
):
    ex_count, ey_count, lin_count, layers, width = sizes
    ex, ey, lin = lax.axis_index("ex"), lax.axis_index("ey"), lax.axis_index("lin")
    rows = ey_count * lin_count
    row = ey * lin_count + lin
    par = lax.rem(lin, 2)
    sgn = 1 - 2 * par
    fold = width // HALO
    groups = 80 // fold
    first = 16 // fold

    sub = lax.broadcasted_iota(jnp.int32, (2 * layers, width), 0)
    lane = lax.broadcasted_iota(jnp.int32, (2 * layers, width), 1)
    layer = sub % layers
    bottom, top = layer == 0, layer == layers - 1
    first_lane, last_lane = lane == 0, lane == width - 1
    near = jnp.where(ex == 0, lane, width - 1 - lane)
    real = (sub < layers) | (near < HALO)
    lower = sub < layers

    def before(x):
        y = pltpu.roll(x, 1, 1)
        return jnp.where(first_lane, pltpu.roll(y, layers, 0), y)

    def after(x):
        y = pltpu.roll(x, width - 1, 1)
        return jnp.where(last_lane, pltpu.roll(y, layers, 0), y)

    def below(low, high):
        return jnp.where(bottom, low, low + pltpu.roll(high, 1, 0))

    def above(low):
        return jnp.where(top, 0.0, pltpu.roll(low, 2 * layers - 1, 0))

    def there(d):
        at = row + sgn * d
        return (at >= 0) & (at < rows)

    def place(d, other=False):
        at = row + sgn * d
        return (1 - ex if other else ex, at // lin_count, at % lin_count)

    def when_there(d, fn):
        @pl.when(there(d))
        def _():
            fn(d)

    def slot_at(d):
        return REACH + (-d if d % 2 == 0 else d)

    def remote(src, dst, send, recv, device):
        return pltpu.make_async_remote_copy(
            src_ref=src, dst_ref=dst, send_sem=send, recv_sem=recv, device_id=device, device_id_type=MESH)

    fetches = [pltpu.make_async_copy(src, dst, load_sem.at[k]) for k, (src, dst) in enumerate(
        ((kappa_ref, kappa), (wet_ref, wet), (load_ref, load)))]
    for fetch in fetches:
        fetch.start()
    halves_of[...] = jnp.zeros_like(halves_of)
    cgot[...] = jnp.zeros_like(cgot)

    @pl.when(jnp.logical_not(there(-1)))
    def _():
        got_part[...] = jnp.zeros_like(got_part)
        got_halo[1] = jnp.zeros_like(got_halo[1])

    def greet(device):
        pl.semaphore_signal(pltpu.get_barrier_semaphore(), inc=1, device_id=device, device_id_type=MESH)

    greet((1 - ex, ey, lin))
    expected = jnp.int32(1)
    for d in range(1, REACH + 1):
        for e in (-d, d):
            @pl.when(there(e))
            def _():
                greet(place(e))
                if d <= 2:
                    greet(place(e, True))
            expected = expected + jnp.where(there(e), 2 if d <= 2 else 1, 0)

    fetches[0].wait()
    fetches[1].wait()
    halves_of[0, OWN] = kappa[...] * jnp.where(wet[...] == 1, F32(1.0), F32(0.05))

    def raw(a, b, c):
        return (a * N + b + par * (N - 1 - 2 * b)) * N + c

    def to_dual(f):
        return [(f[1] + f[3]) * 0.5, f[2] * 0.5, (f[1] - f[3]) * float(0.5 / KAPPA)]

    def load_plane(b):
        nothing = jnp.zeros((layers, width), F32)
        tiles = [jnp.concatenate([load[raw(n // N, b, n % N)], nothing], axis=0) for n in range(N * N)]
        lines = []
        for a in range(N):
            f = tiles[a * N:a * N + N]
            lines.append([f[0] + before(f[4])] + to_dual(f))
        columns = []
        for c in range(4):
            f = [lines[a][c] for a in range(N)]
            columns.append([below(f[0], f[4])] + to_dual(f))
        return [columns[c][a] for a in range(4) for c in range(4)]

    fetches[2].wait()
    for b in (0, 4, 2, 1, 3):
        for n, x in enumerate(load_plane(b)):
            if b == 3:
                other = rhs[0, 16 + n]
                rhs[0, 48 + n] = (other - x) * float(0.5 / KAPPA)
                rhs[0, 16 + n] = (other + x) * 0.5
            else:
                rhs[0, b * 16 + n] = x * 0.5 if b == 2 else x
    def at_group(g):
        return g if g < first else g + 1

    source = jnp.where(ex == 0, fold - 1, 0)
    turn = (lane // HALO + fold - source) % fold
    for g in range(groups):
        mixed = None
        for j in range(fold):
            x = rhs[0, g * fold + j]
            part[groups + 2 + g * fold + j] = x[0:layers]
            mixed = x if j == 0 else jnp.where(turn == j, pltpu.roll(x, HALO * j, 1), mixed)
        part[at_group(g)] = mixed[0:layers]
    mixed = None
    for j in range(20):
        x = rhs[0, 4 * j]
        mixed = x if j == 0 else jnp.where(lane == j, pltpu.roll(x, j, 1), mixed)
    for at in (first, groups + 1):
        part[at] = pltpu.roll(mixed, layers, 0)[0:layers]

    pl.semaphore_wait(pltpu.get_barrier_semaphore(), expected)

    def half_copy(h, d, slot, device, source=0):
        return remote(halves_of.at[source, OWN], halves_of.at[h, slot], k_send.at[h, REACH + d], k_recv.at[h, slot],
                      device)

    def half_sent(h, d):
        half_copy(h, d, OWN, place(d), h).wait_send()

    def half_came(h, d):
        half_copy(h, d, REACH + d, place(d), h).wait_recv()

    half_copy(1, 0, OWN, place(0, True)).start()
    for d in NEAR_SENDS:
        @pl.when(there(d))
        def _():
            half_copy(0, d, slot_at(d), place(d)).start()
            half_copy(1, d, slot_at(d), place(d, True)).start()

    def halo_copy(k):
        at, size = ((0, groups + 1), (0, first + 1), (first + 1, groups - first))[k]
        return remote(part.at[at:at + size], got_halo.at[min(k, 1), at:at + size], x_send.at[k], x_recv.at[k],
                      place(-1 if k else 0, True))

    def part_copy(k):
        at, size = ((0, 17), (17, 64))[k]
        return remote(part.at[groups + 1 + at:groups + 1 + at + size], got_part.at[at:at + size], x_send.at[3 + k],
                      x_recv.at[3 + k], place(-1))

    halo_copy(0).start()

    @pl.when(there(-1))
    def _():
        halo_copy(1).start()
        part_copy(0).start()
        part_copy(1).start()
        halo_copy(2).start()

    for d in SENDS:
        if d not in NEAR_SENDS:
            when_there(d, lambda d: half_copy(0, d, slot_at(d), place(d)).start())

    outer = (sub >= layers) & (near < HALO)
    entering = first_lane & ((sub >= layers) | (ex == 1))

    def assemble(r, b):
        source_b = b if r == 0 or 0 < b < 4 else 4 - b
        nothing = jnp.zeros((layers, width), F32)
        spill = jnp.concatenate([got_halo[r, first], got_part[0] if r else nothing], axis=0)
        for a in range(4):
            for c in range(4):
                n, m = st(b, a, c), st(source_b, a, c)
                h = got_halo[r, at_group(m // fold)]
                h = jnp.concatenate([h, h], axis=0)
                if m % fold:
                    h = pltpu.roll(h, width - HALO * (m % fold), 1)
                h = jnp.where(outer, h, 0.0)
                if r == 0:
                    x = rhs[0, n] + h
                else:
                    p = got_part[1 + m]
                    x = jnp.where(lower, jnp.concatenate([p, p], axis=0), h)
                if c == 0:
                    j = m // 4
                    x = x + jnp.where(entering, pltpu.roll(spill, width - j, 1) if j else spill, 0.0)
                rhs[r, n] = -x if r == 1 and b == 3 else x

    block = lax.rem(lane + jnp.where(ex == 0, 0, HALO - 1), width) // HALO

    def swap(x):
        return pltpu.roll(x, layers, 0)

    def pack(s, x):
        for p in range(8):
            packed[s, p] = jnp.where(lower, x[2 * p], swap(x[2 * p + 1]))
        for p in range(8 // fold):
            halves = []
            for h in range(2):
                group = x[(2 * p + h) * fold:(2 * p + h + 1) * fold]
                mixed = group[0]
                for j in range(1, fold):
                    mixed = jnp.where(block == j, pltpu.roll(group[j], HALO * j, 1), mixed)
                halves.append(mixed)
            packed[s, 8 + p] = jnp.where(lower, swap(halves[0]), halves[1])

    def unpack(kind, s):
        x = []
        for p in range(8 // fold):
            tile = got[kind, s, 8 + p]
            for half in (swap(tile), tile):
                for j in range(fold):
                    other = half if j == 0 else pltpu.roll(half, width - HALO * j, 1)
                    n = len(x)
                    mine = got[kind, s, n // 2]
                    mine = mine if n % 2 == 0 else swap(mine)
                    x.append(jnp.where(lower, mine, jnp.where(block == 0, other, 0.0)))
        return x

    def near_copy(s):
        return remote(packed.at[s], got.at[0, s], f_send.at[0, s], f_recv.at[0, s], place(1))

    def far_copy(s):
        return remote(packed.at[s], got.at[1, s], f_send.at[1, s], f_recv.at[1, s], place(2))

    def send_face(s, values):
        pack(s, values)
        near_copy(s).start()

        @pl.when(there(2) & (s < STEPS - 1))
        def _():
            far_copy(s).start()

    def add_near(s):
        near_copy(s).wait()
        for n, x in enumerate(unpack(0, s)):
            tot[0, 64 + n] = tot[0, 64 + n] + x

    def add_far(s):
        @pl.when(there(-2))
        def _():
            far_copy(s).wait_recv()
            for n, x in enumerate(unpack(1, s)):
                tot[1, n] = tot[1, n] + x

    def expand(r, planes):
        for b in planes:
            w = []
            for a in range(4):
                v = [sol[r, st(b, a, c)] for c in range(4)]
                up = after(v[0])
                w.append([v[0] + up, v[1], v[2], v[3], v[0] - up])
            for k in range(N):
                up = above(w[0][k])
                xs[r, xi(b, 0, k)] = w[0][k] + up
                xs[r, xi(b, 4, k)] = w[0][k] - up
                for a in range(1, 4):
                    xs[r, xi(b, a, k)] = w[a][k]

    def cross(r):
        for i in range(N):
            for k in range(N):
                v = [xs[r, xi(b, i, k)] for b in range(N)]
                r0, r1, rz, s1, s0 = line_apply(v[0] + v[4], v[1], v[2], v[3], v[0] - v[4], MU[i] * MU[k])
                for b, x in enumerate((r0 + s0, r1, rz, s1, r0 - s0)):
                    bs[r, xi(b, i, k)] = x

    def gather(y):
        g = []
        for k in range(N):
            low, high = plus(y[0][k], y[4][k]), minus(y[0][k], y[4][k])
            g.append([None if low is None else below(low, high)] + [y[i][k] for i in range(1, 4)])
        h = []
        for a in range(4):
            low, high = plus(g[0][a], g[4][a]), minus(g[0][a], g[4][a])
            h.append([None if low is None else low + before(high)] + [g[k][a] for k in range(1, 4)])
        return h

    def plane(r, b):
        coeff = coeffs[OWN - r]
        x = [[xs[r, xi(b, i, k)] for k in range(N)] for i in range(N)]
        along_c = [line_apply(*x[i], MUB[b] * MU[i]) for i in range(N)]
        along_a = [line_apply(*[x[i][k] for i in range(N)], MUB[b] * MU[k]) for k in range(N)]
        y = []
        for i in range(N):
            line = []
            for k in range(N):
                terms = sorted(((b == 2, bs[r, xi(b, i, k)]), (k == 2, along_c[i][k]), (i == 2, along_a[k][i])),
                               key=lambda t: t[0])
                total = -terms[0][1] if terms[0][0] else terms[0][1]
                for negative, term in terms[1:]:
                    total = total - term if negative else total + term
                line.append(coeff * total)
            y.append(line)
        h = gather(y)
        return [rhs[r, st(b, a, c)] - h[a][c] for a in range(4) for c in range(4)]

    def put(r, b, values):
        for n, x in enumerate(values):
            tot[r, b * 16 + n] = x

    def update(r, b):
        for n in range(b * 16, b * 16 + 16):
            sol[r, n] = sol[r, n] + sinv[r, n] * tot[r, n]

    def inverted(x):
        return jnp.where(x > 0.0, 1.0 / jnp.where(x > 0.0, x, 1.0), 0.0)

    def invert():
        for r in range(2):
            here = coeffs[OWN - r]
            for bl, x in (((1, 2, 3), here), ((0,), here + coeffs[OWN - r - 1]), ((4,), here + coeffs[OWN - r + 1])):
                xc = x + before(x)
                tiles = [[inverted(below(xc, xc)), inverted(below(x, x))], [inverted(xc), inverted(x)]]
                for b in bl:
                    for a in range(4):
                        for c in range(4):
                            factor = FINE_RELAX * NU[a] * NU[b] * NU[c] / K3[NODE[a], NODE[b], NODE[c]]
                            sinv[r, st(b, a, c)] = float(factor) * tiles[min(a, 1)][min(c, 1)]

    def join_coeff(e):
        coeffs[e] = jnp.where(real, jnp.concatenate([halves_of[0, e], halves_of[1, e]], axis=0), 0.0)

    def coarse_invert():
        for d in SENDS:
            @pl.when(there(d))
            def _():
                half_sent(0, d)
                half_sent(1, d)
        for d in RECVS:
            if d not in NEAR_RECVS:
                @pl.when(there(d))
                def _():
                    half_came(0, d)
                    half_came(1, d)
        for e in range(SPAN):
            if abs(e - OWN + 0.5) > 2:
                join_coeff(e)
        corner = 3.0 * SC[0, 0] * WC[0, 0] ** 2
        for i in range(SPAN - 1):
            pair = coeffs[i] + coeffs[i + 1]
            pair = pair + before(pair)
            cinv[i] = float(COARSE_RELAX / corner) * inverted(below(pair, pair))

    def halves(v):
        even, odd = v[1] + v[2], float(SLOPE) * v[3]
        return even + odd, even - odd

    def restrict_load():
        q = [[], []]
        for n in range(16):
            v = [rhs[0, b * 16 + n] for b in range(N)]
            low, high = halves(v)
            q[0].append(v[0] + low)
            q[1].append(v[4] + high)
        for j in range(2):
            lines = []
            for a in range(4):
                v = q[j][a * 4:a * 4 + 4]
                low, high = halves(v)
                lines.append((v[0] + low) + before(high))
            low, high = halves(lines)
            coarse_load[j] = below(lines[0] + low, high)

    def moments(first, mids, second):
        even, odd = first + second, first - second
        return (
            float(RISE) * odd,
            float(W0 / 2) * even + float(W1 / 2) * mids[0] + float(W2 / 4) * mids[1],
            float(W0 / 2) * odd + float(W1 * SLOPE / (2 * KAPPA ** 2)) * mids[2],
        )

    def coarse_send(cycle):
        along_b = []
        for n in range(16):
            v = [sol[0, b * 16 + n] for b in range(N)]
            along_b.append(moments(v[0], v[1:4], v[4]))
        mixed = [[], [], [], []]
        plain = [[], [], [], []]
        for c in range(4):
            along_a = []
            for kind in range(3):
                v = [along_b[a * 4 + c][kind] for a in range(4)]
                along_a.append(moments(v[0], v[1:4], above(v[0])))
            rise, even, odd = along_a
            mixed[1].append(rise[1])
            mixed[2].append(even[0])
            mixed[3].append(rise[2] + odd[0])
            for m, x in enumerate((even[1], odd[1], even[2], odd[2])):
                plain[m].append(x)
        coeff = coeffs[OWN]
        y = [None] * 4
        for m in range(4):
            steep = float(RISE) * (plain[m][0] - after(plain[m][0]))
            if m == 0:
                y[m] = (None, coeff * steep)
            else:
                v = mixed[m]
                part = moments(v[0], v[1:4], after(v[0]))
                y[m] = (coeff * part[1], coeff * (part[2] + steep))
        for j in range(2):
            g = []
            for k in range(2):
                r = []
                for a in range(2):
                    one, two = y[2 * a][k], y[2 * a + 1][k]
                    r.append(plus(one, two) if j == 0 else minus(one, two))
                g.append(below(r[0] + r[1], r[0] - r[1]))
            cgot[cycle, OWN, j] = coarse_load[j] - ((g[0] + g[1]) + before(g[0] - g[1]))
        for d in SENDS:
            when_there(d, lambda d: remote(
                cgot.at[cycle, OWN], cgot.at[cycle, slot_at(d)], c_send.at[REACH + d], c_recv.at[cycle, slot_at(d)],
                place(d)).start())

    def correct(cycle):
        @pl.when(cycle == 0)
        def _():
            coarse_invert()

        for d in SENDS:
            when_there(d, lambda d: remote(
                cgot.at[cycle, OWN], cgot.at[cycle, OWN], c_send.at[REACH + d], c_recv.at[cycle, OWN],
                place(d)).wait_send())
        for d in RECVS:
            when_there(d, lambda d: remote(
                cgot.at[cycle, OWN], cgot.at[cycle, REACH + d], c_send.at[OWN], c_recv.at[cycle, REACH + d],
                place(d)).wait_recv())

        def q(e, j):
            return cgot[cycle, e, j if (e - OWN) % 2 == 0 else 1 - j]

        lines = SPAN - 1
        rc = [q(i, 1) + q(i + 1, 0) for i in range(lines)]
        x = [cinv[i] * rc[i] for i in range(lines)]

        def modes(v):
            up = after(v)
            parts = []
            for k in (v + up, v - up):
                high = above(k)
                parts.append((k + high, k - high))
            return [[parts[k][i] for k in range(2)] for i in range(2)]

        begin, end = 0, lines - 1
        for sweep in range(NC - 1):
            m = {i: modes(x[i]) for i in range(begin, end + 1)}
            sides = {}
            for e in range(begin + 1, end + 1):
                coeff = coeffs[e]
                factor = [float(C1) * coeff, float(C2) * coeff, float(C3) * coeff]
                low, high = m[e - 1], m[e]
                part = []
                for i in range(2):
                    pair = []
                    for k in range(2):
                        odd = factor[i + k] * (low[i][k] - high[i][k])
                        if i + k == 0:
                            pair.append((odd, -odd))
                        else:
                            even = factor[i + k - 1] * (low[i][k] + high[i][k])
                            pair.append((even + odd, even - odd))
                    part.append(pair)
                sides[e] = part
            begin, end = begin + 1, end - 1
            new = list(x)
            for i in range(begin, end + 1):
                y = [[sides[i + 1][a][k][0] + sides[i][a][k][1] for k in range(2)] for a in range(2)]
                g = [below(y[0][k] + y[1][k], y[0][k] - y[1][k]) for k in range(2)]
                image = (g[0] + g[1]) + before(g[0] - g[1])
                new[i] = x[i] + cinv[i] * (rc[i] - image)
            x = new

        base = OWN - 3
        m = {i: modes(x[i]) for i in range(base, base + 5)}
        kind = [0, 0, 0, 1, 1]
        grow = [1.0, 1.0, 1.0, SLOPE, 1.0]

        def ends(centre, weight, tilt):
            y = [[None] * N for _ in range(N)]
            for i in range(N):
                for k in range(N):
                    value = None
                    if centre is not None:
                        value = float(MU[i] * MU[k] * grow[i] * grow[k]) * centre[kind[i]][kind[k]]
                    if i == 4:
                        value = plus(value, float(RISE * weight * MU[k] * grow[k]) * tilt[1][kind[k]])
                    if k == 4:
                        value = plus(value, float(RISE * weight * MU[i] * grow[i]) * tilt[kind[i]][1])
                    y[i][k] = value
            return gather(y)

        def face_image(i):
            up, down = coeffs[i + 1], coeffs[i]
            both = up + down
            centre = [[float(RISE) * (up * (m[i][a][k] - m[i + 1][a][k]) - down * (m[i - 1][a][k] - m[i][a][k]))
                       for k in range(2)] for a in range(2)]
            tilt = [[None if a + k == 0 else both * m[i][a][k] for k in range(2)] for a in range(2)]
            h = ends(centre, W0, tilt)
            return [h[a][c] for a in range(4) for c in range(4)]

        for i, targets in ((OWN - 2, ((1, 0),)), (OWN - 1, ((1, 64), (0, 0))), (OWN, ((0, 64),))):
            values = face_image(i)
            for r, at in targets:
                for n, value in enumerate(values):
                    tot[r, at + n] = tot[r, at + n] - value
        scale = [1.0, 1.0, 1.0, SLOPE]

        def nodal(i):
            v = x[i]
            up = after(v)
            high = above(v)
            tiles = [[v, v + up, v - up], [v + high, m[i][0][0], m[i][0][1]], [v - high, m[i][1][0], m[i][1][1]]]
            pick = [0, 1, 1, 2]
            made = {}
            out = []
            for a in range(4):
                for c in range(4):
                    key = (pick[a], pick[c])
                    if key not in made:
                        factor = float(scale[a] * scale[c])
                        made[key] = tiles[key[0]][key[1]] if factor == 1.0 else factor * tiles[key[0]][key[1]]
                    out.append((key, made[key]))
            return out

        at_line = {i: nodal(i) for i in (OWN - 2, OWN - 1, OWN)}
        for r in range(2):
            low, high = OWN - 1 - r, OWN - r
            coeff = coeffs[OWN - r]
            for kindb in range(2):
                diff = [[None if a + k == 0 else
                         coeff * (m[low][a][k] - m[high][a][k] if kindb else m[low][a][k] + m[high][a][k])
                         for k in range(2)] for a in range(2)]
                h = ends(None, 1.0, diff)
                for b in ((3,) if kindb else (1, 2)):
                    factor = float(MUB[b] * (SLOPE if kindb else 1.0))
                    for a in range(4):
                        for c in range(4):
                            if h[a][c] is not None:
                                tot[r, st(b, a, c)] = tot[r, st(b, a, c)] - factor * h[a][c]
                made = {}
                for n in range(16):
                    key, lower_value = at_line[low][n]
                    upper_value = at_line[high][n][1]
                    if key not in made:
                        made[key] = (float(SLOPE) * (lower_value - upper_value) if kindb
                                     else lower_value + upper_value)
                    for b in ((3,) if kindb else (1, 2)):
                        sol[r, b * 16 + n] = sol[r, b * 16 + n] + made[key]
            for n in range(16):
                sol[r, n] = sol[r, n] + at_line[low][n][1]
                sol[r, 64 + n] = sol[r, 64 + n] + at_line[high][n][1]

    def emit(field, out_ref, dual):
        def split(mid, double, odd):
            if dual:
                odd = float(KAPPA) * odd
                return mid + odd, 2.0 * double, mid - odd
            even, odd = 0.5 * mid, float(0.5 / KAPPA) * odd
            return even + odd, 0.5 * double, even - odd

        def one(b, values):
            lines = []
            for a in range(4):
                v = values[a * 4:a * 4 + 4]
                lines.append([v[0], *split(*v[1:]), after(v[0])])
            for c in range(N):
                v = [lines[a][c] for a in range(4)]
                for a, tile in enumerate([v[0], *split(*v[1:]), above(v[0])]):
                    out_ref[raw(a, b, c)] = tile[0:layers]

        for b in (0, 4):
            one(b, [field[0, b * 16 + n] for n in range(16)])
        mids = [split(field[0, 16 + n], field[0, 32 + n], field[0, 48 + n]) for n in range(16)]
        for b in range(1, 4):
            one(b, [v[b - 1] for v in mids])

    halo_copy(0).wait()
    for b in (4, 0, 1, 2, 3):
        assemble(0, b)
        put(0, b, [rhs[0, b * 16 + n] for n in range(16)])
        if b == 4:
            send_face(0, [tot[0, 64 + n] for n in range(16)])
    sol[...] = jnp.zeros_like(sol)
    half_copy(1, 0, OWN, place(0, True)).wait()
    for d in SENDS:
        if d not in NEAR_SENDS:
            when_there(d, lambda d: half_copy(1, d, slot_at(d), place(d), 1).start())
    for d in NEAR_RECVS:
        @pl.when(there(d))
        def _():
            half_came(0, d)
            half_came(1, d)
    for e in range(OWN - 2, OWN + 2):
        join_coeff(e)
    invert()
    restrict_load()

    @pl.when(there(-1))
    def _():
        part_copy(0).wait()
        halo_copy(1).wait()

    assemble(1, 4)
    for n in range(16):
        joined = tot[0, n] + rhs[1, 64 + n]
        tot[0, n] = joined
        tot[1, 64 + n] = joined
    for b in range(4):
        update(0, b)
    add_near(0)
    update(0, 4)

    def step(s, _):
        cycle = s // PERIOD
        live = s < STEPS - 1
        coarse = (lax.rem(s, PERIOD) == NPRE) & live
        deferred = lax.rem(s - 1, PERIOD) != NPRE

        behind = deferred & (s > 1)

        @pl.when(coarse)
        def _():
            coarse_send(cycle)

        expand(0, range(N))
        cross(0)
        mine = plane(0, 4)
        put(0, 4, mine)
        send_face(s, mine)

        @pl.when(there(2))
        def _():
            far_copy(s - 1).wait_send()

        @pl.when(behind)
        def _():
            for b in range(4):
                put(1, b, plane(1, b))
                if b:
                    update(1, b)
            update(1, 4)

        for b in range(4):
            put(0, b, plane(0, b))

        @pl.when(s == 1)
        def _():
            @pl.when(there(-1))
            def _():
                part_copy(1).wait()
                halo_copy(2).wait()

            for b in range(4):
                assemble(1, b)
                put(1, b, [rhs[1, b * 16 + n] for n in range(16)])
                if b:
                    update(1, b)
            update(1, 4)

        expand(1, range(1, N))

        @pl.when(deferred)
        def _():
            add_far(s - 1)
            update(1, 0)

        expand(1, (0,))
        cross(1)
        for n, x in enumerate(plane(1, 4)):
            joined = tot[0, n] + x
            tot[0, n] = joined
            tot[1, 64 + n] = joined

        @pl.when(coarse)
        def _():
            for b in range(4):
                put(1, b, plane(1, b))

        @pl.when(jnp.logical_not(live))
        def _():
            emit(sol, sol_out, False)

        @pl.when(jnp.logical_not(coarse))
        def _():
            for b in range(4):
                update(0, b)

        add_near(s)

        @pl.when(coarse)
        def _():
            add_far(s)
            correct(cycle)
            for b in range(4):
                update(0, b)
                update(1, b + 1)
            update(1, 0)

        update(0, 4)
        return 0

    lax.fori_loop(1, STEPS, step, 0)
    emit(tot, res_out, True)


def per_device(sizes, load, kappa, wet):
    layers, _, width = kappa.shape
    nodes = N * N * N
    tile = (2 * layers, width)
    half = (layers, width)
    sizes = sizes + (layers, width)
    out = jax.ShapeDtypeStruct((nodes, layers, width), F32)
    vmem = pl.BlockSpec(memory_space=pltpu.VMEM)
    fold = width // HALO
    groups = 80 // fold
    messages = 8 + 8 // fold
    dma = pltpu.SemaphoreType.DMA
    solution, residual = pl.pallas_call(
        functools.partial(kernel, sizes),
        out_shape=(out, out),
        in_specs=[pl.BlockSpec(memory_space=pltpu.HBM)] * 3,
        out_specs=(vmem, vmem),
        scratch_shapes=[
            pltpu.VMEM((nodes,) + half, F32),
            pltpu.VMEM(half, F32),
            pltpu.VMEM(half, jnp.int32),
            pltpu.VMEM((groups + 82,) + half, F32),
            pltpu.VMEM((81,) + half, F32),
            pltpu.VMEM((2, groups + 1) + half, F32),
            pltpu.VMEM((2, SPAN + 1) + half, F32),
            pltpu.VMEM((SPAN,) + tile, F32),
            pltpu.VMEM((2, 80) + tile, F32),
            pltpu.VMEM((2, 80) + tile, F32),
            pltpu.VMEM((2, 80) + tile, F32),
            pltpu.VMEM((2, 80) + tile, F32),
            pltpu.VMEM((2, nodes) + tile, F32),
            pltpu.VMEM((2, nodes) + tile, F32),
            pltpu.VMEM((2,) + tile, F32),
            pltpu.VMEM((STEPS, messages) + tile, F32),
            pltpu.VMEM((2, STEPS, messages) + tile, F32),
            pltpu.VMEM((CYCLES, SPAN, 2) + tile, F32),
            pltpu.VMEM((SPAN - 1,) + tile, F32),
            dma((3,)), dma((5,)), dma((5,)), dma((2, SPAN + 1)), dma((2, SPAN + 1)),
            dma((2, STEPS)), dma((2, STEPS)), dma((SPAN + 1,)), dma((CYCLES, SPAN + 1)),
        ],
        compiler_params=pltpu.CompilerParams(collective_id=0, has_side_effects=True, vmem_limit_bytes=16 * 2 ** 20),
    )(*[pltpu.with_memory_space_constraint(x, pltpu.HBM) for x in (
        load.reshape(nodes, layers, width), kappa.reshape(layers, width), wet.reshape(layers, width))])
    return solution.reshape(load.shape), residual.reshape(load.shape)


def solution(mesh):
    sizes = tuple(mesh.shape[name] for name in ("ex", "ey", "lin"))
    field = P(None, None, None, None, ("ey", "lin"), "ex")
    cell = P(None, ("ey", "lin"), "ex")
    return jax.shard_map(
        functools.partial(per_device, sizes), mesh=mesh, in_specs=(field, cell, cell),
        out_specs=(field, field), check_vma=False,
    )
```

```python
import functools
import math

import jax
import jax.numpy as jnp
import numpy as np
from jax import lax
from jax.experimental import pallas as pl
from jax.experimental.pallas import tpu as pltpu
from jax.sharding import PartitionSpec as P

N = 5
CYCLES = 2
NPRE = 2
NPOST = 2
NC = 4
PERIOD = NPRE + NPOST
FINE_RELAX = 0.25
COARSE_RELAX = 0.4
STEPS = CYCLES * PERIOD + 1
REACH = NC + 2
SPAN = 2 * REACH
OWN = REACH
HALO = 32
MESH = pl.DeviceIdType.MESH
F32 = jnp.float32


def node_tables():
    points = np.array([-1.0, -math.sqrt(3.0 / 7.0), 0.0, math.sqrt(3.0 / 7.0), 1.0])
    weights = np.array([0.1, 49.0 / 90.0, 32.0 / 45.0, 49.0 / 90.0, 0.1])
    eye_table = np.eye(points.shape[0])
    spread = points[:, None] - points[None, :] + eye_table
    factors = np.prod(spread, axis=1)
    deriv = factors[:, None] / (factors[None, :] * spread)
    deriv = np.where(eye_table > 0, (np.sum(1.0 / spread, axis=1) - 1.0)[:, None], deriv)
    stiff = deriv.T @ (weights[:, None] * deriv)
    mass = eye_table * weights[:, None]
    interp = np.stack([(1.0 - points) / 2.0, (1.0 + points) / 2.0], axis=1)
    return stiff, weights, interp, interp.T @ stiff @ interp, interp.T @ mass @ interp


S, WEIGHTS, INTERP, SC, WC = node_tables()
ALPHA = (S[0, 0] + S[0, 4]) / 2
BETA = (S[0, 1] + S[0, 3]) / 2
GAMMA = (S[1, 1] + S[1, 3]) / 2
KAPPA = (S[0, 1] - S[0, 3]) / (S[0, 0] - S[0, 4])
ODD = (S[0, 0] - S[0, 4]) / 2
DELTA = (S[1, 1] - S[1, 3]) / (2 * KAPPA ** 2) - ODD
W0, W1, W2 = WEIGHTS[:3]
MU = [W0 / 2, W1 / 2, W2 / 4, W1 / (2 * KAPPA ** 2), W0 / 2]
MUB = [W0, W1 / 2, W2 / 4, W1 / (2 * KAPPA ** 2), W0]
NU = [1.0, 2.0, 4.0, 2 * KAPPA ** 2, 1.0]
SLOPE = KAPPA * (INTERP[1, 0] - INTERP[3, 0])
RISE = ODD * (1 + SLOPE)
NODE = [0, 1, 2, 1, 4]
DIAG = np.diag(S) / WEIGHTS
W3 = WEIGHTS[:, None, None] * WEIGHTS[None, :, None] * WEIGHTS[None, None, :]
K3 = W3 * (DIAG[:, None, None] + DIAG[None, :, None] + DIAG[None, None, :])
CS = (SC[0, 0] - SC[0, 1]) / 2
CE, CO = (WC[0, 0] + WC[0, 1]) / 2, (WC[0, 0] - WC[0, 1]) / 2
C1, C2, C3 = CS * CE * CE, 2 * CS * CO * CE, 3 * CS * CO * CO
SENDS = [d for d in range(-REACH + 1, REACH + 1) if d != 0]
RECVS = [d for d in range(-REACH, REACH) if d != 0]
NEAR_SENDS = [-1, 1, 2]
NEAR_RECVS = [-1, 1, -2]


def st(b, a, c):
    return (b * 4 + a) * 4 + c


def xi(b, i, k):
    return (b * N + i) * N + k


def line_apply(e0, e1, z, o1, o0, scale):
    q0, q1 = e0 - z, e1 - z
    r0 = float(ALPHA * scale) * q0 + float(BETA * scale) * q1
    r1 = float(BETA * scale) * q0 + float(GAMMA * scale) * q1
    s0 = float(ODD * scale) * (o0 + o1)
    return r0, r1, r0 + r1, s0 + float(DELTA * scale) * o1, s0


def plus(x, y):
    if x is None or y is None:
        return x if y is None else y
    return x + y


def minus(x, y):
    if y is None:
        return x
    return -y if x is None else x - y


def kernel(
    sizes, load_ref, kappa_ref, wet_ref, sol_out, res_out,
    load, kappa, wet, part, got_part, got_halo, halves_of, coeffs,
    rhs, sol, tot, sinv, xs, bs, coarse_load, shares, packed, got, cgot, cinv,
    load_sem, x_send, x_recv, k_send, k_recv, f_send, f_recv, c_send, c_recv,
):
    ex_count, ey_count, lin_count, layers, width = sizes
    ex, ey, lin = lax.axis_index("ex"), lax.axis_index("ey"), lax.axis_index("lin")
    rows = ey_count * lin_count
    row = ey * lin_count + lin
    par = lax.rem(lin, 2)
    sgn = 1 - 2 * par
    fold = width // HALO
    groups = 80 // fold
    first = 16 // fold

    sub = lax.broadcasted_iota(jnp.int32, (2 * layers, width), 0)
    lane = lax.broadcasted_iota(jnp.int32, (2 * layers, width), 1)
    layer = sub % layers
    bottom, top = layer == 0, layer == layers - 1
    first_lane, last_lane = lane == 0, lane == width - 1
    near = jnp.where(ex == 0, lane, width - 1 - lane)
    real = (sub < layers) | (near < HALO)
    lower = sub < layers

    def before(x):
        y = pltpu.roll(x, 1, 1)
        return jnp.where(first_lane, pltpu.roll(y, layers, 0), y)

    def after(x):
        y = pltpu.roll(x, width - 1, 1)
        return jnp.where(last_lane, pltpu.roll(y, layers, 0), y)

    def below(low, high):
        return jnp.where(bottom, low, low + pltpu.roll(high, 1, 0))

    def above(low):
        return jnp.where(top, 0.0, pltpu.roll(low, 2 * layers - 1, 0))

    def there(d):
        at = row + sgn * d
        return (at >= 0) & (at < rows)

    def place(d, other=False):
        at = row + sgn * d
        return (1 - ex if other else ex, at // lin_count, at % lin_count)

    def when_there(d, fn):
        @pl.when(there(d))
        def _():
            fn(d)

    def slot_at(d):
        return REACH + (-d if d % 2 == 0 else d)

    def remote(src, dst, send, recv, device):
        return pltpu.make_async_remote_copy(
            src_ref=src, dst_ref=dst, send_sem=send, recv_sem=recv, device_id=device, device_id_type=MESH)

    fetches = [pltpu.make_async_copy(src, dst, load_sem.at[k]) for k, (src, dst) in enumerate(
        ((kappa_ref, kappa), (wet_ref, wet), (load_ref, load)))]
    for fetch in fetches:
        fetch.start()
    halves_of[...] = jnp.zeros_like(halves_of)
    cgot[...] = jnp.zeros_like(cgot)

    @pl.when(jnp.logical_not(there(-1)))
    def _():
        got_part[...] = jnp.zeros_like(got_part)
        got_halo[1] = jnp.zeros_like(got_halo[1])

    def greet(device):
        pl.semaphore_signal(pltpu.get_barrier_semaphore(), inc=1, device_id=device, device_id_type=MESH)

    greet((1 - ex, ey, lin))
    expected = jnp.int32(1)
    for d in range(1, REACH + 1):
        for e in (-d, d):
            @pl.when(there(e))
            def _():
                greet(place(e))
                if d <= 2:
                    greet(place(e, True))
            expected = expected + jnp.where(there(e), 2 if d <= 2 else 1, 0)

    fetches[0].wait()
    fetches[1].wait()
    halves_of[0, OWN] = kappa[...] * jnp.where(wet[...] == 1, F32(1.0), F32(0.05))

    def raw(a, b, c):
        return (a * N + b + par * (N - 1 - 2 * b)) * N + c

    def to_dual(f):
        return [(f[1] + f[3]) * 0.5, f[2] * 0.5, (f[1] - f[3]) * float(0.5 / KAPPA)]

    def load_plane(b):
        nothing = jnp.zeros((layers, width), F32)
        tiles = [jnp.concatenate([load[raw(n // N, b, n % N)], nothing], axis=0) for n in range(N * N)]
        lines = []
        for a in range(N):
            f = tiles[a * N:a * N + N]
            lines.append([f[0] + before(f[4])] + to_dual(f))
        columns = []
        for c in range(4):
            f = [lines[a][c] for a in range(N)]
            columns.append([below(f[0], f[4])] + to_dual(f))
        return [columns[c][a] for a in range(4) for c in range(4)]

    fetches[2].wait()
    for b in (0, 4, 2, 1, 3):
        for n, x in enumerate(load_plane(b)):
            if b == 3:
                other = rhs[0, 16 + n]
                rhs[0, 48 + n] = (other - x) * float(0.5 / KAPPA)
                rhs[0, 16 + n] = (other + x) * 0.5
            else:
                rhs[0, b * 16 + n] = x * 0.5 if b == 2 else x
    def at_group(g):
        return g if g < first else g + 1

    source = jnp.where(ex == 0, fold - 1, 0)
    turn = (lane // HALO + fold - source) % fold
    for g in range(groups):
        mixed = None
        for j in range(fold):
            x = rhs[0, g * fold + j]
            part[groups + 2 + g * fold + j] = x[0:layers]
            mixed = x if j == 0 else jnp.where(turn == j, pltpu.roll(x, HALO * j, 1), mixed)
        part[at_group(g)] = mixed[0:layers]
    mixed = None
    for j in range(20):
        x = rhs[0, 4 * j]
        mixed = x if j == 0 else jnp.where(lane == j, pltpu.roll(x, j, 1), mixed)
    for at in (first, groups + 1):
        part[at] = pltpu.roll(mixed, layers, 0)[0:layers]

    pl.semaphore_wait(pltpu.get_barrier_semaphore(), expected)

    def half_copy(h, d, slot, device, source=0):
        return remote(halves_of.at[source, OWN], halves_of.at[h, slot], k_send.at[h, REACH + d], k_recv.at[h, slot],
                      device)

    def half_sent(h, d):
        half_copy(h, d, OWN, place(d), h).wait_send()

    def half_came(h, d):
        half_copy(h, d, REACH + d, place(d), h).wait_recv()

    half_copy(1, 0, OWN, place(0, True)).start()
    for d in NEAR_SENDS:
        @pl.when(there(d))
        def _():
            half_copy(0, d, slot_at(d), place(d)).start()
            half_copy(1, d, slot_at(d), place(d, True)).start()

    def halo_copy(k):
        at, size = ((0, groups + 1), (0, first + 1), (first + 1, groups - first))[k]
        return remote(part.at[at:at + size], got_halo.at[min(k, 1), at:at + size], x_send.at[k], x_recv.at[k],
                      place(-1 if k else 0, True))

    def part_copy(k):
        at, size = ((0, 17), (17, 64))[k]
        return remote(part.at[groups + 1 + at:groups + 1 + at + size], got_part.at[at:at + size], x_send.at[3 + k],
                      x_recv.at[3 + k], place(-1))

    halo_copy(0).start()

    @pl.when(there(-1))
    def _():
        halo_copy(1).start()
        part_copy(0).start()
        part_copy(1).start()
        halo_copy(2).start()

    for d in SENDS:
        if d not in NEAR_SENDS:
            when_there(d, lambda d: half_copy(0, d, slot_at(d), place(d)).start())

    outer = (sub >= layers) & (near < HALO)
    entering = first_lane & ((sub >= layers) | (ex == 1))

    def assemble(r, b):
        source_b = b if r == 0 or 0 < b < 4 else 4 - b
        nothing = jnp.zeros((layers, width), F32)
        spill = jnp.concatenate([got_halo[r, first], got_part[0] if r else nothing], axis=0)
        for a in range(4):
            for c in range(4):
                n, m = st(b, a, c), st(source_b, a, c)
                h = got_halo[r, at_group(m // fold)]
                h = jnp.concatenate([h, h], axis=0)
                if m % fold:
                    h = pltpu.roll(h, width - HALO * (m % fold), 1)
                h = jnp.where(outer, h, 0.0)
                if r == 0:
                    x = rhs[0, n] + h
                else:
                    p = got_part[1 + m]
                    x = jnp.where(lower, jnp.concatenate([p, p], axis=0), h)
                if c == 0:
                    j = m // 4
                    x = x + jnp.where(entering, pltpu.roll(spill, width - j, 1) if j else spill, 0.0)
                rhs[r, n] = -x if r == 1 and b == 3 else x

    block = lax.rem(lane + jnp.where(ex == 0, 0, HALO - 1), width) // HALO

    def swap(x):
        return pltpu.roll(x, layers, 0)

    def pack(s, x):
        for p in range(8):
            packed[s, p] = jnp.where(lower, x[2 * p], swap(x[2 * p + 1]))
        for p in range(8 // fold):
            halves = []
            for h in range(2):
                group = x[(2 * p + h) * fold:(2 * p + h + 1) * fold]
                mixed = group[0]
                for j in range(1, fold):
                    mixed = jnp.where(block == j, pltpu.roll(group[j], HALO * j, 1), mixed)
                halves.append(mixed)
            packed[s, 8 + p] = jnp.where(lower, swap(halves[0]), halves[1])

    def unpack(kind, s):
        x = []
        for p in range(8 // fold):
            tile = got[kind, s, 8 + p]
            for half in (swap(tile), tile):
                for j in range(fold):
                    other = half if j == 0 else pltpu.roll(half, width - HALO * j, 1)
                    n = len(x)
                    mine = got[kind, s, n // 2]
                    mine = mine if n % 2 == 0 else swap(mine)
                    x.append(jnp.where(lower, mine, jnp.where(block == 0, other, 0.0)))
        return x

    def near_copy(s):
        return remote(packed.at[s], got.at[0, s], f_send.at[0, s], f_recv.at[0, s], place(1))

    def far_copy(s):
        return remote(packed.at[s], got.at[1, s], f_send.at[1, s], f_recv.at[1, s], place(2))

    def send_face(s, values):
        pack(s, values)
        near_copy(s).start()

        @pl.when(there(2) & (s < STEPS - 1))
        def _():
            far_copy(s).start()

    def add_near(s):
        near_copy(s).wait()
        for n, x in enumerate(unpack(0, s)):
            tot[0, 64 + n] = tot[0, 64 + n] + x

    def add_far(s):
        @pl.when(there(-2))
        def _():
            far_copy(s).wait_recv()
            for n, x in enumerate(unpack(1, s)):
                tot[1, n] = tot[1, n] + x

    def expand(r, planes):
        for b in planes:
            w = []
            for a in range(4):
                v = [sol[r, st(b, a, c)] for c in range(4)]
                up = after(v[0])
                w.append([v[0] + up, v[1], v[2], v[3], v[0] - up])
            for k in range(N):
                up = above(w[0][k])
                xs[r, xi(b, 0, k)] = w[0][k] + up
                xs[r, xi(b, 4, k)] = w[0][k] - up
                for a in range(1, 4):
                    xs[r, xi(b, a, k)] = w[a][k]

    def cross(r):
        for i in range(N):
            for k in range(N):
                v = [xs[r, xi(b, i, k)] for b in range(N)]
                r0, r1, rz, s1, s0 = line_apply(v[0] + v[4], v[1], v[2], v[3], v[0] - v[4], MU[i] * MU[k])
                for b, x in enumerate((r0 + s0, r1, rz, s1)):
                    bs[r, xi(b, i, k)] = x

    def gather(y):
        g = []
        for k in range(N):
            low, high = plus(y[0][k], y[4][k]), minus(y[0][k], y[4][k])
            g.append([None if low is None else below(low, high)] + [y[i][k] for i in range(1, 4)])
        h = []
        for a in range(4):
            low, high = plus(g[0][a], g[4][a]), minus(g[0][a], g[4][a])
            h.append([None if low is None else low + before(high)] + [g[k][a] for k in range(1, 4)])
        return h

    def top_term(r, i, k):
        v = [xs[r, xi(b, i, k)] for b in range(N)]
        scale = MU[i] * MU[k]
        r0 = float(ALPHA * scale) * (v[0] + v[4] - v[2]) + float(BETA * scale) * (v[1] - v[2])
        return r0 - float(ODD * scale) * ((v[0] - v[4]) + v[3])

    def plane(r, b):
        coeff = coeffs[OWN - r]
        x = [[xs[r, xi(b, i, k)] for k in range(N)] for i in range(N)]
        along_c = [line_apply(*x[i], MUB[b] * MU[i]) for i in range(N)]
        along_a = [line_apply(*[x[i][k] for i in range(N)], MUB[b] * MU[k]) for k in range(N)]
        y = []
        for i in range(N):
            line = []
            for k in range(N):
                along_b = top_term(r, i, k) if b == 4 else bs[r, xi(b, i, k)]
                terms = sorted(((b == 2, along_b), (k == 2, along_c[i][k]), (i == 2, along_a[k][i])),
                               key=lambda t: t[0])
                total = -terms[0][1] if terms[0][0] else terms[0][1]
                for negative, term in terms[1:]:
                    total = total - term if negative else total + term
                line.append(coeff * total)
            y.append(line)
        h = gather(y)
        return [rhs[r, st(b, a, c)] - h[a][c] for a in range(4) for c in range(4)]

    def put(r, b, values):
        for n, x in enumerate(values):
            tot[r, b * 16 + n] = x

    def update(r, b):
        for n in range(b * 16, b * 16 + 16):
            sol[r, n] = sol[r, n] + sinv[r, n] * tot[r, n]

    def inverted(x):
        return jnp.where(x > 0.0, 1.0 / jnp.where(x > 0.0, x, 1.0), 0.0)

    def invert():
        for r in range(2):
            here = coeffs[OWN - r]
            two = here + before(here)
            for k, x in enumerate((here, two, below(here, here), below(two, two))):
                shares[r, k] = x
            for bl, x in (((1, 2, 3), here), ((0,), here + coeffs[OWN - r - 1]), ((4,), here + coeffs[OWN - r + 1])):
                xc = x + before(x)
                tiles = [[inverted(below(xc, xc)), inverted(below(x, x))], [inverted(xc), inverted(x)]]
                for b in bl:
                    for a in range(4):
                        for c in range(4):
                            factor = FINE_RELAX * NU[a] * NU[b] * NU[c] / K3[NODE[a], NODE[b], NODE[c]]
                            sinv[r, st(b, a, c)] = float(factor) * tiles[min(a, 1)][min(c, 1)]

    def shift_top(r, at, n):
        delta = sinv[r, n] * tot[r, n]
        sol[r, n] = sol[r, n] + delta
        a, c = n // 4, n % 4
        factor = S[4, 0] * (MU[a] if a else W0) * (MU[c] if c else W0)
        tot[r, at + n] = tot[r, at + n] - float(factor) * shares[r, (0 if a else 2) + (0 if c else 1)] * delta

    def join_coeff(e):
        coeffs[e] = jnp.where(real, jnp.concatenate([halves_of[0, e], halves_of[1, e]], axis=0), 0.0)

    def coarse_invert():
        for d in SENDS:
            @pl.when(there(d))
            def _():
                half_sent(0, d)
                half_sent(1, d)
        for d in RECVS:
            if d not in NEAR_RECVS:
                @pl.when(there(d))
                def _():
                    half_came(0, d)
                    half_came(1, d)
        for e in range(SPAN):
            if abs(e - OWN + 0.5) > 2:
                join_coeff(e)
        corner = 3.0 * SC[0, 0] * WC[0, 0] ** 2
        for i in range(SPAN - 1):
            pair = coeffs[i] + coeffs[i + 1]
            pair = pair + before(pair)
            cinv[i] = float(COARSE_RELAX / corner) * inverted(below(pair, pair))

    def halves(v):
        even, odd = v[1] + v[2], float(SLOPE) * v[3]
        return even + odd, even - odd

    def restrict_load():
        q = [[], []]
        for n in range(16):
            v = [rhs[0, b * 16 + n] for b in range(N)]
            low, high = halves(v)
            q[0].append(v[0] + low)
            q[1].append(v[4] + high)
        for j in range(2):
            lines = []
            for a in range(4):
                v = q[j][a * 4:a * 4 + 4]
                low, high = halves(v)
                lines.append((v[0] + low) + before(high))
            low, high = halves(lines)
            coarse_load[j] = below(lines[0] + low, high)

    def moments(first, mids, second):
        even, odd = first + second, first - second
        return (
            float(RISE) * odd,
            float(W0 / 2) * even + float(W1 / 2) * mids[0] + float(W2 / 4) * mids[1],
            float(W0 / 2) * odd + float(W1 * SLOPE / (2 * KAPPA ** 2)) * mids[2],
        )

    def coarse_send(cycle):
        along_b = []
        for n in range(16):
            v = [sol[0, b * 16 + n] for b in range(N)]
            along_b.append(moments(v[0], v[1:4], v[4]))
        mixed = [[], [], [], []]
        plain = [[], [], [], []]
        for c in range(4):
            along_a = []
            for kind in range(3):
                v = [along_b[a * 4 + c][kind] for a in range(4)]
                along_a.append(moments(v[0], v[1:4], above(v[0])))
            rise, even, odd = along_a
            mixed[1].append(rise[1])
            mixed[2].append(even[0])
            mixed[3].append(rise[2] + odd[0])
            for m, x in enumerate((even[1], odd[1], even[2], odd[2])):
                plain[m].append(x)
        coeff = coeffs[OWN]
        y = [None] * 4
        for m in range(4):
            steep = float(RISE) * (plain[m][0] - after(plain[m][0]))
            if m == 0:
                y[m] = (None, coeff * steep)
            else:
                v = mixed[m]
                part = moments(v[0], v[1:4], after(v[0]))
                y[m] = (coeff * part[1], coeff * (part[2] + steep))
        for j in range(2):
            g = []
            for k in range(2):
                r = []
                for a in range(2):
                    one, two = y[2 * a][k], y[2 * a + 1][k]
                    r.append(plus(one, two) if j == 0 else minus(one, two))
                g.append(below(r[0] + r[1], r[0] - r[1]))
            cgot[cycle, OWN, j] = coarse_load[j] - ((g[0] + g[1]) + before(g[0] - g[1]))
        for d in SENDS:
            when_there(d, lambda d: remote(
                cgot.at[cycle, OWN], cgot.at[cycle, slot_at(d)], c_send.at[REACH + d], c_recv.at[cycle, slot_at(d)],
                place(d)).start())

    def correct(cycle):
        @pl.when(cycle == 0)
        def _():
            coarse_invert()

        for d in SENDS:
            when_there(d, lambda d: remote(
                cgot.at[cycle, OWN], cgot.at[cycle, OWN], c_send.at[REACH + d], c_recv.at[cycle, OWN],
                place(d)).wait_send())
        for d in RECVS:
            when_there(d, lambda d: remote(
                cgot.at[cycle, OWN], cgot.at[cycle, REACH + d], c_send.at[OWN], c_recv.at[cycle, REACH + d],
                place(d)).wait_recv())

        def q(e, j):
            return cgot[cycle, e, j if (e - OWN) % 2 == 0 else 1 - j]

        lines = SPAN - 1
        rc = [q(i, 1) + q(i + 1, 0) for i in range(lines)]
        x = [cinv[i] * rc[i] for i in range(lines)]

        def modes(v):
            up = after(v)
            parts = []
            for k in (v + up, v - up):
                high = above(k)
                parts.append((k + high, k - high))
            return [[parts[k][i] for k in range(2)] for i in range(2)]

        begin, end = 0, lines - 1
        for sweep in range(NC - 1):
            m = {i: modes(x[i]) for i in range(begin, end + 1)}
            sides = {}
            for e in range(begin + 1, end + 1):
                coeff = coeffs[e]
                factor = [float(C1) * coeff, float(C2) * coeff, float(C3) * coeff]
                low, high = m[e - 1], m[e]
                part = []
                for i in range(2):
                    pair = []
                    for k in range(2):
                        odd = factor[i + k] * (low[i][k] - high[i][k])
                        if i + k == 0:
                            pair.append((odd, -odd))
                        else:
                            even = factor[i + k - 1] * (low[i][k] + high[i][k])
                            pair.append((even + odd, even - odd))
                    part.append(pair)
                sides[e] = part
            begin, end = begin + 1, end - 1
            new = list(x)
            for i in range(begin, end + 1):
                y = [[sides[i + 1][a][k][0] + sides[i][a][k][1] for k in range(2)] for a in range(2)]
                g = [below(y[0][k] + y[1][k], y[0][k] - y[1][k]) for k in range(2)]
                image = (g[0] + g[1]) + before(g[0] - g[1])
                new[i] = x[i] + cinv[i] * (rc[i] - image)
            x = new

        base = OWN - 3
        m = {i: modes(x[i]) for i in range(base, base + 5)}
        kind = [0, 0, 0, 1, 1]
        grow = [1.0, 1.0, 1.0, SLOPE, 1.0]

        def ends(centre, weight, tilt):
            y = [[None] * N for _ in range(N)]
            for i in range(N):
                for k in range(N):
                    value = None
                    if centre is not None:
                        value = float(MU[i] * MU[k] * grow[i] * grow[k]) * centre[kind[i]][kind[k]]
                    if i == 4:
                        value = plus(value, float(RISE * weight * MU[k] * grow[k]) * tilt[1][kind[k]])
                    if k == 4:
                        value = plus(value, float(RISE * weight * MU[i] * grow[i]) * tilt[kind[i]][1])
                    y[i][k] = value
            return gather(y)

        def face_image(i):
            up, down = coeffs[i + 1], coeffs[i]
            both = up + down
            centre = [[float(RISE) * (up * (m[i][a][k] - m[i + 1][a][k]) - down * (m[i - 1][a][k] - m[i][a][k]))
                       for k in range(2)] for a in range(2)]
            tilt = [[None if a + k == 0 else both * m[i][a][k] for k in range(2)] for a in range(2)]
            h = ends(centre, W0, tilt)
            return [h[a][c] for a in range(4) for c in range(4)]

        for i, targets in ((OWN - 2, ((1, 0),)), (OWN - 1, ((1, 64), (0, 0))), (OWN, ((0, 64),))):
            values = face_image(i)
            for r, at in targets:
                for n, value in enumerate(values):
                    tot[r, at + n] = tot[r, at + n] - value
        scale = [1.0, 1.0, 1.0, SLOPE]

        def nodal(i):
            v = x[i]
            up = after(v)
            high = above(v)
            tiles = [[v, v + up, v - up], [v + high, m[i][0][0], m[i][0][1]], [v - high, m[i][1][0], m[i][1][1]]]
            pick = [0, 1, 1, 2]
            made = {}
            out = []
            for a in range(4):
                for c in range(4):
                    key = (pick[a], pick[c])
                    if key not in made:
                        factor = float(scale[a] * scale[c])
                        made[key] = tiles[key[0]][key[1]] if factor == 1.0 else factor * tiles[key[0]][key[1]]
                    out.append((key, made[key]))
            return out

        at_line = {i: nodal(i) for i in (OWN - 2, OWN - 1, OWN)}
        for r in range(2):
            low, high = OWN - 1 - r, OWN - r
            coeff = coeffs[OWN - r]
            for kindb in range(2):
                diff = [[None if a + k == 0 else
                         coeff * (m[low][a][k] - m[high][a][k] if kindb else m[low][a][k] + m[high][a][k])
                         for k in range(2)] for a in range(2)]
                h = ends(None, 1.0, diff)
                for b in ((3,) if kindb else (1, 2)):
                    factor = float(MUB[b] * (SLOPE if kindb else 1.0))
                    for a in range(4):
                        for c in range(4):
                            if h[a][c] is not None:
                                tot[r, st(b, a, c)] = tot[r, st(b, a, c)] - factor * h[a][c]
                made = {}
                for n in range(16):
                    key, lower_value = at_line[low][n]
                    upper_value = at_line[high][n][1]
                    if key not in made:
                        made[key] = (float(SLOPE) * (lower_value - upper_value) if kindb
                                     else lower_value + upper_value)
                    for b in ((3,) if kindb else (1, 2)):
                        sol[r, b * 16 + n] = sol[r, b * 16 + n] + made[key]
            for n in range(16):
                sol[r, n] = sol[r, n] + at_line[low][n][1]
                sol[r, 64 + n] = sol[r, 64 + n] + at_line[high][n][1]

    def emit(field, out_ref, dual):
        def split(mid, double, odd):
            if dual:
                odd = float(KAPPA) * odd
                return mid + odd, 2.0 * double, mid - odd
            even, odd = 0.5 * mid, float(0.5 / KAPPA) * odd
            return even + odd, 0.5 * double, even - odd

        def one(b, values):
            lines = []
            for a in range(4):
                v = values[a * 4:a * 4 + 4]
                lines.append([v[0], *split(*v[1:]), after(v[0])])
            for c in range(N):
                v = [lines[a][c] for a in range(4)]
                for a, tile in enumerate([v[0], *split(*v[1:]), above(v[0])]):
                    out_ref[raw(a, b, c)] = tile[0:layers]

        for b in (0, 4):
            one(b, [field[0, b * 16 + n] for n in range(16)])
        mids = [split(field[0, 16 + n], field[0, 32 + n], field[0, 48 + n]) for n in range(16)]
        for b in range(1, 4):
            one(b, [v[b - 1] for v in mids])

    halo_copy(0).wait()
    for b in (4, 0, 1, 2, 3):
        assemble(0, b)
        put(0, b, [rhs[0, b * 16 + n] for n in range(16)])
        if b == 4:
            send_face(0, [tot[0, 64 + n] for n in range(16)])
    sol[...] = jnp.zeros_like(sol)
    half_copy(1, 0, OWN, place(0, True)).wait()
    for d in SENDS:
        if d not in NEAR_SENDS:
            when_there(d, lambda d: half_copy(1, d, slot_at(d), place(d), 1).start())
    for d in NEAR_RECVS:
        @pl.when(there(d))
        def _():
            half_came(0, d)
            half_came(1, d)
    for e in range(OWN - 2, OWN + 2):
        join_coeff(e)
    invert()
    restrict_load()

    @pl.when(there(-1))
    def _():
        part_copy(0).wait()
        halo_copy(1).wait()

    assemble(1, 4)
    for n in range(16):
        joined = tot[0, n] + rhs[1, 64 + n]
        tot[0, n] = joined
        tot[1, 64 + n] = joined
    for b in range(4):
        update(0, b)
    add_near(0)
    update(0, 4)

    def ready_face(s):
        expand(0, range(N))
        put(0, 4, plane(0, 4))

    def next_face(s):
        send_face(s, [tot[0, 64 + n] for n in range(16)])

    ready_face(1)
    next_face(1)

    def step(s, _):
        cycle = s // PERIOD
        live = s < STEPS - 1
        coarse = (lax.rem(s, PERIOD) == NPRE) & live
        deferred = lax.rem(s - 1, PERIOD) != NPRE
        behind = deferred & (s > 1)
        plain = jnp.logical_not(coarse) & live

        expand(0, (0,))
        cross(0)
        for b in range(4):
            put(0, b, plane(0, b))

        @pl.when(there(2))
        def _():
            far_copy(s - 1).wait_send()

        @pl.when(behind)
        def _():
            expand(1, (0,))
            cross(1)
            for b in range(4):
                put(1, b, plane(1, b))
                if b:
                    update(1, b)
            update(1, 4)

        @pl.when(s == 1)
        def _():
            @pl.when(there(-1))
            def _():
                part_copy(1).wait()
                halo_copy(2).wait()

            for b in range(4):
                assemble(1, b)
                put(1, b, [rhs[1, b * 16 + n] for n in range(16)])
                if b:
                    update(1, b)
            update(1, 4)

        @pl.when(coarse)
        def _():
            add_far(s - 1)
            update(1, 0)

        expand(1, range(N))
        put(1, 4, plane(1, 4))

        @pl.when(coarse)
        def _():
            cross(1)
            for b in range(4):
                put(1, b, plane(1, b))

        @pl.when(jnp.logical_not(live))
        def _():
            emit(sol, sol_out, False)

        @pl.when(plain)
        def _():
            for b in range(1, 4):
                update(0, b)

        add_near(s)

        @pl.when(plain)
        def _():
            update(0, 4)
            ready_face(s + 1)

        @pl.when(deferred & jnp.logical_not(coarse))
        def _():
            add_far(s - 1)
            for n in range(16):
                shift_top(1, 64, n)

        for n in range(16):
            joined = tot[0, n] + tot[1, 64 + n]
            tot[0, n] = joined
            tot[1, 64 + n] = joined

        @pl.when(plain)
        def _():
            for n in range(16):
                shift_top(0, 64, n)

        @pl.when(coarse)
        def _():
            add_far(s)
            correct(cycle)
            for b in range(N):
                update(0, b)
                update(1, b)
            ready_face(s + 1)

        @pl.when((lax.rem(s + 1, PERIOD) == NPRE) & (s + 1 < STEPS - 1))
        def _():
            coarse_send((s + 1) // PERIOD)

        @pl.when(live)
        def _():
            next_face(s + 1)

        return 0

    lax.fori_loop(1, STEPS, step, 0)
    emit(tot, res_out, True)


def hand_over(sol_ref, res_ref, sol_out, res_out, sems):
    copies = [pltpu.make_async_copy(src, dst, sems.at[k]) for k, (src, dst) in enumerate(
        ((sol_ref, sol_out), (res_ref, res_out)))]
    for copy in copies:
        copy.start()
    for copy in copies:
        copy.wait()


def per_device(sizes, load, kappa, wet):
    layers, _, width = kappa.shape
    nodes = N * N * N
    tile = (2 * layers, width)
    half = (layers, width)
    sizes = sizes + (layers, width)
    out = jax.ShapeDtypeStruct((nodes, layers, width), F32)
    vmem = pl.BlockSpec(memory_space=pltpu.VMEM)
    fold = width // HALO
    groups = 80 // fold
    messages = 8 + 8 // fold
    dma = pltpu.SemaphoreType.DMA
    solution, residual = pl.pallas_call(
        functools.partial(kernel, sizes),
        out_shape=(out, out),
        in_specs=[pl.BlockSpec(memory_space=pltpu.HBM)] * 3,
        out_specs=(vmem, vmem),
        scratch_shapes=[
            pltpu.VMEM((nodes,) + half, F32),
            pltpu.VMEM(half, F32),
            pltpu.VMEM(half, jnp.int32),
            pltpu.VMEM((groups + 82,) + half, F32),
            pltpu.VMEM((81,) + half, F32),
            pltpu.VMEM((2, groups + 1) + half, F32),
            pltpu.VMEM((2, SPAN + 1) + half, F32),
            pltpu.VMEM((SPAN,) + tile, F32),
            pltpu.VMEM((2, 80) + tile, F32),
            pltpu.VMEM((2, 80) + tile, F32),
            pltpu.VMEM((2, 80) + tile, F32),
            pltpu.VMEM((2, 80) + tile, F32),
            pltpu.VMEM((2, nodes) + tile, F32),
            pltpu.VMEM((2, nodes) + tile, F32),
            pltpu.VMEM((2,) + tile, F32),
            pltpu.VMEM((2, 4) + tile, F32),
            pltpu.VMEM((STEPS, messages) + tile, F32),
            pltpu.VMEM((2, STEPS, messages) + tile, F32),
            pltpu.VMEM((CYCLES, SPAN, 2) + tile, F32),
            pltpu.VMEM((SPAN - 1,) + tile, F32),
            dma((3,)), dma((5,)), dma((5,)), dma((2, SPAN + 1)), dma((2, SPAN + 1)),
            dma((2, STEPS)), dma((2, STEPS)), dma((SPAN + 1,)), dma((CYCLES, SPAN + 1)),
        ],
        compiler_params=pltpu.CompilerParams(collective_id=0, has_side_effects=True, vmem_limit_bytes=16 * 2 ** 20),
    )(*[pltpu.with_memory_space_constraint(x, pltpu.HBM) for x in (
        load.reshape(nodes, layers, width), kappa.reshape(layers, width), wet.reshape(layers, width))])
    place = pl.BlockSpec(memory_space=pl.ANY)
    solution, residual = pl.pallas_call(
        hand_over, out_shape=(out, out), in_specs=[place] * 2, out_specs=(place, place),
        scratch_shapes=[dma((2,))],
        compiler_params=pltpu.CompilerParams(vmem_limit_bytes=2 ** 20),
    )(solution, residual)
    return solution.reshape(load.shape), residual.reshape(load.shape)


def solution(mesh):
    sizes = tuple(mesh.shape[name] for name in ("ex", "ey", "lin"))
    field = P(None, None, None, None, ("ey", "lin"), "ex")
    cell = P(None, ("ey", "lin"), "ex")
    return jax.shard_map(
        functools.partial(per_device, sizes), mesh=mesh, in_specs=(field, cell, cell),
        out_specs=(field, field), check_vma=False,
    )
```

```python
import functools
import math

import jax
import jax.numpy as jnp
import numpy as np
from jax import lax
from jax.experimental import pallas as pl
from jax.experimental.pallas import tpu as pltpu
from jax.sharding import PartitionSpec as P

N = 5
CYCLES = 2
NPRE = 2
NPOST = 2
NC = 4
PERIOD = NPRE + NPOST
FINE_RELAX = 0.25
COARSE_RELAX = 0.4
STEPS = CYCLES * PERIOD + 1
REACH = NC + 2
SPAN = 2 * REACH
OWN = REACH
HALO = 32
MESH = pl.DeviceIdType.MESH
F32 = jnp.float32


def node_tables():
    points = np.array([-1.0, -math.sqrt(3.0 / 7.0), 0.0, math.sqrt(3.0 / 7.0), 1.0])
    weights = np.array([0.1, 49.0 / 90.0, 32.0 / 45.0, 49.0 / 90.0, 0.1])
    eye_table = np.eye(points.shape[0])
    spread = points[:, None] - points[None, :] + eye_table
    factors = np.prod(spread, axis=1)
    deriv = factors[:, None] / (factors[None, :] * spread)
    deriv = np.where(eye_table > 0, (np.sum(1.0 / spread, axis=1) - 1.0)[:, None], deriv)
    stiff = deriv.T @ (weights[:, None] * deriv)
    mass = eye_table * weights[:, None]
    interp = np.stack([(1.0 - points) / 2.0, (1.0 + points) / 2.0], axis=1)
    return stiff, weights, interp, interp.T @ stiff @ interp, interp.T @ mass @ interp


S, WEIGHTS, INTERP, SC, WC = node_tables()
ALPHA = (S[0, 0] + S[0, 4]) / 2
BETA = (S[0, 1] + S[0, 3]) / 2
GAMMA = (S[1, 1] + S[1, 3]) / 2
KAPPA = (S[0, 1] - S[0, 3]) / (S[0, 0] - S[0, 4])
ODD = (S[0, 0] - S[0, 4]) / 2
DELTA = (S[1, 1] - S[1, 3]) / (2 * KAPPA ** 2) - ODD
W0, W1, W2 = WEIGHTS[:3]
MU = [W0 / 2, W1 / 2, W2 / 4, W1 / (2 * KAPPA ** 2), W0 / 2]
MUB = [W0, W1 / 2, W2 / 4, W1 / (2 * KAPPA ** 2), W0]
NU = [1.0, 2.0, 4.0, 2 * KAPPA ** 2, 1.0]
SLOPE = KAPPA * (INTERP[1, 0] - INTERP[3, 0])
RISE = ODD * (1 + SLOPE)
NODE = [0, 1, 2, 1, 4]
DIAG = np.diag(S) / WEIGHTS
W3 = WEIGHTS[:, None, None] * WEIGHTS[None, :, None] * WEIGHTS[None, None, :]
K3 = W3 * (DIAG[:, None, None] + DIAG[None, :, None] + DIAG[None, None, :])
CS = (SC[0, 0] - SC[0, 1]) / 2
CE, CO = (WC[0, 0] + WC[0, 1]) / 2, (WC[0, 0] - WC[0, 1]) / 2
C1, C2, C3 = CS * CE * CE, 2 * CS * CO * CE, 3 * CS * CO * CO
SENDS = [d for d in range(-REACH + 1, REACH + 1) if d != 0]
RECVS = [d for d in range(-REACH, REACH) if d != 0]
NEAR_SENDS = [-1, 1, 2]
NEAR_RECVS = [-1, 1, -2]


def st(b, a, c):
    return (b * 4 + a) * 4 + c


def xi(b, i, k):
    return (b * N + i) * N + k


def line_apply(e0, e1, z, o1, o0, scale):
    q0, q1 = e0 - z, e1 - z
    r0 = float(ALPHA * scale) * q0 + float(BETA * scale) * q1
    r1 = float(BETA * scale) * q0 + float(GAMMA * scale) * q1
    s0 = float(ODD * scale) * (o0 + o1)
    return r0, r1, r0 + r1, s0 + float(DELTA * scale) * o1, s0


def plus(x, y):
    if x is None or y is None:
        return x if y is None else y
    return x + y


def minus(x, y):
    if y is None:
        return x
    return -y if x is None else x - y


def kernel(
    sizes, load_ref, kappa_ref, wet_ref, sol_out, res_out,
    load, kappa, wet, part, got_part, got_halo, halves_of, coeffs,
    rhs, sol, tot, sinv, xs, bs, coarse_load, shares, packed, got, cgot, cinv,
    load_sem, x_send, x_recv, k_send, k_recv, f_send, f_recv, c_send, c_recv,
):
    ex_count, ey_count, lin_count, layers, width = sizes
    ex, ey, lin = lax.axis_index("ex"), lax.axis_index("ey"), lax.axis_index("lin")
    rows = ey_count * lin_count
    row = ey * lin_count + lin
    par = lax.rem(lin, 2)
    sgn = 1 - 2 * par
    fold = width // HALO
    groups = 80 // fold
    first = 16 // fold

    sub = lax.broadcasted_iota(jnp.int32, (2 * layers, width), 0)
    lane = lax.broadcasted_iota(jnp.int32, (2 * layers, width), 1)
    layer = sub % layers
    bottom, top = layer == 0, layer == layers - 1
    first_lane, last_lane = lane == 0, lane == width - 1
    near = jnp.where(ex == 0, lane, width - 1 - lane)
    real = (sub < layers) | (near < HALO)
    lower = sub < layers

    def before(x):
        y = pltpu.roll(x, 1, 1)
        return jnp.where(first_lane, pltpu.roll(y, layers, 0), y)

    def after(x):
        y = pltpu.roll(x, width - 1, 1)
        return jnp.where(last_lane, pltpu.roll(y, layers, 0), y)

    def below(low, high):
        return jnp.where(bottom, low, low + pltpu.roll(high, 1, 0))

    def above(low):
        return jnp.where(top, 0.0, pltpu.roll(low, 2 * layers - 1, 0))

    def there(d):
        at = row + sgn * d
        return (at >= 0) & (at < rows)

    def place(d, other=False):
        at = row + sgn * d
        return (1 - ex if other else ex, at // lin_count, at % lin_count)

    def when_there(d, fn):
        @pl.when(there(d))
        def _():
            fn(d)

    def slot_at(d):
        return REACH + (-d if d % 2 == 0 else d)

    def remote(src, dst, send, recv, device):
        return pltpu.make_async_remote_copy(
            src_ref=src, dst_ref=dst, send_sem=send, recv_sem=recv, device_id=device, device_id_type=MESH)

    fetches = [pltpu.make_async_copy(src, dst, load_sem.at[k]) for k, (src, dst) in enumerate(
        ((kappa_ref, kappa), (wet_ref, wet), (load_ref, load)))]
    for fetch in fetches:
        fetch.start()
    halves_of[...] = jnp.zeros_like(halves_of)
    cgot[...] = jnp.zeros_like(cgot)

    @pl.when(jnp.logical_not(there(-1)))
    def _():
        got_part[...] = jnp.zeros_like(got_part)
        got_halo[1] = jnp.zeros_like(got_halo[1])

    def greet(device):
        pl.semaphore_signal(pltpu.get_barrier_semaphore(), inc=1, device_id=device, device_id_type=MESH)

    greet((1 - ex, ey, lin))
    expected = jnp.int32(1)
    for d in range(1, REACH + 1):
        for e in (-d, d):
            @pl.when(there(e))
            def _():
                greet(place(e))
                if d <= 2:
                    greet(place(e, True))
            expected = expected + jnp.where(there(e), 2 if d <= 2 else 1, 0)

    fetches[0].wait()
    fetches[1].wait()
    halves_of[0, OWN] = kappa[...] * jnp.where(wet[...] == 1, F32(1.0), F32(0.05))

    def raw(a, b, c):
        return (a * N + b + par * (N - 1 - 2 * b)) * N + c

    def to_dual(f):
        return [(f[1] + f[3]) * 0.5, f[2] * 0.5, (f[1] - f[3]) * float(0.5 / KAPPA)]

    def load_plane(b):
        nothing = jnp.zeros((layers, width), F32)
        tiles = [jnp.concatenate([load[raw(n // N, b, n % N)], nothing], axis=0) for n in range(N * N)]
        lines = []
        for a in range(N):
            f = tiles[a * N:a * N + N]
            lines.append([f[0] + before(f[4])] + to_dual(f))
        columns = []
        for c in range(4):
            f = [lines[a][c] for a in range(N)]
            columns.append([below(f[0], f[4])] + to_dual(f))
        return [columns[c][a] for a in range(4) for c in range(4)]

    fetches[2].wait()
    for b in (0, 4, 2, 1, 3):
        for n, x in enumerate(load_plane(b)):
            if b == 3:
                other = rhs[0, 16 + n]
                rhs[0, 48 + n] = (other - x) * float(0.5 / KAPPA)
                rhs[0, 16 + n] = (other + x) * 0.5
            else:
                rhs[0, b * 16 + n] = x * 0.5 if b == 2 else x
    def at_group(g):
        return g if g < first else g + 1

    source = jnp.where(ex == 0, fold - 1, 0)
    turn = (lane // HALO + fold - source) % fold
    for g in range(groups):
        mixed = None
        for j in range(fold):
            x = rhs[0, g * fold + j]
            part[groups + 2 + g * fold + j] = x[0:layers]
            mixed = x if j == 0 else jnp.where(turn == j, pltpu.roll(x, HALO * j, 1), mixed)
        part[at_group(g)] = mixed[0:layers]
    mixed = None
    for j in range(20):
        x = rhs[0, 4 * j]
        mixed = x if j == 0 else jnp.where(lane == j, pltpu.roll(x, j, 1), mixed)
    for at in (first, groups + 1):
        part[at] = pltpu.roll(mixed, layers, 0)[0:layers]

    sol[...] = jnp.zeros_like(sol)
    pl.semaphore_wait(pltpu.get_barrier_semaphore(), expected)

    def half_copy(h, d, slot, device, source=0):
        return remote(halves_of.at[source, OWN], halves_of.at[h, slot], k_send.at[h, REACH + d], k_recv.at[h, slot],
                      device)

    def half_sent(h, d):
        half_copy(h, d, OWN, place(d), h).wait_send()

    def half_came(h, d):
        half_copy(h, d, REACH + d, place(d), h).wait_recv()

    half_copy(1, 0, OWN, place(0, True)).start()
    for d in NEAR_SENDS:
        @pl.when(there(d))
        def _():
            half_copy(0, d, slot_at(d), place(d)).start()
            half_copy(1, d, slot_at(d), place(d, True)).start()

    def halo_copy(k):
        at, size = ((0, groups + 1), (0, first + 1), (first + 1, groups - first))[k]
        return remote(part.at[at:at + size], got_halo.at[min(k, 1), at:at + size], x_send.at[k], x_recv.at[k],
                      place(-1 if k else 0, True))

    def part_copy(k):
        at, size = ((0, 17), (17, 64))[k]
        return remote(part.at[groups + 1 + at:groups + 1 + at + size], got_part.at[at:at + size], x_send.at[3 + k],
                      x_recv.at[3 + k], place(-1))

    halo_copy(0).start()

    @pl.when(there(-1))
    def _():
        halo_copy(1).start()
        part_copy(0).start()
        part_copy(1).start()
        halo_copy(2).start()

    for d in SENDS:
        if d not in NEAR_SENDS:
            when_there(d, lambda d: half_copy(0, d, slot_at(d), place(d)).start())

    outer = (sub >= layers) & (near < HALO)
    entering = first_lane & ((sub >= layers) | (ex == 1))

    def assemble(r, b):
        source_b = b if r == 0 or 0 < b < 4 else 4 - b
        nothing = jnp.zeros((layers, width), F32)
        spill = jnp.concatenate([got_halo[r, first], got_part[0] if r else nothing], axis=0)
        for a in range(4):
            for c in range(4):
                n, m = st(b, a, c), st(source_b, a, c)
                h = got_halo[r, at_group(m // fold)]
                h = jnp.concatenate([h, h], axis=0)
                if m % fold:
                    h = pltpu.roll(h, width - HALO * (m % fold), 1)
                h = jnp.where(outer, h, 0.0)
                if r == 0:
                    x = rhs[0, n] + h
                else:
                    p = got_part[1 + m]
                    x = jnp.where(lower, jnp.concatenate([p, p], axis=0), h)
                if c == 0:
                    j = m // 4
                    x = x + jnp.where(entering, pltpu.roll(spill, width - j, 1) if j else spill, 0.0)
                rhs[r, n] = -x if r == 1 and b == 3 else x

    block = lax.rem(lane + jnp.where(ex == 0, 0, HALO - 1), width) // HALO

    def swap(x):
        return pltpu.roll(x, layers, 0)

    def pack(s, x):
        for p in range(8):
            packed[s, p] = jnp.where(lower, x[2 * p], swap(x[2 * p + 1]))
        for p in range(8 // fold):
            halves = []
            for h in range(2):
                group = x[(2 * p + h) * fold:(2 * p + h + 1) * fold]
                mixed = group[0]
                for j in range(1, fold):
                    mixed = jnp.where(block == j, pltpu.roll(group[j], HALO * j, 1), mixed)
                halves.append(mixed)
            packed[s, 8 + p] = jnp.where(lower, swap(halves[0]), halves[1])

    def unpack(kind, s):
        x = []
        for p in range(8 // fold):
            tile = got[kind, s, 8 + p]
            for half in (swap(tile), tile):
                for j in range(fold):
                    other = half if j == 0 else pltpu.roll(half, width - HALO * j, 1)
                    n = len(x)
                    mine = got[kind, s, n // 2]
                    mine = mine if n % 2 == 0 else swap(mine)
                    x.append(jnp.where(lower, mine, jnp.where(block == 0, other, 0.0)))
        return x

    def near_copy(s):
        return remote(packed.at[s], got.at[0, s], f_send.at[0, s], f_recv.at[0, s], place(1))

    def far_copy(s):
        return remote(packed.at[s], got.at[1, s], f_send.at[1, s], f_recv.at[1, s], place(2))

    def send_face(s, values):
        pack(s, values)
        near_copy(s).start()

        @pl.when(there(2) & (s < STEPS - 1))
        def _():
            far_copy(s).start()

    def add_near(s):
        near_copy(s).wait()
        for n, x in enumerate(unpack(0, s)):
            tot[0, 64 + n] = tot[0, 64 + n] + x

    def add_far(s):
        @pl.when(there(-2))
        def _():
            far_copy(s).wait_recv()
            for n, x in enumerate(unpack(1, s)):
                tot[1, n] = tot[1, n] + x

    def expand(r, planes):
        for b in planes:
            w = []
            for a in range(4):
                v = [sol[r, st(b, a, c)] for c in range(4)]
                up = after(v[0])
                w.append([v[0] + up, v[1], v[2], v[3], v[0] - up])
            for k in range(N):
                up = above(w[0][k])
                xs[r, xi(b, 0, k)] = w[0][k] + up
                xs[r, xi(b, 4, k)] = w[0][k] - up
                for a in range(1, 4):
                    xs[r, xi(b, a, k)] = w[a][k]

    def cross(r):
        for i in range(N):
            for k in range(N):
                v = [xs[r, xi(b, i, k)] for b in range(N)]
                r0, r1, rz, s1, s0 = line_apply(v[0] + v[4], v[1], v[2], v[3], v[0] - v[4], MU[i] * MU[k])
                for b, x in enumerate((r0 + s0, r1, rz, s1)):
                    bs[r, xi(b, i, k)] = x

    def gather(y):
        g = []
        for k in range(N):
            low, high = plus(y[0][k], y[4][k]), minus(y[0][k], y[4][k])
            g.append([None if low is None else below(low, high)] + [y[i][k] for i in range(1, 4)])
        h = []
        for a in range(4):
            low, high = plus(g[0][a], g[4][a]), minus(g[0][a], g[4][a])
            h.append([None if low is None else low + before(high)] + [g[k][a] for k in range(1, 4)])
        return h

    def slot_of(a, c):
        return (0 if a else 2) + (0 if c else 1)

    def lumped(a, c):
        return (MU[a] if a else W0) * (MU[c] if c else W0)

    def top_plane(r):
        h = plane_image(r, 4, [[None] * N for _ in range(N)])
        weights = [ALPHA - ODD, BETA, -ALPHA - BETA, -ODD, ALPHA + ODD]
        out = []
        for a in range(4):
            for c in range(4):
                v = [float(weights[b] * lumped(a, c)) * sol[r, st(b, a, c)] for b in range(N)]
                line = ((v[0] + v[1]) + (v[2] + v[3])) + v[4]
                out.append(rhs[r, st(4, a, c)] - h[a][c] - shares[r, slot_of(a, c)] * line)
        return out

    def plane_image(r, b, along_b):
        coeff = coeffs[OWN - r]
        x = [[xs[r, xi(b, i, k)] for k in range(N)] for i in range(N)]
        along_c = [line_apply(*x[i], MUB[b] * MU[i]) for i in range(N)]
        along_a = [line_apply(*[x[i][k] for i in range(N)], MUB[b] * MU[k]) for k in range(N)]
        y = []
        for i in range(N):
            line = []
            for k in range(N):
                terms = sorted(((b == 2, along_b[i][k]), (k == 2, along_c[i][k]), (i == 2, along_a[k][i])),
                               key=lambda t: t[0])
                terms = [t for t in terms if t[1] is not None]
                total = -terms[0][1] if terms[0][0] else terms[0][1]
                for negative, term in terms[1:]:
                    total = total - term if negative else total + term
                line.append(coeff * total)
            y.append(line)
        return gather(y)

    def plane(r, b):
        h = plane_image(r, b, [[bs[r, xi(b, i, k)] for k in range(N)] for i in range(N)])
        return [rhs[r, st(b, a, c)] - h[a][c] for a in range(4) for c in range(4)]

    def put(r, b, values):
        for n, x in enumerate(values):
            tot[r, b * 16 + n] = x

    def update(r, b):
        for n in range(b * 16, b * 16 + 16):
            sol[r, n] = sol[r, n] + sinv[r, n] * tot[r, n]

    def inverted(x):
        return jnp.where(x > 0.0, 1.0 / jnp.where(x > 0.0, x, 1.0), 0.0)

    def invert():
        for r in range(2):
            here = coeffs[OWN - r]
            two = here + before(here)
            for k, x in enumerate((here, two, below(here, here), below(two, two))):
                shares[r, k] = x
            for bl, x in (((1, 2, 3), here), ((0,), here + coeffs[OWN - r - 1]), ((4,), here + coeffs[OWN - r + 1])):
                xc = x + before(x)
                tiles = [[inverted(below(xc, xc)), inverted(below(x, x))], [inverted(xc), inverted(x)]]
                for b in bl:
                    for a in range(4):
                        for c in range(4):
                            factor = FINE_RELAX * NU[a] * NU[b] * NU[c] / K3[NODE[a], NODE[b], NODE[c]]
                            sinv[r, st(b, a, c)] = float(factor) * tiles[min(a, 1)][min(c, 1)]

    def shift_top(r, at, n):
        delta = sinv[r, n] * tot[r, n]
        sol[r, n] = sol[r, n] + delta
        a, c = n // 4, n % 4
        factor = float((ALPHA - ODD) * lumped(a, c))
        tot[r, at + n] = tot[r, at + n] - factor * shares[r, slot_of(a, c)] * delta

    def join_coeff(e):
        coeffs[e] = jnp.where(real, jnp.concatenate([halves_of[0, e], halves_of[1, e]], axis=0), 0.0)

    def coarse_invert():
        for d in SENDS:
            @pl.when(there(d))
            def _():
                half_sent(0, d)
                half_sent(1, d)
        for d in RECVS:
            if d not in NEAR_RECVS:
                @pl.when(there(d))
                def _():
                    half_came(0, d)
                    half_came(1, d)
        for e in range(SPAN):
            if abs(e - OWN + 0.5) > 2:
                join_coeff(e)
        corner = 3.0 * SC[0, 0] * WC[0, 0] ** 2
        for i in range(SPAN - 1):
            pair = coeffs[i] + coeffs[i + 1]
            pair = pair + before(pair)
            cinv[i] = float(COARSE_RELAX / corner) * inverted(below(pair, pair))

    def halves(v):
        even, odd = v[1] + v[2], float(SLOPE) * v[3]
        return even + odd, even - odd

    def restrict_load():
        q = [[], []]
        for n in range(16):
            v = [rhs[0, b * 16 + n] for b in range(N)]
            low, high = halves(v)
            q[0].append(v[0] + low)
            q[1].append(v[4] + high)
        for j in range(2):
            lines = []
            for a in range(4):
                v = q[j][a * 4:a * 4 + 4]
                low, high = halves(v)
                lines.append((v[0] + low) + before(high))
            low, high = halves(lines)
            coarse_load[j] = below(lines[0] + low, high)

    def moments(first, mids, second):
        even, odd = first + second, first - second
        return (
            float(RISE) * odd,
            float(W0 / 2) * even + float(W1 / 2) * mids[0] + float(W2 / 4) * mids[1],
            float(W0 / 2) * odd + float(W1 * SLOPE / (2 * KAPPA ** 2)) * mids[2],
        )

    def coarse_send(cycle):
        along_b = []
        for n in range(16):
            v = [sol[0, b * 16 + n] for b in range(N)]
            along_b.append(moments(v[0], v[1:4], v[4]))
        mixed = [[], [], [], []]
        plain = [[], [], [], []]
        for c in range(4):
            along_a = []
            for kind in range(3):
                v = [along_b[a * 4 + c][kind] for a in range(4)]
                along_a.append(moments(v[0], v[1:4], above(v[0])))
            rise, even, odd = along_a
            mixed[1].append(rise[1])
            mixed[2].append(even[0])
            mixed[3].append(rise[2] + odd[0])
            for m, x in enumerate((even[1], odd[1], even[2], odd[2])):
                plain[m].append(x)
        coeff = coeffs[OWN]
        y = [None] * 4
        for m in range(4):
            steep = float(RISE) * (plain[m][0] - after(plain[m][0]))
            if m == 0:
                y[m] = (None, coeff * steep)
            else:
                v = mixed[m]
                part = moments(v[0], v[1:4], after(v[0]))
                y[m] = (coeff * part[1], coeff * (part[2] + steep))
        for j in range(2):
            g = []
            for k in range(2):
                r = []
                for a in range(2):
                    one, two = y[2 * a][k], y[2 * a + 1][k]
                    r.append(plus(one, two) if j == 0 else minus(one, two))
                g.append(below(r[0] + r[1], r[0] - r[1]))
            cgot[cycle, OWN, j] = coarse_load[j] - ((g[0] + g[1]) + before(g[0] - g[1]))
        for d in SENDS:
            when_there(d, lambda d: remote(
                cgot.at[cycle, OWN], cgot.at[cycle, slot_at(d)], c_send.at[REACH + d], c_recv.at[cycle, slot_at(d)],
                place(d)).start())

    def correct(cycle, own_done):
        @pl.when(cycle == 0)
        def _():
            coarse_invert()

        for d in SENDS:
            when_there(d, lambda d: remote(
                cgot.at[cycle, OWN], cgot.at[cycle, OWN], c_send.at[REACH + d], c_recv.at[cycle, OWN],
                place(d)).wait_send())
        for d in RECVS:
            when_there(d, lambda d: remote(
                cgot.at[cycle, OWN], cgot.at[cycle, REACH + d], c_send.at[OWN], c_recv.at[cycle, REACH + d],
                place(d)).wait_recv())

        def q(e, j):
            return cgot[cycle, e, j if (e - OWN) % 2 == 0 else 1 - j]

        lines = SPAN - 1
        rc = [q(i, 1) + q(i + 1, 0) for i in range(lines)]
        x = [cinv[i] * rc[i] for i in range(lines)]

        def modes(v):
            up = after(v)
            parts = []
            for k in (v + up, v - up):
                high = above(k)
                parts.append((k + high, k - high))
            return [[parts[k][i] for k in range(2)] for i in range(2)]

        begin, end = 0, lines - 1
        for sweep in range(NC - 1):
            m = {i: modes(x[i]) for i in range(begin, end + 1)}
            sides = {}
            for e in range(begin + 1, end + 1):
                coeff = coeffs[e]
                factor = [float(C1) * coeff, float(C2) * coeff, float(C3) * coeff]
                low, high = m[e - 1], m[e]
                part = []
                for i in range(2):
                    pair = []
                    for k in range(2):
                        odd = factor[i + k] * (low[i][k] - high[i][k])
                        if i + k == 0:
                            pair.append((odd, -odd))
                        else:
                            even = factor[i + k - 1] * (low[i][k] + high[i][k])
                            pair.append((even + odd, even - odd))
                    part.append(pair)
                sides[e] = part
            begin, end = begin + 1, end - 1
            new = list(x)
            for i in range(begin, end + 1):
                y = [[sides[i + 1][a][k][0] + sides[i][a][k][1] for k in range(2)] for a in range(2)]
                g = [below(y[0][k] + y[1][k], y[0][k] - y[1][k]) for k in range(2)]
                image = (g[0] + g[1]) + before(g[0] - g[1])
                new[i] = x[i] + cinv[i] * (rc[i] - image)
            x = new

        base = OWN - 3
        m = {i: modes(x[i]) for i in range(base, base + 5)}
        kind = [0, 0, 0, 1, 1]
        grow = [1.0, 1.0, 1.0, SLOPE, 1.0]

        def ends(centre, weight, tilt):
            y = [[None] * N for _ in range(N)]
            for i in range(N):
                for k in range(N):
                    value = None
                    if centre is not None:
                        value = float(MU[i] * MU[k] * grow[i] * grow[k]) * centre[kind[i]][kind[k]]
                    if i == 4:
                        value = plus(value, float(RISE * weight * MU[k] * grow[k]) * tilt[1][kind[k]])
                    if k == 4:
                        value = plus(value, float(RISE * weight * MU[i] * grow[i]) * tilt[kind[i]][1])
                    y[i][k] = value
            return gather(y)

        def face_image(i):
            up, down = coeffs[i + 1], coeffs[i]
            both = up + down
            centre = [[float(RISE) * (up * (m[i][a][k] - m[i + 1][a][k]) - down * (m[i - 1][a][k] - m[i][a][k]))
                       for k in range(2)] for a in range(2)]
            tilt = [[None if a + k == 0 else both * m[i][a][k] for k in range(2)] for a in range(2)]
            h = ends(centre, W0, tilt)
            return [h[a][c] for a in range(4) for c in range(4)]

        def correct_face(i, targets):
            values = face_image(i)
            for r, at in targets:
                for n, value in enumerate(values):
                    tot[r, at + n] = tot[r, at + n] - value
        scale = [1.0, 1.0, 1.0, SLOPE]

        def nodal(i):
            v = x[i]
            up = after(v)
            high = above(v)
            tiles = [[v, v + up, v - up], [v + high, m[i][0][0], m[i][0][1]], [v - high, m[i][1][0], m[i][1][1]]]
            pick = [0, 1, 1, 2]
            made = {}
            out = []
            for a in range(4):
                for c in range(4):
                    key = (pick[a], pick[c])
                    if key not in made:
                        factor = float(scale[a] * scale[c])
                        made[key] = tiles[key[0]][key[1]] if factor == 1.0 else factor * tiles[key[0]][key[1]]
                    out.append((key, made[key]))
            return out

        at_line = {i: nodal(i) for i in (OWN - 2, OWN - 1, OWN)}

        def correct_row(r):
            low, high = OWN - 1 - r, OWN - r
            coeff = coeffs[OWN - r]
            for kindb in range(2):
                diff = [[None if a + k == 0 else
                         coeff * (m[low][a][k] - m[high][a][k] if kindb else m[low][a][k] + m[high][a][k])
                         for k in range(2)] for a in range(2)]
                h = ends(None, 1.0, diff)
                for b in ((3,) if kindb else (1, 2)):
                    factor = float(MUB[b] * (SLOPE if kindb else 1.0))
                    for a in range(4):
                        for c in range(4):
                            if h[a][c] is not None:
                                tot[r, st(b, a, c)] = tot[r, st(b, a, c)] - factor * h[a][c]
                made = {}
                for n in range(16):
                    key, lower_value = at_line[low][n]
                    upper_value = at_line[high][n][1]
                    if key not in made:
                        made[key] = (float(SLOPE) * (lower_value - upper_value) if kindb
                                     else lower_value + upper_value)
                    for b in ((3,) if kindb else (1, 2)):
                        sol[r, b * 16 + n] = sol[r, b * 16 + n] + made[key]
            for n in range(16):
                sol[r, n] = sol[r, n] + at_line[low][n][1]
                sol[r, 64 + n] = sol[r, 64 + n] + at_line[high][n][1]

        correct_face(OWN - 1, ((1, 64), (0, 0)))
        correct_face(OWN, ((0, 64),))
        correct_row(0)
        own_done()
        correct_face(OWN - 2, ((1, 0),))
        correct_row(1)

    def emit(field, out_ref, dual, planes=range(N)):
        def split(mid, double, odd):
            if dual:
                odd = float(KAPPA) * odd
                return mid + odd, 2.0 * double, mid - odd
            even, odd = 0.5 * mid, float(0.5 / KAPPA) * odd
            return even + odd, 0.5 * double, even - odd

        def one(b, values):
            lines = []
            for a in range(4):
                v = values[a * 4:a * 4 + 4]
                lines.append([v[0], *split(*v[1:]), after(v[0])])
            for c in range(N):
                v = [lines[a][c] for a in range(4)]
                for a, tile in enumerate([v[0], *split(*v[1:]), above(v[0])]):
                    out_ref[raw(a, b, c)] = tile[0:layers]

        for b in (0, 4):
            if b in planes:
                one(b, [field[0, b * 16 + n] for n in range(16)])
        if 1 in planes:
            mids = [split(field[0, 16 + n], field[0, 32 + n], field[0, 48 + n]) for n in range(16)]
            for b in range(1, 4):
                one(b, [v[b - 1] for v in mids])

    halo_copy(0).wait()
    for b in (4, 0, 1, 2, 3):
        assemble(0, b)
        put(0, b, [rhs[0, b * 16 + n] for n in range(16)])
        if b == 4:
            send_face(0, [tot[0, 64 + n] for n in range(16)])
    half_copy(1, 0, OWN, place(0, True)).wait()
    for d in SENDS:
        if d not in NEAR_SENDS:
            when_there(d, lambda d: half_copy(1, d, slot_at(d), place(d), 1).start())
    for d in NEAR_RECVS:
        @pl.when(there(d))
        def _():
            half_came(0, d)
            half_came(1, d)
    for e in range(OWN - 2, OWN + 2):
        join_coeff(e)
    invert()

    @pl.when(there(-1))
    def _():
        part_copy(0).wait()
        halo_copy(1).wait()

    assemble(1, 4)
    for n in range(16):
        joined = tot[0, n] + rhs[1, 64 + n]
        tot[0, n] = joined
        tot[1, 64 + n] = joined
    for b in range(4):
        update(0, b)
    add_near(0)
    update(0, 4)

    def ready_face(s):
        expand(0, (4,))
        put(0, 4, top_plane(0))

    def next_face(s):
        send_face(s, [tot[0, 64 + n] for n in range(16)])

    ready_face(1)
    next_face(1)
    restrict_load()

    def step(s, _):
        cycle = s // PERIOD
        live = s < STEPS - 1
        coarse = (lax.rem(s, PERIOD) == NPRE) & live
        deferred = lax.rem(s - 1, PERIOD) != NPRE
        behind = deferred & (s > 1)
        plain = jnp.logical_not(coarse) & live

        expand(0, range(4))
        cross(0)
        for b in range(4):
            put(0, b, plane(0, b))

        @pl.when(there(2))
        def _():
            far_copy(s - 1).wait_send()

        @pl.when(behind)
        def _():
            expand(1, range(4))
            cross(1)
            for b in range(4):
                put(1, b, plane(1, b))
                if b:
                    update(1, b)
            update(1, 4)

        @pl.when(coarse)
        def _():
            add_far(s - 1)
            update(1, 0)

        @pl.when(s > 1)
        def _():
            expand(1, (4,))
            put(1, 4, top_plane(1))

        @pl.when(coarse)
        def _():
            expand(1, range(4))
            cross(1)
            for b in range(4):
                put(1, b, plane(1, b))

        @pl.when(jnp.logical_not(live))
        def _():
            emit(sol, sol_out, False)

        @pl.when(plain)
        def _():
            for b in range(1, 4):
                update(0, b)

        add_near(s)

        @pl.when(jnp.logical_not(live))
        def _():
            emit(tot, res_out, True, range(1, N))

        @pl.when(plain)
        def _():
            update(0, 4)
            ready_face(s + 1)

        @pl.when(s == 1)
        def _():
            @pl.when(there(-1))
            def _():
                part_copy(1).wait()
                halo_copy(2).wait()

            for b in range(4):
                assemble(1, b)
                put(1, b, [rhs[1, b * 16 + n] for n in range(16)])
                if b:
                    update(1, b)
            update(1, 4)
            expand(1, (4,))
            put(1, 4, top_plane(1))

        def join(n):
            joined = tot[0, n] + tot[1, 64 + n]
            tot[0, n] = joined
            tot[1, 64 + n] = joined

        @pl.when(deferred & plain)
        def _():
            add_far(s - 1)
            for n in range(16):
                shift_top(1, 64, n)
                join(n)
                shift_top(0, 64, n)

        @pl.when(jnp.logical_not(deferred & plain))
        def _():
            @pl.when(deferred & jnp.logical_not(coarse))
            def _():
                add_far(s - 1)
                for n in range(16):
                    shift_top(1, 64, n)

            for n in range(16):
                join(n)

            @pl.when(plain)
            def _():
                for n in range(16):
                    shift_top(0, 64, n)

        @pl.when(coarse)
        def _():
            add_far(s)

            def own_done():
                for b in range(N):
                    update(0, b)
                ready_face(s + 1)
                next_face(s + 1)

            correct(cycle, own_done)
            for b in range(N):
                update(1, b)

        @pl.when((lax.rem(s + 1, PERIOD) == NPRE) & (s + 1 < STEPS - 1))
        def _():
            coarse_send((s + 1) // PERIOD)

        @pl.when(plain)
        def _():
            next_face(s + 1)

        return 0

    lax.fori_loop(1, STEPS, step, 0)
    emit(tot, res_out, True, (0,))


def hand_over(sol_ref, res_ref, sol_out, res_out, sems):
    copies = [pltpu.make_async_copy(src, dst, sems.at[k]) for k, (src, dst) in enumerate(
        ((sol_ref, sol_out), (res_ref, res_out)))]
    for copy in copies:
        copy.start()
    for copy in copies:
        copy.wait()


def per_device(sizes, load, kappa, wet):
    layers, _, width = kappa.shape
    nodes = N * N * N
    tile = (2 * layers, width)
    half = (layers, width)
    sizes = sizes + (layers, width)
    out = jax.ShapeDtypeStruct((nodes, layers, width), F32)
    vmem = pl.BlockSpec(memory_space=pltpu.VMEM)
    fold = width // HALO
    groups = 80 // fold
    messages = 8 + 8 // fold
    dma = pltpu.SemaphoreType.DMA
    solution, residual = pl.pallas_call(
        functools.partial(kernel, sizes),
        out_shape=(out, out),
        in_specs=[pl.BlockSpec(memory_space=pltpu.HBM)] * 3,
        out_specs=(vmem, vmem),
        scratch_shapes=[
            pltpu.VMEM((nodes,) + half, F32),
            pltpu.VMEM(half, F32),
            pltpu.VMEM(half, jnp.int32),
            pltpu.VMEM((groups + 82,) + half, F32),
            pltpu.VMEM((81,) + half, F32),
            pltpu.VMEM((2, groups + 1) + half, F32),
            pltpu.VMEM((2, SPAN + 1) + half, F32),
            pltpu.VMEM((SPAN,) + tile, F32),
            pltpu.VMEM((2, 80) + tile, F32),
            pltpu.VMEM((2, 80) + tile, F32),
            pltpu.VMEM((2, 80) + tile, F32),
            pltpu.VMEM((2, 80) + tile, F32),
            pltpu.VMEM((2, nodes) + tile, F32),
            pltpu.VMEM((2, nodes) + tile, F32),
            pltpu.VMEM((2,) + tile, F32),
            pltpu.VMEM((2, 4) + tile, F32),
            pltpu.VMEM((STEPS, messages) + tile, F32),
            pltpu.VMEM((2, STEPS, messages) + tile, F32),
            pltpu.VMEM((CYCLES, SPAN, 2) + tile, F32),
            pltpu.VMEM((SPAN - 1,) + tile, F32),
            dma((3,)), dma((5,)), dma((5,)), dma((2, SPAN + 1)), dma((2, SPAN + 1)),
            dma((2, STEPS)), dma((2, STEPS)), dma((SPAN + 1,)), dma((CYCLES, SPAN + 1)),
        ],
        compiler_params=pltpu.CompilerParams(collective_id=0, has_side_effects=True, vmem_limit_bytes=16 * 2 ** 20),
    )(*[pltpu.with_memory_space_constraint(x, pltpu.HBM) for x in (
        load.reshape(nodes, layers, width), kappa.reshape(layers, width), wet.reshape(layers, width))])
    place = pl.BlockSpec(memory_space=pl.ANY)
    solution, residual = pl.pallas_call(
        hand_over, out_shape=(out, out), in_specs=[place] * 2, out_specs=(place, place),
        scratch_shapes=[dma((2,))],
        compiler_params=pltpu.CompilerParams(vmem_limit_bytes=2 ** 20),
    )(solution, residual)
    return solution.reshape(load.shape), residual.reshape(load.shape)


def solution(mesh):
    sizes = tuple(mesh.shape[name] for name in ("ex", "ey", "lin"))
    field = P(None, None, None, None, ("ey", "lin"), "ex")
    cell = P(None, ("ey", "lin"), "ex")
    return jax.shard_map(
        functools.partial(per_device, sizes), mesh=mesh, in_specs=(field, cell, cell),
        out_specs=(field, field), check_vma=False,
    )
```

```python
import functools
import math

import jax
import jax.numpy as jnp
import numpy as np
from jax import lax
from jax.experimental import pallas as pl
from jax.experimental.pallas import tpu as pltpu
from jax.sharding import PartitionSpec as P

N = 5
CYCLES = 2
NPRE = 2
NPOST = 2
NC = 4
PERIOD = NPRE + NPOST
FINE_RELAX = 0.25
COARSE_RELAX = 0.4
STEPS = CYCLES * PERIOD + 1
REACH = NC + 2
SPAN = 2 * REACH
OWN = REACH
HALO = 32
MESH = pl.DeviceIdType.MESH
F32 = jnp.float32


def node_tables():
    points = np.array([-1.0, -math.sqrt(3.0 / 7.0), 0.0, math.sqrt(3.0 / 7.0), 1.0])
    weights = np.array([0.1, 49.0 / 90.0, 32.0 / 45.0, 49.0 / 90.0, 0.1])
    eye_table = np.eye(points.shape[0])
    spread = points[:, None] - points[None, :] + eye_table
    factors = np.prod(spread, axis=1)
    deriv = factors[:, None] / (factors[None, :] * spread)
    deriv = np.where(eye_table > 0, (np.sum(1.0 / spread, axis=1) - 1.0)[:, None], deriv)
    stiff = deriv.T @ (weights[:, None] * deriv)
    mass = eye_table * weights[:, None]
    interp = np.stack([(1.0 - points) / 2.0, (1.0 + points) / 2.0], axis=1)
    return stiff, weights, interp, interp.T @ stiff @ interp, interp.T @ mass @ interp


S, WEIGHTS, INTERP, SC, WC = node_tables()
ALPHA = (S[0, 0] + S[0, 4]) / 2
BETA = (S[0, 1] + S[0, 3]) / 2
GAMMA = (S[1, 1] + S[1, 3]) / 2
KAPPA = (S[0, 1] - S[0, 3]) / (S[0, 0] - S[0, 4])
ODD = (S[0, 0] - S[0, 4]) / 2
DELTA = (S[1, 1] - S[1, 3]) / (2 * KAPPA ** 2) - ODD
W0, W1, W2 = WEIGHTS[:3]
MU = [W0 / 2, W1 / 2, W2 / 4, W1 / (2 * KAPPA ** 2), W0 / 2]
MUB = [W0, W1 / 2, W2 / 4, W1 / (2 * KAPPA ** 2), W0]
NU = [1.0, 2.0, 4.0, 2 * KAPPA ** 2, 1.0]
SLOPE = KAPPA * (INTERP[1, 0] - INTERP[3, 0])
RISE = ODD * (1 + SLOPE)
NODE = [0, 1, 2, 1, 4]
DIAG = np.diag(S) / WEIGHTS
W3 = WEIGHTS[:, None, None] * WEIGHTS[None, :, None] * WEIGHTS[None, None, :]
K3 = W3 * (DIAG[:, None, None] + DIAG[None, :, None] + DIAG[None, None, :])
CS = (SC[0, 0] - SC[0, 1]) / 2
CE, CO = (WC[0, 0] + WC[0, 1]) / 2, (WC[0, 0] - WC[0, 1]) / 2
C1, C2, C3 = CS * CE * CE, 2 * CS * CO * CE, 3 * CS * CO * CO
SENDS = sorted((d for d in range(-REACH + 1, REACH + 1) if d != 0), key=abs)
RECVS = [d for d in range(-REACH, REACH) if d != 0]
NEAR_SENDS = [-1, 1, 2]
NEAR_RECVS = [-1, 1, -2]


def st(b, a, c):
    return (b * 4 + a) * 4 + c


def xi(b, i, k):
    return (b * N + i) * N + k


def line_apply(e0, e1, z, o1, o0, scale):
    q0, q1 = e0 - z, e1 - z
    r0 = float(ALPHA * scale) * q0 + float(BETA * scale) * q1
    r1 = float(BETA * scale) * q0 + float(GAMMA * scale) * q1
    s0 = float(ODD * scale) * (o0 + o1)
    return r0, r1, r0 + r1, s0 + float(DELTA * scale) * o1, s0


def plus(x, y):
    if x is None or y is None:
        return x if y is None else y
    return x + y


def minus(x, y):
    if y is None:
        return x
    return -y if x is None else x - y


def kernel(
    sizes, load_ref, kappa_ref, wet_ref, sol_out, res_out,
    load, kappa, wet, part, got_part, got_halo, halves_of, coeffs,
    rhs, sol, tot, sinv, xs, bs, coarse_load, shares, packed, got, cgot, cinv,
    load_sem, x_send, x_recv, k_send, k_recv, f_send, f_recv, c_send, c_recv,
):
    ex_count, ey_count, lin_count, layers, width = sizes
    ex, ey, lin = lax.axis_index("ex"), lax.axis_index("ey"), lax.axis_index("lin")
    rows = ey_count * lin_count
    row = ey * lin_count + lin
    par = lax.rem(lin, 2)
    sgn = 1 - 2 * par
    fold = width // HALO
    groups = 80 // fold
    first = 16 // fold

    sub = lax.broadcasted_iota(jnp.int32, (2 * layers, width), 0)
    lane = lax.broadcasted_iota(jnp.int32, (2 * layers, width), 1)
    layer = sub % layers
    bottom, top = layer == 0, layer == layers - 1
    first_lane, last_lane = lane == 0, lane == width - 1
    near = jnp.where(ex == 0, lane, width - 1 - lane)
    real = (sub < layers) | (near < HALO)
    lower = sub < layers

    def before(x):
        y = pltpu.roll(x, 1, 1)
        return jnp.where(first_lane, pltpu.roll(y, layers, 0), y)

    def after(x):
        y = pltpu.roll(x, width - 1, 1)
        return jnp.where(last_lane, pltpu.roll(y, layers, 0), y)

    def below(low, high):
        return jnp.where(bottom, low, low + pltpu.roll(high, 1, 0))

    def above(low):
        return jnp.where(top, 0.0, pltpu.roll(low, 2 * layers - 1, 0))

    def there(d):
        at = row + sgn * d
        return (at >= 0) & (at < rows)

    def place(d, other=False):
        at = row + sgn * d
        return (1 - ex if other else ex, at // lin_count, at % lin_count)

    def when_there(d, fn):
        @pl.when(there(d))
        def _():
            fn(d)

    def slot_at(d):
        return REACH + (-d if d % 2 == 0 else d)

    def remote(src, dst, send, recv, device):
        return pltpu.make_async_remote_copy(
            src_ref=src, dst_ref=dst, send_sem=send, recv_sem=recv, device_id=device, device_id_type=MESH)

    fetches = [pltpu.make_async_copy(src, dst, load_sem.at[k]) for k, (src, dst) in enumerate(
        ((kappa_ref, kappa), (wet_ref, wet), (load_ref, load)))]
    for fetch in fetches:
        fetch.start()
    halves_of[...] = jnp.zeros_like(halves_of)
    cgot[...] = jnp.zeros_like(cgot)

    @pl.when(jnp.logical_not(there(-1)))
    def _():
        got_part[...] = jnp.zeros_like(got_part)
        got_halo[1] = jnp.zeros_like(got_halo[1])

    def greet(device):
        pl.semaphore_signal(pltpu.get_barrier_semaphore(), inc=1, device_id=device, device_id_type=MESH)

    greet((1 - ex, ey, lin))
    expected = jnp.int32(1)
    for d in range(1, REACH + 1):
        for e in (-d, d):
            @pl.when(there(e))
            def _():
                greet(place(e))
                if d <= 2:
                    greet(place(e, True))
            expected = expected + jnp.where(there(e), 2 if d <= 2 else 1, 0)

    fetches[0].wait()
    fetches[1].wait()
    halves_of[0, OWN] = kappa[...] * jnp.where(wet[...] == 1, F32(1.0), F32(0.05))

    def raw(a, b, c):
        return (a * N + b + par * (N - 1 - 2 * b)) * N + c

    def to_dual(f):
        return [(f[1] + f[3]) * 0.5, f[2] * 0.5, (f[1] - f[3]) * float(0.5 / KAPPA)]

    def load_plane(b):
        nothing = jnp.zeros((layers, width), F32)
        tiles = [jnp.concatenate([load[raw(n // N, b, n % N)], nothing], axis=0) for n in range(N * N)]
        lines = []
        for a in range(N):
            f = tiles[a * N:a * N + N]
            lines.append([f[0] + before(f[4])] + to_dual(f))
        columns = []
        for c in range(4):
            f = [lines[a][c] for a in range(N)]
            columns.append([below(f[0], f[4])] + to_dual(f))
        return [columns[c][a] for a in range(4) for c in range(4)]

    fetches[2].wait()
    for b in (0, 4, 2, 1, 3):
        for n, x in enumerate(load_plane(b)):
            if b == 3:
                other = rhs[0, 16 + n]
                rhs[0, 48 + n] = (other - x) * float(0.5 / KAPPA)
                rhs[0, 16 + n] = (other + x) * 0.5
            else:
                rhs[0, b * 16 + n] = x * 0.5 if b == 2 else x
    def at_group(g):
        return g if g < first else g + 1

    source = jnp.where(ex == 0, fold - 1, 0)
    turn = (lane // HALO + fold - source) % fold
    for g in range(groups):
        mixed = None
        for j in range(fold):
            x = rhs[0, g * fold + j]
            part[groups + 2 + g * fold + j] = x[0:layers]
            mixed = x if j == 0 else jnp.where(turn == j, pltpu.roll(x, HALO * j, 1), mixed)
        part[at_group(g)] = mixed[0:layers]
    mixed = None
    for j in range(20):
        x = rhs[0, 4 * j]
        mixed = x if j == 0 else jnp.where(lane == j, pltpu.roll(x, j, 1), mixed)
    for at in (first, groups + 1):
        part[at] = pltpu.roll(mixed, layers, 0)[0:layers]

    sol[...] = jnp.zeros_like(sol)
    pl.semaphore_wait(pltpu.get_barrier_semaphore(), expected)

    def half_copy(h, d, slot, device, source=0):
        return remote(halves_of.at[source, OWN], halves_of.at[h, slot], k_send.at[h, REACH + d], k_recv.at[h, slot],
                      device)

    def half_sent(h, d):
        half_copy(h, d, OWN, place(d), h).wait_send()

    def half_came(h, d):
        half_copy(h, d, REACH + d, place(d), h).wait_recv()

    half_copy(1, 0, OWN, place(0, True)).start()
    for d in NEAR_SENDS:
        @pl.when(there(d))
        def _():
            half_copy(0, d, slot_at(d), place(d)).start()
            half_copy(1, d, slot_at(d), place(d, True)).start()

    def halo_copy(k):
        at, size = ((0, groups + 1), (0, first + 1), (first + 1, groups - first))[k]
        return remote(part.at[at:at + size], got_halo.at[min(k, 1), at:at + size], x_send.at[k], x_recv.at[k],
                      place(-1 if k else 0, True))

    def part_copy(k):
        at, size = ((0, 17), (17, 64))[k]
        return remote(part.at[groups + 1 + at:groups + 1 + at + size], got_part.at[at:at + size], x_send.at[3 + k],
                      x_recv.at[3 + k], place(-1))

    halo_copy(0).start()

    @pl.when(there(-1))
    def _():
        halo_copy(1).start()
        part_copy(0).start()
        part_copy(1).start()
        halo_copy(2).start()

    for d in SENDS:
        if d not in NEAR_SENDS:
            when_there(d, lambda d: half_copy(0, d, slot_at(d), place(d)).start())

    outer = (sub >= layers) & (near < HALO)
    entering = first_lane & ((sub >= layers) | (ex == 1))

    def assemble(r, b):
        source_b = b if r == 0 or 0 < b < 4 else 4 - b
        nothing = jnp.zeros((layers, width), F32)
        spill = jnp.concatenate([got_halo[r, first], got_part[0] if r else nothing], axis=0)
        for a in range(4):
            for c in range(4):
                n, m = st(b, a, c), st(source_b, a, c)
                h = got_halo[r, at_group(m // fold)]
                h = jnp.concatenate([h, h], axis=0)
                if m % fold:
                    h = pltpu.roll(h, width - HALO * (m % fold), 1)
                h = jnp.where(outer, h, 0.0)
                if r == 0:
                    x = rhs[0, n] + h
                else:
                    p = got_part[1 + m]
                    x = jnp.where(lower, jnp.concatenate([p, p], axis=0), h)
                if c == 0:
                    j = m // 4
                    x = x + jnp.where(entering, pltpu.roll(spill, width - j, 1) if j else spill, 0.0)
                rhs[r, n] = -x if r == 1 and b == 3 else x

    block = lax.rem(lane + jnp.where(ex == 0, 0, HALO - 1), width) // HALO

    def swap(x):
        return pltpu.roll(x, layers, 0)

    def pack(s, x):
        for p in range(8):
            packed[s, p] = jnp.where(lower, x[2 * p], swap(x[2 * p + 1]))
        for p in range(8 // fold):
            halves = []
            for h in range(2):
                group = x[(2 * p + h) * fold:(2 * p + h + 1) * fold]
                mixed = group[0]
                for j in range(1, fold):
                    mixed = jnp.where(block == j, pltpu.roll(group[j], HALO * j, 1), mixed)
                halves.append(mixed)
            packed[s, 8 + p] = jnp.where(lower, swap(halves[0]), halves[1])

    def unpack(kind, s):
        x = []
        for p in range(8 // fold):
            tile = got[kind, s, 8 + p]
            for half in (swap(tile), tile):
                for j in range(fold):
                    other = half if j == 0 else pltpu.roll(half, width - HALO * j, 1)
                    n = len(x)
                    mine = got[kind, s, n // 2]
                    mine = mine if n % 2 == 0 else swap(mine)
                    x.append(jnp.where(lower, mine, jnp.where(block == 0, other, 0.0)))
        return x

    def near_copy(s):
        return remote(packed.at[s], got.at[0, s], f_send.at[0, s], f_recv.at[0, s], place(1))

    def far_copy(s):
        return remote(packed.at[s], got.at[1, s], f_send.at[1, s], f_recv.at[1, s], place(2))

    def send_face(s, values):
        pack(s, values)

        @pl.when(there(2) & (s < STEPS - 1))
        def _():
            far_copy(s).start()

        near_copy(s).start()

    def add_near(s):
        near_copy(s).wait()
        for n, x in enumerate(unpack(0, s)):
            tot[0, 64 + n] = tot[0, 64 + n] + x

    def add_far(s):
        @pl.when(there(-2))
        def _():
            far_copy(s).wait_recv()
            for n, x in enumerate(unpack(1, s)):
                tot[1, n] = tot[1, n] + x

    def expand(r, planes):
        for b in planes:
            w = []
            for a in range(4):
                v = [sol[r, st(b, a, c)] for c in range(4)]
                up = after(v[0])
                w.append([v[0] + up, v[1], v[2], v[3], v[0] - up])
            for k in range(N):
                up = above(w[0][k])
                xs[r, xi(b, 0, k)] = w[0][k] + up
                xs[r, xi(b, 4, k)] = w[0][k] - up
                for a in range(1, 4):
                    xs[r, xi(b, a, k)] = w[a][k]

    def cross(r):
        for i in range(N):
            for k in range(N):
                v = [xs[r, xi(b, i, k)] for b in range(N)]
                r0, r1, rz, s1, s0 = line_apply(v[0] + v[4], v[1], v[2], v[3], v[0] - v[4], MU[i] * MU[k])
                for b, x in enumerate((r0 + s0, r1, rz, s1)):
                    bs[r, xi(b, i, k)] = x

    def gather(y):
        g = []
        for k in range(N):
            low, high = plus(y[0][k], y[4][k]), minus(y[0][k], y[4][k])
            g.append([None if low is None else below(low, high)] + [y[i][k] for i in range(1, 4)])
        h = []
        for a in range(4):
            low, high = plus(g[0][a], g[4][a]), minus(g[0][a], g[4][a])
            h.append([None if low is None else low + before(high)] + [g[k][a] for k in range(1, 4)])
        return h

    def slot_of(a, c):
        return (0 if a else 2) + (0 if c else 1)

    def lumped(a, c):
        return (MU[a] if a else W0) * (MU[c] if c else W0)

    def top_plane(r):
        h = plane_image(r, 4, [[None] * N for _ in range(N)])
        weights = [ALPHA - ODD, BETA, -ALPHA - BETA, -ODD, ALPHA + ODD]
        out = []
        for a in range(4):
            for c in range(4):
                v = [float(weights[b] * lumped(a, c)) * sol[r, st(b, a, c)] for b in range(N)]
                line = ((v[0] + v[1]) + (v[2] + v[3])) + v[4]
                out.append(rhs[r, st(4, a, c)] - h[a][c] - shares[r, slot_of(a, c)] * line)
        return out

    def plane_image(r, b, along_b):
        coeff = coeffs[OWN - r]
        x = [[xs[r, xi(b, i, k)] for k in range(N)] for i in range(N)]
        along_c = [line_apply(*x[i], MUB[b] * MU[i]) for i in range(N)]
        along_a = [line_apply(*[x[i][k] for i in range(N)], MUB[b] * MU[k]) for k in range(N)]
        y = []
        for i in range(N):
            line = []
            for k in range(N):
                terms = sorted(((b == 2, along_b[i][k]), (k == 2, along_c[i][k]), (i == 2, along_a[k][i])),
                               key=lambda t: t[0])
                terms = [t for t in terms if t[1] is not None]
                total = -terms[0][1] if terms[0][0] else terms[0][1]
                for negative, term in terms[1:]:
                    total = total - term if negative else total + term
                line.append(coeff * total)
            y.append(line)
        return gather(y)

    def plane(r, b):
        h = plane_image(r, b, [[bs[r, xi(b, i, k)] for k in range(N)] for i in range(N)])
        return [rhs[r, st(b, a, c)] - h[a][c] for a in range(4) for c in range(4)]

    def put(r, b, values):
        for n, x in enumerate(values):
            tot[r, b * 16 + n] = x

    def update(r, b):
        for n in range(b * 16, b * 16 + 16):
            sol[r, n] = sol[r, n] + sinv[r, n] * tot[r, n]

    def inverted(x):
        return jnp.where(x > 0.0, 1.0 / jnp.where(x > 0.0, x, 1.0), 0.0)

    def invert():
        for r in range(2):
            here = coeffs[OWN - r]
            two = here + before(here)
            for k, x in enumerate((here, two, below(here, here), below(two, two))):
                shares[r, k] = x
            for bl, x in (((1, 2, 3), here), ((0,), here + coeffs[OWN - r - 1]), ((4,), here + coeffs[OWN - r + 1])):
                xc = x + before(x)
                tiles = [[inverted(below(xc, xc)), inverted(below(x, x))], [inverted(xc), inverted(x)]]
                for b in bl:
                    for a in range(4):
                        for c in range(4):
                            factor = FINE_RELAX * NU[a] * NU[b] * NU[c] / K3[NODE[a], NODE[b], NODE[c]]
                            sinv[r, st(b, a, c)] = float(factor) * tiles[min(a, 1)][min(c, 1)]

    def shift_top(r, at, n):
        delta = sinv[r, n] * tot[r, n]
        sol[r, n] = sol[r, n] + delta
        a, c = n // 4, n % 4
        factor = float((ALPHA - ODD) * lumped(a, c))
        tot[r, at + n] = tot[r, at + n] - factor * shares[r, slot_of(a, c)] * delta

    def join_coeff(e):
        coeffs[e] = jnp.where(real, jnp.concatenate([halves_of[0, e], halves_of[1, e]], axis=0), 0.0)

    def coarse_invert():
        for d in SENDS:
            @pl.when(there(d))
            def _():
                half_sent(0, d)
                half_sent(1, d)
        for d in RECVS:
            if d not in NEAR_RECVS:
                @pl.when(there(d))
                def _():
                    half_came(0, d)
                    half_came(1, d)
        for e in range(SPAN):
            if abs(e - OWN + 0.5) > 2:
                join_coeff(e)
        corner = 3.0 * SC[0, 0] * WC[0, 0] ** 2
        for i in range(SPAN - 1):
            pair = coeffs[i] + coeffs[i + 1]
            pair = pair + before(pair)
            cinv[i] = float(COARSE_RELAX / corner) * inverted(below(pair, pair))

    def halves(v):
        even, odd = v[1] + v[2], float(SLOPE) * v[3]
        return even + odd, even - odd

    def restrict_load():
        q = [[], []]
        for n in range(16):
            v = [rhs[0, b * 16 + n] for b in range(N)]
            low, high = halves(v)
            q[0].append(v[0] + low)
            q[1].append(v[4] + high)
        for j in range(2):
            lines = []
            for a in range(4):
                v = q[j][a * 4:a * 4 + 4]
                low, high = halves(v)
                lines.append((v[0] + low) + before(high))
            low, high = halves(lines)
            coarse_load[j] = below(lines[0] + low, high)

    def moments(first, mids, second):
        even, odd = first + second, first - second
        return (
            float(RISE) * odd,
            float(W0 / 2) * even + float(W1 / 2) * mids[0] + float(W2 / 4) * mids[1],
            float(W0 / 2) * odd + float(W1 * SLOPE / (2 * KAPPA ** 2)) * mids[2],
        )

    def coarse_send(cycle):
        along_b = []
        for n in range(16):
            v = [sol[0, b * 16 + n] for b in range(N)]
            along_b.append(moments(v[0], v[1:4], v[4]))
        mixed = [[], [], [], []]
        plain = [[], [], [], []]
        for c in range(4):
            along_a = []
            for kind in range(3):
                v = [along_b[a * 4 + c][kind] for a in range(4)]
                along_a.append(moments(v[0], v[1:4], above(v[0])))
            rise, even, odd = along_a
            mixed[1].append(rise[1])
            mixed[2].append(even[0])
            mixed[3].append(rise[2] + odd[0])
            for m, x in enumerate((even[1], odd[1], even[2], odd[2])):
                plain[m].append(x)
        coeff = coeffs[OWN]
        y = [None] * 4
        for m in range(4):
            steep = float(RISE) * (plain[m][0] - after(plain[m][0]))
            if m == 0:
                y[m] = (None, coeff * steep)
            else:
                v = mixed[m]
                part = moments(v[0], v[1:4], after(v[0]))
                y[m] = (coeff * part[1], coeff * (part[2] + steep))
        for j in range(2):
            g = []
            for k in range(2):
                r = []
                for a in range(2):
                    one, two = y[2 * a][k], y[2 * a + 1][k]
                    r.append(plus(one, two) if j == 0 else minus(one, two))
                g.append(below(r[0] + r[1], r[0] - r[1]))
            cgot[cycle, OWN, j] = coarse_load[j] - ((g[0] + g[1]) + before(g[0] - g[1]))
        for d in SENDS:
            when_there(d, lambda d: remote(
                cgot.at[cycle, OWN], cgot.at[cycle, slot_at(d)], c_send.at[REACH + d], c_recv.at[cycle, slot_at(d)],
                place(d)).start())

    def correct(cycle, own_done):
        @pl.when(cycle == 0)
        def _():
            coarse_invert()

        for d in SENDS:
            when_there(d, lambda d: remote(
                cgot.at[cycle, OWN], cgot.at[cycle, OWN], c_send.at[REACH + d], c_recv.at[cycle, OWN],
                place(d)).wait_send())
        for d in RECVS:
            when_there(d, lambda d: remote(
                cgot.at[cycle, OWN], cgot.at[cycle, REACH + d], c_send.at[OWN], c_recv.at[cycle, REACH + d],
                place(d)).wait_recv())

        def q(e, j):
            return cgot[cycle, e, j if (e - OWN) % 2 == 0 else 1 - j]

        lines = SPAN - 1
        rc = [q(i, 1) + q(i + 1, 0) for i in range(lines)]
        x = [cinv[i] * rc[i] for i in range(lines)]

        def modes(v):
            up = after(v)
            parts = []
            for k in (v + up, v - up):
                high = above(k)
                parts.append((k + high, k - high))
            return [[parts[k][i] for k in range(2)] for i in range(2)]

        begin, end = 0, lines - 1
        for sweep in range(NC - 1):
            m = {i: modes(x[i]) for i in range(begin, end + 1)}
            sides = {}
            for e in range(begin + 1, end + 1):
                coeff = coeffs[e]
                factor = [float(C1) * coeff, float(C2) * coeff, float(C3) * coeff]
                low, high = m[e - 1], m[e]
                part = []
                for i in range(2):
                    pair = []
                    for k in range(2):
                        odd = factor[i + k] * (low[i][k] - high[i][k])
                        if i + k == 0:
                            pair.append((odd, -odd))
                        else:
                            even = factor[i + k - 1] * (low[i][k] + high[i][k])
                            pair.append((even + odd, even - odd))
                    part.append(pair)
                sides[e] = part
            begin, end = begin + 1, end - 1
            new = list(x)
            for i in range(begin, end + 1):
                y = [[sides[i + 1][a][k][0] + sides[i][a][k][1] for k in range(2)] for a in range(2)]
                g = [below(y[0][k] + y[1][k], y[0][k] - y[1][k]) for k in range(2)]
                image = (g[0] + g[1]) + before(g[0] - g[1])
                new[i] = x[i] + cinv[i] * (rc[i] - image)
            x = new

        base = OWN - 3
        m = {i: modes(x[i]) for i in range(base, base + 5)}
        kind = [0, 0, 0, 1, 1]
        grow = [1.0, 1.0, 1.0, SLOPE, 1.0]

        def ends(centre, weight, tilt):
            y = [[None] * N for _ in range(N)]
            for i in range(N):
                for k in range(N):
                    value = None
                    if centre is not None:
                        value = float(MU[i] * MU[k] * grow[i] * grow[k]) * centre[kind[i]][kind[k]]
                    if i == 4:
                        value = plus(value, float(RISE * weight * MU[k] * grow[k]) * tilt[1][kind[k]])
                    if k == 4:
                        value = plus(value, float(RISE * weight * MU[i] * grow[i]) * tilt[kind[i]][1])
                    y[i][k] = value
            return gather(y)

        def face_image(i):
            up, down = coeffs[i + 1], coeffs[i]
            both = up + down
            centre = [[float(RISE) * (up * (m[i][a][k] - m[i + 1][a][k]) - down * (m[i - 1][a][k] - m[i][a][k]))
                       for k in range(2)] for a in range(2)]
            tilt = [[None if a + k == 0 else both * m[i][a][k] for k in range(2)] for a in range(2)]
            h = ends(centre, W0, tilt)
            return [h[a][c] for a in range(4) for c in range(4)]

        def correct_face(i, targets):
            values = face_image(i)
            for r, at in targets:
                for n, value in enumerate(values):
                    tot[r, at + n] = tot[r, at + n] - value
        scale = [1.0, 1.0, 1.0, SLOPE]

        def nodal(i):
            v = x[i]
            up = after(v)
            high = above(v)
            tiles = [[v, v + up, v - up], [v + high, m[i][0][0], m[i][0][1]], [v - high, m[i][1][0], m[i][1][1]]]
            pick = [0, 1, 1, 2]
            made = {}
            out = []
            for a in range(4):
                for c in range(4):
                    key = (pick[a], pick[c])
                    if key not in made:
                        factor = float(scale[a] * scale[c])
                        made[key] = tiles[key[0]][key[1]] if factor == 1.0 else factor * tiles[key[0]][key[1]]
                    out.append((key, made[key]))
            return out

        at_line = {i: nodal(i) for i in (OWN - 2, OWN - 1, OWN)}

        def correct_row(r):
            low, high = OWN - 1 - r, OWN - r
            coeff = coeffs[OWN - r]
            for kindb in range(2):
                diff = [[None if a + k == 0 else
                         coeff * (m[low][a][k] - m[high][a][k] if kindb else m[low][a][k] + m[high][a][k])
                         for k in range(2)] for a in range(2)]
                h = ends(None, 1.0, diff)
                for b in ((3,) if kindb else (1, 2)):
                    factor = float(MUB[b] * (SLOPE if kindb else 1.0))
                    for a in range(4):
                        for c in range(4):
                            if h[a][c] is not None:
                                tot[r, st(b, a, c)] = tot[r, st(b, a, c)] - factor * h[a][c]
                made = {}
                for n in range(16):
                    key, lower_value = at_line[low][n]
                    upper_value = at_line[high][n][1]
                    if key not in made:
                        made[key] = (float(SLOPE) * (lower_value - upper_value) if kindb
                                     else lower_value + upper_value)
                    for b in ((3,) if kindb else (1, 2)):
                        sol[r, b * 16 + n] = sol[r, b * 16 + n] + made[key]
            for n in range(16):
                sol[r, n] = sol[r, n] + at_line[low][n][1]
                sol[r, 64 + n] = sol[r, 64 + n] + at_line[high][n][1]

        correct_face(OWN - 1, ((1, 64), (0, 0)))
        correct_face(OWN, ((0, 64),))
        correct_row(0)
        own_done()
        correct_face(OWN - 2, ((1, 0),))
        correct_row(1)

    def emit(field, out_ref, dual, planes=range(N)):
        def split(mid, double, odd):
            if dual:
                odd = float(KAPPA) * odd
                return mid + odd, 2.0 * double, mid - odd
            even, odd = 0.5 * mid, float(0.5 / KAPPA) * odd
            return even + odd, 0.5 * double, even - odd

        def one(b, values):
            lines = []
            for a in range(4):
                v = values[a * 4:a * 4 + 4]
                lines.append([v[0], *split(*v[1:]), after(v[0])])
            for c in range(N):
                v = [lines[a][c] for a in range(4)]
                for a, tile in enumerate([v[0], *split(*v[1:]), above(v[0])]):
                    out_ref[raw(a, b, c)] = tile[0:layers]

        for b in (0, 4):
            if b in planes:
                one(b, [field[0, b * 16 + n] for n in range(16)])
        if 1 in planes:
            mids = [split(field[0, 16 + n], field[0, 32 + n], field[0, 48 + n]) for n in range(16)]
            for b in range(1, 4):
                one(b, [v[b - 1] for v in mids])

    halo_copy(0).wait()
    for b in (4, 0, 1, 2, 3):
        assemble(0, b)
        put(0, b, [rhs[0, b * 16 + n] for n in range(16)])
        if b == 4:
            send_face(0, [tot[0, 64 + n] for n in range(16)])
    half_copy(1, 0, OWN, place(0, True)).wait()
    for d in SENDS:
        if d not in NEAR_SENDS:
            when_there(d, lambda d: half_copy(1, d, slot_at(d), place(d), 1).start())
    for d in NEAR_RECVS:
        @pl.when(there(d))
        def _():
            half_came(0, d)
            half_came(1, d)
    for e in range(OWN - 2, OWN + 2):
        join_coeff(e)
    invert()

    @pl.when(there(-1))
    def _():
        part_copy(0).wait()
        halo_copy(1).wait()

    assemble(1, 4)
    for n in range(16):
        joined = tot[0, n] + rhs[1, 64 + n]
        tot[0, n] = joined
        tot[1, 64 + n] = joined
    for b in range(4):
        update(0, b)
    add_near(0)
    update(0, 4)

    def ready_face(s):
        expand(0, (4,))
        put(0, 4, top_plane(0))

    def next_face(s):
        send_face(s, [tot[0, 64 + n] for n in range(16)])

    ready_face(1)
    next_face(1)
    restrict_load()

    def step(s, _):
        cycle = s // PERIOD
        live = s < STEPS - 1
        coarse = (lax.rem(s, PERIOD) == NPRE) & live
        deferred = lax.rem(s - 1, PERIOD) != NPRE
        behind = deferred & (s > 1)
        plain = jnp.logical_not(coarse) & live

        expand(0, range(4))
        cross(0)
        for b in range(4):
            put(0, b, plane(0, b))

        @pl.when(there(2))
        def _():
            far_copy(s - 1).wait_send()

        @pl.when(behind)
        def _():
            expand(1, range(4))
            cross(1)
            for b in range(4):
                put(1, b, plane(1, b))
                if b:
                    update(1, b)
            update(1, 4)

        @pl.when(coarse)
        def _():
            add_far(s - 1)
            update(1, 0)

        @pl.when(s > 1)
        def _():
            expand(1, (4,))
            put(1, 4, top_plane(1))

        @pl.when(coarse)
        def _():
            expand(1, range(4))
            cross(1)
            for b in range(4):
                put(1, b, plane(1, b))

        @pl.when(jnp.logical_not(live))
        def _():
            emit(sol, sol_out, False)

        @pl.when(plain)
        def _():
            for b in range(1, 4):
                update(0, b)

        add_near(s)

        @pl.when(jnp.logical_not(live))
        def _():
            emit(tot, res_out, True, range(1, N))

        @pl.when(plain)
        def _():
            update(0, 4)
            ready_face(s + 1)

        @pl.when(s == 1)
        def _():
            @pl.when(there(-1))
            def _():
                part_copy(1).wait()
                halo_copy(2).wait()

            for b in range(4):
                assemble(1, b)
                put(1, b, [rhs[1, b * 16 + n] for n in range(16)])
                if b:
                    update(1, b)
            update(1, 4)
            expand(1, (4,))
            put(1, 4, top_plane(1))

        def join(n):
            joined = tot[0, n] + tot[1, 64 + n]
            tot[0, n] = joined
            tot[1, 64 + n] = joined

        @pl.when(deferred & plain)
        def _():
            add_far(s - 1)
            for n in range(16):
                shift_top(1, 64, n)
                join(n)
                shift_top(0, 64, n)

        @pl.when(jnp.logical_not(deferred & plain))
        def _():
            @pl.when(deferred & jnp.logical_not(coarse))
            def _():
                add_far(s - 1)
                for n in range(16):
                    shift_top(1, 64, n)

            for n in range(16):
                join(n)

            @pl.when(plain)
            def _():
                for n in range(16):
                    shift_top(0, 64, n)

        @pl.when(coarse)
        def _():
            add_far(s)

            def own_done():
                for b in range(N):
                    update(0, b)
                ready_face(s + 1)
                next_face(s + 1)

            correct(cycle, own_done)
            for b in range(N):
                update(1, b)

        @pl.when((lax.rem(s + 1, PERIOD) == NPRE) & (s + 1 < STEPS - 1))
        def _():
            coarse_send((s + 1) // PERIOD)

        @pl.when(plain)
        def _():
            next_face(s + 1)

        return 0

    lax.fori_loop(1, STEPS, step, 0)
    emit(tot, res_out, True, (0,))


def hand_over(sol_ref, res_ref, sol_out, res_out, sems):
    copies = [pltpu.make_async_copy(src, dst, sems.at[k]) for k, (src, dst) in enumerate(
        ((sol_ref, sol_out), (res_ref, res_out)))]
    for copy in copies:
        copy.start()
    for copy in copies:
        copy.wait()


def per_device(sizes, load, kappa, wet):
    layers, _, width = kappa.shape
    nodes = N * N * N
    tile = (2 * layers, width)
    half = (layers, width)
    sizes = sizes + (layers, width)
    out = jax.ShapeDtypeStruct((nodes, layers, width), F32)
    vmem = pl.BlockSpec(memory_space=pltpu.VMEM)
    fold = width // HALO
    groups = 80 // fold
    messages = 8 + 8 // fold
    dma = pltpu.SemaphoreType.DMA
    solution, residual = pl.pallas_call(
        functools.partial(kernel, sizes),
        out_shape=(out, out),
        in_specs=[pl.BlockSpec(memory_space=pltpu.HBM)] * 3,
        out_specs=(vmem, vmem),
        scratch_shapes=[
            pltpu.VMEM((nodes,) + half, F32),
            pltpu.VMEM(half, F32),
            pltpu.VMEM(half, jnp.int32),
            pltpu.VMEM((groups + 82,) + half, F32),
            pltpu.VMEM((81,) + half, F32),
            pltpu.VMEM((2, groups + 1) + half, F32),
            pltpu.VMEM((2, SPAN + 1) + half, F32),
            pltpu.VMEM((SPAN,) + tile, F32),
            pltpu.VMEM((2, 80) + tile, F32),
            pltpu.VMEM((2, 80) + tile, F32),
            pltpu.VMEM((2, 80) + tile, F32),
            pltpu.VMEM((2, 80) + tile, F32),
            pltpu.VMEM((2, nodes) + tile, F32),
            pltpu.VMEM((2, nodes) + tile, F32),
            pltpu.VMEM((2,) + tile, F32),
            pltpu.VMEM((2, 4) + tile, F32),
            pltpu.VMEM((STEPS, messages) + tile, F32),
            pltpu.VMEM((2, STEPS, messages) + tile, F32),
            pltpu.VMEM((CYCLES, SPAN, 2) + tile, F32),
            pltpu.VMEM((SPAN - 1,) + tile, F32),
            dma((3,)), dma((5,)), dma((5,)), dma((2, SPAN + 1)), dma((2, SPAN + 1)),
            dma((2, STEPS)), dma((2, STEPS)), dma((SPAN + 1,)), dma((CYCLES, SPAN + 1)),
        ],
        compiler_params=pltpu.CompilerParams(collective_id=0, has_side_effects=True, vmem_limit_bytes=16 * 2 ** 20),
    )(*[pltpu.with_memory_space_constraint(x, pltpu.HBM) for x in (
        load.reshape(nodes, layers, width), kappa.reshape(layers, width), wet.reshape(layers, width))])
    place = pl.BlockSpec(memory_space=pl.ANY)
    solution, residual = pl.pallas_call(
        hand_over, out_shape=(out, out), in_specs=[place] * 2, out_specs=(place, place),
        scratch_shapes=[dma((2,))],
        compiler_params=pltpu.CompilerParams(vmem_limit_bytes=2 ** 20),
    )(solution, residual)
    return solution.reshape(load.shape), residual.reshape(load.shape)


def solution(mesh):
    sizes = tuple(mesh.shape[name] for name in ("ex", "ey", "lin"))
    field = P(None, None, None, None, ("ey", "lin"), "ex")
    cell = P(None, ("ey", "lin"), "ex")
    return jax.shard_map(
        functools.partial(per_device, sizes), mesh=mesh, in_specs=(field, cell, cell),
        out_specs=(field, field), check_vma=False,
    )
```
